32 devices in a mesh: dp: 8 (over z, x), row: 2 (over y), col: 2 (over core).
Axes of the slice: x: 2, y: 2, z: 4, core: 2. Of those that a mesh axis runs over, the one named last changes fastest.
Arguments:
- tokens: bfloat16 [4096, 2048], P(('dp', 'col'), 'row'), may hold values from -30 to 30
- cotangent: bfloat16 [4096, 2048], P(('dp', 'col'), 'row'), may hold values from -6 to 6
- seq_lengths: int32 [8, 3], P('dp'), may hold values from 1 to 256, 512 in all within a row
- balance_order: int32 [8, 512], P('dp'), may hold values from 0 to 511, each once within a row
- attention_gain: bfloat16 [2048], P('row'), may hold values from 0.25 to 1.75
- query_weight: bfloat16 [2048, 2048], P('row', 'col'), may hold values from -0.125 to 0.125
- key_weight: bfloat16 [2048, 1024], P('row', 'col'), may hold values from -0.125 to 0.125
- value_projection: bfloat16 [2048, 1024], P('row', 'col'), may hold values from -0.125 to 0.125
- query_gain: bfloat16 [128], replicated, may hold values from 0.25 to 1.75
- key_norm_gain: bfloat16 [128], replicated, may hold values from 0.25 to 1.75
- output_weight: bfloat16 [2048, 2048], P('col', 'row'), may hold values from -1.5 to 1.5
- feedforward_gain: bfloat16 [2048], P('row'), may hold values from 0.25 to 1.75
- gate_weight: bfloat16 [2048, 6144], P('row', 'col'), may hold values from -0.125 to 0.125
- up_weight: bfloat16 [2048, 6144], P('row', 'col'), may hold values from -0.125 to 0.125
- down_weight: bfloat16 [6144, 2048], P('col', 'row'), may hold values from -0.109375 to 0.109375
Outputs:
- layer_out: float32 [4096, 2048], P(('dp', 'col'), 'row')
- input_grad: float32 [4096, 2048], P(('dp', 'col'), 'row')
- attention_gain_grad: float32 [2048], replicated
- query_weight_grad: float32 [2048, 2048], P(('row', 'dp'), 'col')
- key_weight_grad: float32 [2048, 1024], P(('row', 'dp'), 'col')
- value_weight_grad: float32 [2048, 1024], P(('row', 'dp'), 'col')
- query_gain_grad: float32 [128], replicated
- key_gain_grad: float32 [128], replicated
- output_weight_grad: float32 [2048, 2048], P(('col', 'dp'), 'row')
- feedforward_gain_grad: float32 [2048], replicated
- gate_weight_grad: float32 [2048, 6144], P(('row', 'dp'), 'col')
- up_weight_grad: float32 [2048, 6144], P(('row', 'dp'), 'col')
- down_weight_grad: float32 [6144, 2048], P(('col', 'dp'), 'row')
The draws below stay inside these ranges and needn't reach their ends.
Inputs may be any that keep to these rules, and one draw needn't show every extreme that they name: `seq_lengths`: row d lists the lengths of the sequences of data group d in their order; each row sums to 512 and its largest entry is 256. `balance_order`: each row is a permutation of 0 to 511.
All inputs are finite; a program needn't handle non-finite values.
Results may differ from the reference program's by a relative error of at most 0.019.
Values may be sent and summed in bfloat16 or wider, within the bound.
No kernel may reach another device: no remote copies, remote signals or barrier semaphores. Data moves between devices by JAX's collectives and lax.ppermute only.
A program may use at most 192 MiB of HBM per device.

```python
import math
import jax
import jax.numpy as jnp
import numpy as np
from jax import lax

D = 2048
QUERY_HEADS = 16
KEY_VALUE_HEADS = 8
HEAD_SIZE = 128
FF = 6144
SEQS = 3
GROUP = 512
HALF = 256
PIECE = 32
SEQ_MOST = 256
TOKENS = 4096
QW = 2048
KW = 1024
N_DP = 8


def draw_tokens(key, part):
    key_base, key_cols, key_row_matrix = jax.random.split(key, 3)
    columns = jnp.arange(D, dtype=jnp.float32) / (D - 1)
    base_vals = jnp.clip(jax.random.normal(key_base, (TOKENS, D), jnp.float32), -4.0, 4.0)
    slope_vals = jnp.exp(math.log(3.0) * columns)
    column_scale = slope_vals * jnp.exp(jax.random.uniform(key_cols, (D,), jnp.float32, math.log(0.6), math.log(1.6)))
    row_scale = jnp.exp(jax.random.uniform(key_row_matrix, (TOKENS, 1), jnp.float32, math.log(0.5), math.log(1.5)))
    return (base_vals * row_scale * column_scale[None, :]).astype(jnp.bfloat16)


def block_levels(key, extent, pieces, low, high):
    factor_of, own = 1.0, jax.random.fold_in(key, 6)
    for axis_at, parts in pieces:
        steps = jnp.exp(jax.random.uniform(jax.random.fold_in(own, axis_at), (parts,), jnp.float32, low / len(pieces), high / len(pieces)))
        factor_of = factor_of * jnp.repeat(steps, extent[axis_at] // parts).reshape([-1 if axis == axis_at else 1 for axis in range(len(extent))])
    return factor_of


def profile(amount, total, reach, lean):
    portions = [(1 << 20) // math.isqrt(standing ** lean) + 1 for standing in range(2, amount + 1)]
    spare, given = total - reach - (amount - 1), [1] * (amount - 1)
    while spare > 0:
        candidates = [i for i in range(amount - 1) if given[i] < reach]
        pool, remaining = sum([portions[i] for i in candidates]), spare
        for i in candidates:
            more = min(reach - given[i], max(1, remaining * portions[i] // pool), spare)
            given[i] = given[i] + more
            spare = spare - more
    return np.array([reach] + given)


def ragged_sizes(key, amount, total, reach, skew):
    if amount == 2:
        one = jax.random.randint(key, (), max(1, total - reach), min(reach, total - 1) + 1)
        return jnp.stack([one, total - one])
    sizes = jnp.asarray(profile(amount, total, reach, skew), jnp.int32)
    pairs = (amount - 1) // 2
    donor, taker = sizes[1:1 + 2 * pairs:2], sizes[2:2 + 2 * pairs:2]
    margin = jnp.minimum(donor - 1, reach - taker)
    moved = jax.random.randint(jax.random.fold_in(key, 1), (pairs,), 0, 1 << 20) % (margin + 1)
    sizes = sizes.at[1:1 + 2 * pairs:2].set(donor - moved).at[2:2 + 2 * pairs:2].set(taker + moved)
    return sizes[jax.random.permutation(jax.random.fold_in(key, 2), amount)]


def bell_draw(own_key, shape, spread, most, cuts=(), kind=jnp.bfloat16):
    factor_of = block_levels(own_key, shape, cuts, -0.22, 0.18) if cuts else 1.0
    drawn = jax.random.normal(own_key, shape, jnp.float32) * spread * factor_of
    return jnp.minimum(jnp.maximum(drawn, -most), most).astype(kind)


def setup_inputs(seed: int = 0) -> dict:
    splits = jax.random.split(jax.random.key(seed), 16)
    tokens = draw_tokens(jax.random.fold_in(splits[15], 71), 0)
    cotangent = bell_draw(splits[1], (TOKENS, D), 1.0, 6.0, ((0, 16), (1, 2)))
    seq_lengths = jax.vmap(lambda own: ragged_sizes(own, SEQS, GROUP, SEQ_MOST, 2))(jax.random.split(splits[2], N_DP)).reshape((N_DP, SEQS)).astype(jnp.int32)
    balance_order = jax.vmap(lambda own: jax.random.permutation(own, GROUP))(jax.random.split(splits[3], N_DP)).reshape((N_DP, GROUP)).astype(jnp.int32)
    attention_gain = jnp.clip(1.0 + 0.15 * jax.random.normal(splits[4], (D,), jnp.float32), 0.25, 1.75).astype(jnp.bfloat16)
    query_weight = bell_draw(splits[5], (D, QW), D ** -0.5, 0.125, ((0, 2), (1, 2)))
    key_weight = bell_draw(splits[6], (D, KW), D ** -0.5, 0.125, ((0, 2), (1, 2)))
    value_projection = bell_draw(splits[7], (D, KW), D ** -0.5, 0.125, ((0, 2), (1, 2)))
    query_gain = jnp.clip(1.0 + 0.15 * jax.random.normal(splits[8], (HEAD_SIZE,), jnp.float32), 0.25, 1.75).astype(jnp.bfloat16)
    key_norm_gain = jnp.clip(1.0 + 0.15 * jax.random.normal(splits[9], (HEAD_SIZE,), jnp.float32), 0.25, 1.75).astype(jnp.bfloat16)
    output_weight = bell_draw(splits[10], (QW, D), (QW // 128) ** -0.5, 1.5, ((0, 2), (1, 2)))
    feedforward_gain = jnp.clip(1.0 + 0.15 * jax.random.normal(splits[11], (D,), jnp.float32), 0.25, 1.75).astype(jnp.bfloat16)
    gate_weight = bell_draw(splits[12], (D, FF), D ** -0.5, 0.125, ((0, 2), (1, 2)))
    up_weight = bell_draw(splits[13], (D, FF), D ** -0.5, 0.125, ((0, 2), (1, 2)))
    down_weight = bell_draw(splits[14], (FF, D), (FF // 2) ** -0.5, 0.109375, ((0, 2), (1, 2)))
    return {"tokens": tokens, "cotangent": cotangent, "seq_lengths": seq_lengths, "balance_order": balance_order, "attention_gain": attention_gain, "query_weight": query_weight, "key_weight": key_weight, "value_projection": value_projection, "query_gain": query_gain, "key_norm_gain": key_norm_gain, "output_weight": output_weight, "feedforward_gain": feedforward_gain, "gate_weight": gate_weight, "up_weight": up_weight, "down_weight": down_weight}


EPSILON = 1e-06
ROPE_BASE = 1000000.0
NEGATIVE = -1e+30
HIGHEST = lax.Precision.HIGHEST

@jax.custom_vjp
def lower_precision(v):
    return lax.optimization_barrier(v.astype(jnp.bfloat16)).astype(jnp.float32)

@jax.custom_vjp
def lower_precision_back(v):
    return v

def low_keep(v):
    return (lower_precision(v), None)

def low_pass(kept, grad):
    return (grad,)

def back_keep(v):
    return (v, None)

def back_low(kept, grad):
    return (lower_precision(grad),)
lower_precision.defvjp(low_keep, low_pass)
lower_precision_back.defvjp(back_keep, back_low)

def matrix_product(left_matrix, right_matrix):
    return jnp.dot(left_matrix, right_matrix, precision=HIGHEST, preferred_element_type=jnp.float32)

def scaled_values(values, gain_vector):
    return values * lax.rsqrt(lax.optimization_barrier(jnp.mean(values * values, axis=-1, keepdims=True)) + EPSILON) * gain_vector

def apply_rotary(values, token_position):
    half_width = values.shape[-1] // 2
    frequency = ROPE_BASE ** (-2.0 * jnp.arange(half_width, dtype=jnp.float32) / values.shape[-1])
    angles = token_position.astype(jnp.float32)[:, None] * frequency[None, :]
    cosine = jnp.cos(angles)[:, None, :]
    sine_part = jnp.sin(angles)[:, None, :]
    first_half = values[..., :half_width]
    second_half = values[..., half_width:]
    return jnp.concatenate([first_half * cosine - second_half * sine_part, second_half * cosine + first_half * sine_part], axis=-1)

def layer(stream, attention_gain, query_weight, key_weight, value_projection, query_gain, key_norm_gain, output_weight, feedforward_gain, gate_weight, up_weight, down_weight, segment, token_position):
    group_members = stream.shape[0]
    scale_factor = 1.0 / math.sqrt(HEAD_SIZE)
    normed_layer_input = lower_precision(scaled_values(stream, attention_gain))
    query_raw = lower_precision_back(matrix_product(normed_layer_input, query_weight))
    key_unnormed = lower_precision_back(matrix_product(normed_layer_input, key_weight))
    value_row_matrix = lower_precision(lower_precision_back(matrix_product(normed_layer_input, value_projection))).reshape(group_members, KEY_VALUE_HEADS, HEAD_SIZE)
    query_rows = lower_precision(apply_rotary(scaled_values(query_raw.reshape(group_members, QUERY_HEADS, HEAD_SIZE), query_gain), token_position))
    key_row_matrix = lower_precision(apply_rotary(scaled_values(key_unnormed.reshape(group_members, KEY_VALUE_HEADS, HEAD_SIZE), key_norm_gain), token_position))
    rows_per_block = min(512, group_members)
    block_count = group_members // rows_per_block

    def attend(block_items):
        query_row_block, seg_block, pos_block = block_items
        grouped_heads = query_row_block.reshape(rows_per_block, KEY_VALUE_HEADS, QUERY_HEADS // KEY_VALUE_HEADS, HEAD_SIZE)
        scores = lower_precision_back(jnp.einsum('bkrd,tkd->krbt', grouped_heads, key_row_matrix, precision=HIGHEST) * scale_factor)
        allowed = (seg_block[:, None] == segment[None, :]) & (token_position[None, :] <= pos_block[:, None])
        scores = jnp.where(allowed, scores, NEGATIVE)
        row_top = lax.optimization_barrier(jnp.max(scores, axis=-1, keepdims=True))
        exp_scores = jnp.exp(scores - row_top)
        prob_rows = lower_precision(exp_scores / lax.optimization_barrier(jnp.sum(exp_scores, axis=-1, keepdims=True)))
        mixed_out = jnp.einsum('krbt,tkd->bkrd', prob_rows, value_row_matrix, precision=HIGHEST)
        return mixed_out.reshape(rows_per_block, QUERY_HEADS * HEAD_SIZE)
    attention = lax.map(jax.checkpoint(attend), (query_rows.reshape(block_count, rows_per_block, QUERY_HEADS, HEAD_SIZE), segment.reshape(block_count, rows_per_block), token_position.reshape(block_count, rows_per_block)))
    attention = lower_precision(lower_precision_back(attention.reshape(group_members, QUERY_HEADS * HEAD_SIZE)))
    stream_mid = stream + lower_precision_back(matrix_product(attention, output_weight))
    normed_mid = lower_precision(scaled_values(stream_mid, feedforward_gain))
    gate_value = lower_precision_back(matrix_product(normed_mid, gate_weight))
    up_value = lower_precision_back(matrix_product(normed_mid, up_weight))
    activated = lower_precision(jax.nn.silu(gate_value) * up_value)
    return stream_mid + lower_precision_back(matrix_product(activated, down_weight))

def reference(tokens, cotangent, seq_lengths, balance_order, attention_gain, query_weight, key_weight, value_projection, query_gain, key_norm_gain, output_weight, feedforward_gain, gate_weight, up_weight, down_weight):
    groups = jnp.arange(N_DP, dtype=jnp.int32)[:, None]
    half_side = balance_order // HALF
    remainder = balance_order % HALF
    source = (remainder // PIECE * GROUP + half_side * HALF + groups * PIECE + remainder % PIECE).astype(jnp.int32)
    flat_source = source.reshape(-1)
    stream_all = tokens.astype(jnp.float32)[flat_source].reshape(N_DP, GROUP, D)
    upstream_all = cotangent.astype(jnp.float32)[flat_source].reshape(N_DP, GROUP, D)
    seq_ends = jnp.cumsum(seq_lengths, axis=1)
    starts = seq_ends - seq_lengths
    spot_ids = jnp.arange(GROUP, dtype=jnp.int32)
    segment_all = lax.optimization_barrier(jnp.sum((spot_ids[None, :, None] >= seq_ends[:, None, :]).astype(jnp.int32), axis=2))
    seg_hits = segment_all[:, :, None] == jnp.arange(SEQS, dtype=jnp.int32)[None, None, :]
    position_all = spot_ids[None, :] - lax.optimization_barrier(jnp.sum(jnp.where(seg_hits, starts[:, None, :], 0), axis=2))
    weights = tuple((param.astype(jnp.float32) for param in (attention_gain, query_weight, key_weight, value_projection, query_gain, key_norm_gain, output_weight, feedforward_gain, gate_weight, up_weight, down_weight)))

    def one_group(totals, group_items):
        stream, upstream, segment, token_position = group_items

        def forward(stream_in, *params):
            return layer(stream_in, *params, segment, token_position)
        layer_value, pull_back = jax.vjp(forward, stream, *weights)
        pulled = pull_back(upstream)
        return (tuple((left_sum + right_sum for left_sum, right_sum in zip(totals, pulled[1:]))), (layer_value, pulled[0]))
    zero_grads = tuple((jnp.zeros(param.shape, jnp.float32) for param in weights))
    totals, (out_rows, grad_rows) = lax.scan(one_group, zero_grads, (stream_all, upstream_all, segment_all, position_all))
    layer_out = jnp.zeros((TOKENS, D), jnp.float32).at[flat_source].set(out_rows.reshape(-1, D))
    input_grad = jnp.zeros((TOKENS, D), jnp.float32).at[flat_source].set(grad_rows.reshape(-1, D))
    return (layer_out, input_grad, totals[0], totals[1], totals[2], totals[3], totals[4], totals[5], totals[6], totals[7], totals[8], totals[9], totals[10])
```

```python
import math

import jax
import jax.numpy as jnp
from jax import lax
from jax.sharding import PartitionSpec as P

D = 2048
HEAD_SIZE = 128
EPSILON = 1e-06
ROPE_BASE = 1000000.0
NEGATIVE = -1e30
BF16 = jnp.bfloat16
F32 = jnp.float32


def dot_nn(left, right):
    return jnp.dot(left, right, preferred_element_type=F32)


def dot_nt(left, right):
    return lax.dot_general(left, right, (((1,), (1,)), ((), ())), preferred_element_type=F32)


def dot_tn(left, right):
    return lax.dot_general(left, right, (((0,), (0,)), ((), ())), preferred_element_type=F32)


def swap_row(value):
    return lax.ppermute(value, "row", [(0, 1), (1, 0)])


def swap_col(value):
    return lax.ppermute(value, "col", [(0, 1), (1, 0)])


def swap_dp(value, bit):
    count = lax.axis_size("dp")
    return lax.ppermute(value, "dp", [(i, i ^ bit) for i in range(count)])


def swap_z(value):
    return swap_dp(value, 2)


def rotary_tables(position):
    half = HEAD_SIZE // 2
    frequency = ROPE_BASE ** (-2.0 * jnp.arange(half, dtype=F32) / HEAD_SIZE)
    angles = position.astype(F32)[:, None] * frequency[None, :]
    return jnp.cos(angles)[:, None, :], jnp.sin(angles)[:, None, :]


def rotate(values, cosine, sine):
    half = values.shape[-1] // 2
    first, second = values[..., :half], values[..., half:]
    return jnp.concatenate(
        [first * cosine - second * sine, second * cosine + first * sine], axis=-1
    )


def head_norm(raw, heads):
    shaped = raw.reshape(raw.shape[0], heads, HEAD_SIZE)
    inverse = lax.rsqrt(jnp.mean(shaped * shaped, axis=-1, keepdims=True) + EPSILON)
    return shaped * inverse, inverse


def head_norm_back(grad_pre, unit, inverse, gain):
    scaled = grad_pre * gain
    raw = inverse * (scaled - unit * jnp.mean(scaled * unit, axis=-1, keepdims=True))
    return raw.reshape(raw.shape[0], -1), jnp.sum(grad_pre * unit, axis=(0, 1))


def pick(value, index, axis):
    return lax.dynamic_index_in_dim(value, index, axis, keepdims=False)


def scatter_stage(value, axis, bit):
    mine = (lax.axis_index("dp") // bit) % 2
    got = swap_dp(pick(value, 1 - mine, axis).astype(BF16), bit)
    return pick(value, mine, axis).astype(F32) + got.astype(F32)


def high_bits(count):
    bits, bit = [], 4
    while bit < count:
        bits.append(bit)
        bit *= 2
    return bits


def split_rows(value):
    count = lax.axis_size("dp")
    levels = count.bit_length() - 1
    return value.reshape((2,) * levels + (value.shape[0] // count,) + value.shape[1:])


def by_half(index, own, other):
    first = index == 0
    return jnp.where(first, own, other), jnp.where(first, other, own)


def shards(
    tokens,
    cotangent,
    seq_lengths,
    balance_order,
    attention_gain,
    query_weight,
    key_weight,
    value_projection,
    query_gain,
    key_norm_gain,
    output_weight,
    feedforward_gain,
    gate_weight,
    up_weight,
    down_weight,
):
    count = lax.axis_size("dp")
    dp_index = lax.axis_index("dp")
    row = lax.axis_index("row")
    col = lax.axis_index("col")
    zbit = (dp_index // 2) % 2
    xbit = dp_index % 2
    half = tokens.shape[0]
    group = 2 * half
    features = tokens.shape[1]
    query_part = query_weight.shape[1] // 2
    key_part = key_weight.shape[1] // 2
    heads = query_part // HEAD_SIZE
    kv_heads = key_part // HEAD_SIZE
    repeat = heads // kv_heads
    ff_half = gate_weight.shape[1]
    runs = count // 8
    run = 2 * ff_half // count
    ff_part = ff_half // 4
    scale = 1.0 / math.sqrt(HEAD_SIZE)

    def ff_pieces(weight, part, axis):
        pieces = [
            lax.dynamic_slice_in_dim(weight, ((part * runs + i) * 2 + zbit) * run, run, axis)
            for i in range(runs)
        ]
        return pieces[0] if runs == 1 else jnp.concatenate(pieces, axis=axis)

    moved_in = lax.all_to_all(tokens, "dp", split_axis=0, concat_axis=0, tiled=True)
    quarter_rows = features // 2
    send_up = jnp.concatenate(
        [
            ff_pieces(lax.dynamic_slice_in_dim(w, xbit * quarter_rows, quarter_rows, 0), 1 - row, 1)
            for w in (gate_weight, up_weight)
        ],
        axis=1,
    )
    got_up = swap_row(send_up)
    got_up_pair = swap_dp(got_up, 1)
    low_up, high_up = by_half(xbit, got_up, got_up_pair)
    own_up = jnp.concatenate([ff_pieces(w, row, 1) for w in (gate_weight, up_weight)], axis=1)
    up_all = jnp.concatenate([own_up, low_up, high_up], axis=0)

    moved_grad = lax.all_to_all(cotangent, "dp", split_axis=0, concat_axis=0, tiled=True)

    base_ids = jnp.arange(half, dtype=jnp.int32)
    local_ids = jnp.concatenate([col * half + base_ids, (1 - col) * half + base_ids])
    slot_ids = jnp.arange(group, dtype=jnp.int32)
    slot = jnp.sum(
        jnp.where(balance_order[0][None, :] == local_ids[:, None], slot_ids[None, :], 0), axis=1
    )
    lengths = seq_lengths[0]
    seq_ends = jnp.cumsum(lengths)
    starts = seq_ends - lengths
    segment = jnp.sum((slot[:, None] >= seq_ends[None, :]).astype(jnp.int32), axis=1)
    hits = segment[:, None] == jnp.arange(lengths.shape[0], dtype=jnp.int32)[None, :]
    position = slot - jnp.sum(jnp.where(hits, starts[None, :], 0), axis=1)
    cosine, sine = rotary_tables(position)
    allowed = (segment[:, None] == segment[None, :]) & (position[None, :] <= position[:, None])

    def head_columns(part):
        return jnp.concatenate(
            [
                lax.dynamic_slice_in_dim(query_weight, part * query_part, query_part, 1),
                lax.dynamic_slice_in_dim(key_weight, part * key_part, key_part, 1),
                lax.dynamic_slice_in_dim(value_projection, part * key_part, key_part, 1),
            ],
            axis=1,
        )

    heads_own = head_columns(row)
    heads_other = head_columns(1 - row)
    x_low = jnp.concatenate([moved_in, swap_col(moved_in)], axis=0)
    x_all = x_low.astype(F32)
    square = jnp.sum(x_all * x_all, axis=1)
    square = square + swap_row(square)
    inverse_in = lax.rsqrt(square / D + EPSILON)[:, None]
    scaled_in = (x_all * attention_gain).astype(BF16)
    got_heads = swap_row(dot_nn(scaled_in, heads_other).astype(BF16))
    projected = (dot_nn(scaled_in, heads_own) + got_heads.astype(F32)) * inverse_in

    query_unit, query_inverse = head_norm(projected[:, :query_part], heads)
    key_unit, key_inverse = head_norm(projected[:, query_part : query_part + key_part], kv_heads)
    values = projected[:, query_part + key_part :].astype(BF16).reshape(group, kv_heads, HEAD_SIZE)
    query_rot = rotate(query_unit * query_gain, cosine, sine).astype(BF16)
    query_rot = query_rot.reshape(group, kv_heads, repeat, HEAD_SIZE)
    key_rot = rotate(key_unit * key_norm_gain, cosine, sine).astype(BF16)
    scores = jnp.einsum("bkrd,tkd->krbt", query_rot, key_rot, preferred_element_type=F32) * scale
    scores = jnp.where(allowed, scores, NEGATIVE)
    top = jnp.max(scores, axis=-1, keepdims=True)
    exps = jnp.exp(scores - top)
    total = jnp.sum(exps, axis=-1, keepdims=True)
    prob = exps / total
    prob_low = prob.astype(BF16)
    attention = jnp.einsum("krbt,tkd->bkrd", prob_low, values, preferred_element_type=F32)
    attention = attention.reshape(group, query_part).astype(BF16)
    attention_all = jnp.concatenate(by_half(row, attention, swap_row(attention)), axis=1)
    out_part = dot_nn(attention_all, output_weight)
    stream = x_all[:half]
    stream_mid = stream + out_part[:half] + swap_col(out_part[half:].astype(BF16)).astype(F32)

    square_mid = jnp.sum(stream_mid * stream_mid, axis=1)
    square_mid = square_mid + swap_row(square_mid)
    inverse_mid = lax.rsqrt(square_mid / D + EPSILON)[:, None]
    unit_mid = stream_mid * inverse_mid
    normed_mid = (unit_mid * feedforward_gain).astype(BF16)

    quarter = half // 2
    by_row = swap_row(normed_mid)
    by_z = swap_z(normed_mid)
    diagonal = jnp.concatenate([swap_row(by_z[:quarter]), swap_z(by_row[quarter:])], axis=0)
    near = jnp.concatenate([normed_mid, by_row], axis=1)
    far = jnp.concatenate([by_z, diagonal], axis=1)
    mid_all = jnp.concatenate([near, swap_col(near), far, swap_col(far)], axis=0)

    grad_z = swap_z(moved_grad)
    grad_col = swap_col(jnp.concatenate([moved_grad, grad_z], axis=0))
    grad_all = jnp.concatenate([moved_grad, grad_col[:half], grad_z, grad_col[half:]], axis=0)

    down_own = ff_pieces(down_weight, row, 0)
    down_other = ff_pieces(down_weight, 1 - row, 0)
    got_act = swap_row(dot_nt(grad_all, down_other).astype(BF16))
    act_grad = dot_nt(grad_all, down_own) + got_act.astype(F32)

    gate_up = dot_nn(mid_all, up_all)
    gate_value = gate_up[:, :ff_part]
    up_value = gate_up[:, ff_part:]
    sigmoid_gate = jax.nn.sigmoid(gate_value)
    silu_gate = gate_value * sigmoid_gate
    activated = (silu_gate * up_value).astype(BF16)
    gate_grad = act_grad * up_value * sigmoid_gate * (1.0 + gate_value * (1.0 - sigmoid_gate))
    up_grad = act_grad * silu_gate
    gate_up_grad = jnp.concatenate([gate_grad.astype(BF16), up_grad.astype(BF16)], axis=1)

    mid_part = dot_nt(gate_up_grad, up_all)
    got_mid = swap_col(
        jnp.concatenate([mid_part[half:group], mid_part[group + half :]], axis=0).astype(BF16)
    ).astype(F32)
    near_part = mid_part[:half] + got_mid[:half]
    far_part = mid_part[group : group + half] + got_mid[half:]
    to_row = near_part[:, features:]
    to_z = far_part[:, :features]
    to_both = far_part[:, features:].astype(BF16)
    via_row = swap_row(to_both[:quarter]).astype(F32)
    via_z = swap_z(to_both[quarter:]).astype(F32)
    to_z = jnp.concatenate([to_z[:quarter] + via_row, to_z[quarter:]], axis=0)
    to_row = jnp.concatenate([to_row[:quarter], to_row[quarter:] + via_z], axis=0)
    normed_mid_grad = (
        near_part[:, :features]
        + swap_row(to_row.astype(BF16)).astype(F32)
        + swap_z(to_z.astype(BF16)).astype(F32)
    )

    activated_all = jnp.concatenate(by_half(row, activated, swap_row(activated)), axis=1)
    down_pair = jnp.concatenate(by_half(row, down_own, down_other), axis=0)
    out_ff = dot_nn(activated_all, down_pair)
    out_ff = out_ff[:group] + swap_z(out_ff[group:].astype(BF16)).astype(F32)
    layer_out = stream_mid + out_ff[:half] + swap_col(out_ff[half:].astype(BF16)).astype(F32)

    def reduce_high(value, axis):
        for bit in reversed(high_bits(count)):
            value = scatter_stage(value, axis, bit)
        return value

    down_grad = split_units(dot_tn(activated_all, grad_all).astype(BF16), count)
    down_grad = scatter_stage(down_grad, down_grad.ndim - 3, 1)
    down_grad = reduce_high(down_grad, 0)

    def up_weight_rows(grad_part):
        whole = dot_tn(mid_all, grad_part).astype(BF16)
        levels = count.bit_length() - 1
        value = whole.reshape((2,) * (levels + 1) + (features // count, ff_part))
        value = scatter_stage(value, value.ndim - 3, 1)
        value = reduce_high(value, 1)
        own, other = value[0], value[1]
        got = swap_row(other.astype(BF16)).astype(F32)
        keep = [pick(part, zbit, 0) for part in (own, got)]
        sent = jnp.stack([pick(part, 1 - zbit, 0) for part in (own, got)]).astype(BF16)
        swapped = swap_z(sent).astype(F32)
        table = []
        for near_piece, far_piece in zip(by_half(row, keep[0], keep[1]), by_half(row, swapped[0], swapped[1])):
            table.append(by_half(zbit, near_piece, far_piece))
        return jnp.concatenate(
            [
                table[part][z][:, i * run : (i + 1) * run]
                for part in range(2)
                for i in range(runs)
                for z in range(2)
            ],
            axis=1,
        )

    gate_weight_grad = up_weight_rows(gate_up_grad[:, :ff_part])
    up_weight_grad = up_weight_rows(gate_up_grad[:, ff_part:])

    upstream = moved_grad.astype(F32)
    weighted_mid = normed_mid_grad * feedforward_gain
    mid_sum = jnp.sum(weighted_mid * unit_mid, axis=1)
    mid_sum = (mid_sum + swap_row(mid_sum))[:, None]
    stream_mid_grad = upstream + inverse_mid * (weighted_mid - unit_mid * mid_sum / D)
    feedforward_part = jnp.sum(normed_mid_grad * unit_mid, axis=0)
    branch_low = stream_mid_grad.astype(BF16)
    branch = jnp.concatenate([branch_low, swap_col(branch_low)], axis=0)

    out_own = lax.dynamic_slice_in_dim(output_weight, row * query_part, query_part, 0)
    out_other = lax.dynamic_slice_in_dim(output_weight, (1 - row) * query_part, query_part, 0)
    got_attention = swap_row(dot_nt(branch, out_other).astype(BF16))
    attention_grad = (dot_nt(branch, out_own) + got_attention.astype(F32)).astype(BF16)

    def reduce_heads(value):
        value = split_rows(value)
        value = scatter_stage(value, value.ndim - 4, 2)
        value = scatter_stage(value, value.ndim - 3, 1)
        return reduce_high(value, 0)

    output_weight_grad = reduce_heads(dot_tn(attention_all, branch).astype(BF16))

    grad_out = attention_grad.reshape(group, kv_heads, repeat, HEAD_SIZE)
    prob_grad = jnp.einsum("bkrd,tkd->krbt", grad_out, values, preferred_element_type=F32)
    centre = jnp.sum(prob * prob_grad, axis=-1, keepdims=True)
    score_grad = (prob * (prob_grad - centre)).astype(BF16)
    query_rot_grad = (
        jnp.einsum("krbt,tkd->bkrd", score_grad, key_rot, preferred_element_type=F32) * scale
    )
    key_rot_grad = (
        jnp.einsum("krbt,bkrd->tkd", score_grad, query_rot, preferred_element_type=F32) * scale
    )
    value_grad = jnp.einsum("krbt,bkrd->tkd", prob_low, grad_out, preferred_element_type=F32)
    query_pre_grad = rotate(query_rot_grad.reshape(group, heads, HEAD_SIZE), cosine, -sine)
    query_raw_grad, query_gain_part = head_norm_back(
        query_pre_grad, query_unit, query_inverse, query_gain
    )
    key_pre_grad = rotate(key_rot_grad, cosine, -sine)
    key_raw_grad, key_gain_part = head_norm_back(key_pre_grad, key_unit, key_inverse, key_norm_gain)
    projected_grad = jnp.concatenate(
        [
            query_raw_grad.astype(BF16),
            key_raw_grad.astype(BF16),
            value_grad.reshape(group, key_part).astype(BF16),
        ],
        axis=1,
    )
    projected_other = swap_row(projected_grad)
    in_part = dot_nt(projected_grad, heads_own) + dot_nt(projected_other, heads_other)
    normed_in_grad = in_part[:half] + swap_col(in_part[half:].astype(BF16)).astype(F32)

    normed_in = (x_all * inverse_in * attention_gain).astype(BF16)
    heads_grad_own = reduce_heads(dot_tn(normed_in, projected_grad).astype(BF16))
    heads_grad_other = reduce_heads(dot_tn(normed_in, projected_other).astype(BF16))

    def head_grad(start, width):
        own = heads_grad_own[:, start : start + width]
        other = heads_grad_other[:, start : start + width]
        return jnp.concatenate(by_half(row, own, other), axis=1)

    query_weight_grad = head_grad(0, query_part)
    key_weight_grad = head_grad(query_part, key_part)
    value_weight_grad = head_grad(query_part + key_part, key_part)

    unit_in = stream * inverse_in[:half]
    weighted_in = normed_in_grad * attention_gain
    in_sum = jnp.sum(weighted_in * unit_in, axis=1)
    in_sum = (in_sum + swap_row(in_sum))[:, None]
    stream_grad = stream_mid_grad + inverse_in[:half] * (weighted_in - unit_in * in_sum / D)
    attention_part = jnp.sum(normed_in_grad * unit_in, axis=0)

    feature_start = row * features
    zero_vector = jnp.zeros((D,), F32)
    gain_totals = lax.psum(
        (
            lax.dynamic_update_slice_in_dim(zero_vector, attention_part, feature_start, 0),
            lax.dynamic_update_slice_in_dim(zero_vector, feedforward_part, feature_start, 0),
            query_gain_part,
            key_gain_part,
        ),
        ("dp", "row", "col"),
    )
    out_back = lax.all_to_all(
        layer_out.astype(BF16), "dp", split_axis=0, concat_axis=0, tiled=True
    ).astype(F32)
    grad_back = lax.all_to_all(
        stream_grad.astype(BF16), "dp", split_axis=0, concat_axis=0, tiled=True
    ).astype(F32)
    return (
        out_back,
        grad_back,
        gain_totals[0],
        query_weight_grad,
        key_weight_grad,
        value_weight_grad,
        gain_totals[2],
        gain_totals[3],
        output_weight_grad,
        gain_totals[1],
        gate_weight_grad,
        up_weight_grad,
        down_grad,
    )


def split_units(value, count):
    levels = count.bit_length() - 1
    return value.reshape((2,) * (levels - 1) + (2 * value.shape[0] // count, value.shape[1]))


def solution(mesh):
    placed = (
        P(("dp", "col"), "row"),
        P(("dp", "col"), "row"),
        P("dp", None),
        P("dp", None),
        P("row"),
        P("row", "col"),
        P("row", "col"),
        P("row", "col"),
        P(),
        P(),
        P("col", "row"),
        P("row"),
        P("row", "col"),
        P("row", "col"),
        P("col", "row"),
    )
    return jax.shard_map(
        shards,
        mesh=mesh,
        in_specs=placed,
        out_specs=(
            P(("dp", "col"), "row"),
            P(("dp", "col"), "row"),
            P(),
            P(("row", "dp"), "col"),
            P(("row", "dp"), "col"),
            P(("row", "dp"), "col"),
            P(),
            P(),
            P(("col", "dp"), "row"),
            P(),
            P(("row", "dp"), "col"),
            P(("row", "dp"), "col"),
            P(("col", "dp"), "row"),
        ),
        check_vma=False,
    )
```

```python
import math

import jax
import jax.numpy as jnp
from jax import lax
from jax.experimental import pallas as pl
from jax.experimental.pallas import tpu as pltpu
from jax.sharding import PartitionSpec as P

D = 2048
HEAD_SIZE = 128
EPSILON = 1e-06
ROPE_BASE = 1000000.0
NEGATIVE = -1e30
EXTRA = 8
VMEM_LIMIT = 40 << 20
BF16 = jnp.bfloat16
F32 = jnp.float32


def dot_nn(left, right):
    return jnp.dot(left, right, preferred_element_type=F32)


def dot_nt(left, right):
    return lax.dot_general(left, right, (((1,), (1,)), ((), ())), preferred_element_type=F32)


def dot_tn(left, right):
    return lax.dot_general(left, right, (((0,), (0,)), ((), ())), preferred_element_type=F32)


def swap_row(value):
    return lax.ppermute(value, "row", [(0, 1), (1, 0)])


def swap_col(value):
    return lax.ppermute(value, "col", [(0, 1), (1, 0)])


def swap_dp(value, bit):
    count = lax.axis_size("dp")
    return lax.ppermute(value, "dp", [(i, i ^ bit) for i in range(count)])


def swap_z(value):
    return swap_dp(value, 2)


def rotary_tables(position):
    half = HEAD_SIZE // 2
    frequency = ROPE_BASE ** (-2.0 * jnp.arange(half, dtype=F32) / HEAD_SIZE)
    angles = position.astype(F32)[:, None] * frequency[None, :]
    cosine, sine = jnp.cos(angles), jnp.sin(angles)
    return jnp.concatenate([cosine, cosine], axis=1), jnp.concatenate([-sine, sine], axis=1)


def pick(value, index, axis):
    return lax.dynamic_index_in_dim(value, index, axis, keepdims=False)


def high_bits(count):
    bits, bit = [], 4
    while bit < count:
        bits.append(bit)
        bit *= 2
    return bits


def split_rows(value, levels):
    return value.reshape((2,) * levels + (value.shape[0] >> levels,) + value.shape[1:])


def two_rows(value):
    high = lax.reduce_precision(value, 8, 7)
    return [high.astype(BF16), (value - high).astype(BF16)]


def with_rows(values, rows):
    count = lax.axis_size("dp")
    width = values[0].shape[1]
    block = jnp.stack([jnp.pad(r, (0, width - r.shape[0])) for r in rows])
    block = jnp.pad(block, ((0, EXTRA - len(rows)), (0, 0)))
    shares = [value.reshape(count, -1, width) for value in values]
    block = jnp.broadcast_to(block[None], (count, EXTRA, width))
    return jnp.concatenate(shares + [block], axis=1)


def exchange(value):
    return lax.all_to_all(value, "dp", split_axis=0, concat_axis=0, tiled=True)


def after(value, *earlier):
    return lax.optimization_barrier((value,) + earlier)[0]


def together(*values):
    return lax.optimization_barrier(values)


class Line:
    def __init__(self, value):
        self.last = value

    def hold(self, *values):
        held = together(*values, self.last)[:-1]
        return held[0] if len(held) == 1 else held

    def passed(self, value):
        self.last = value
        return value


def by_half(index, own, other):
    first = index == 0
    return jnp.where(first, own, other), jnp.where(first, other, own)


TIMES = {
    "gate_and_up": 12.0,
    "gate_and_up_back": 7.0,
    "attend": 7.0,
    "attend_back": 12.0,
    "product_tn": 3.0,
    "product_nt": 3.0,
    "down_proj": 3.0,
    "heads_forward": 3.5,
    "heads_backward": 3.0,
    "mid_all": 2.5,
}


def light(name):
    amount = TIMES.get(name, 1.5) * 0.1
    return pl.CostEstimate(
        flops=int(amount * 1.15e9) + 1, bytes_accessed=int(amount * 3.69e6), transcendentals=0
    )


def params(grid_axes=1):
    return pltpu.CompilerParams(vmem_limit_bytes=VMEM_LIMIT)


def scalars(*values):
    return jnp.stack([jnp.asarray(v, jnp.int32) for v in values])


def lanes_of(sums):
    return jnp.broadcast_to(sums, (sums.shape[0], HEAD_SIZE)).T[:8]


def column_of(lanes):
    return lanes.T[:, :1]


def local_call(kernel, inputs, outputs, name):
    return pl.pallas_call(
        kernel,
        out_shape=[jax.ShapeDtypeStruct(shape, dtype) for shape, dtype in outputs],
        compiler_params=params(),
        cost_estimate=light(name),
        name=name,
    )(*inputs)


def grid_call(kernel, grid, picks, inputs, in_specs, out_specs, outputs, name):
    return pl.pallas_call(
        kernel,
        grid_spec=pltpu.PrefetchScalarGridSpec(
            num_scalar_prefetch=1, grid=(grid,), in_specs=in_specs, out_specs=out_specs
        ),
        out_shape=[jax.ShapeDtypeStruct(shape, dtype) for shape, dtype in outputs],
        compiler_params=params(),
        cost_estimate=light(name),
        name=name,
    )(picks, *inputs)


def assemble(shape, pieces, name):
    def kernel(*refs):
        for (first, column, piece), ref in zip(pieces, refs):
            rows, columns = piece.shape
            refs[-1][first : first + rows, column : column + columns] = ref[...]

    values = [piece for _, _, piece in pieces]
    return local_call(kernel, values, [(shape, values[0].dtype)], name)[0]


def product(left, right, kind, dtype, tile, part=0, size=None, block=0, rows=None):
    contract = {"nn": ((1,), (0,)), "nt": ((1,), (1,)), "tn": ((0,), (0,))}[kind]
    size = right.shape[0] if size is None else size
    rows = left.shape[0] if rows is None else rows
    if kind == "tn":
        shape, steps = (left.shape[1], right.shape[1]), left.shape[1] // tile
        specs = [
            pl.BlockSpec((rows, tile), lambda j, s: (block, j)),
            pl.BlockSpec((size, right.shape[1]), lambda j, s: (s[0], 0)),
        ]
        out = pl.BlockSpec((tile, shape[1]), lambda j, s: (j, 0))
    else:
        width = right.shape[1] if kind == "nn" else size
        shape, steps = (rows, width), width // tile
        if kind == "nn":
            right_spec = pl.BlockSpec((size, tile), lambda j, s: (s[0], j))
        else:
            right_spec = pl.BlockSpec(
                (tile, right.shape[1]), lambda j, s: (s[0] * (size // tile) + j, 0)
            )
        specs = [pl.BlockSpec((rows, left.shape[1]), lambda j, s: (block, 0)), right_spec]
        out = pl.BlockSpec((rows, tile), lambda j, s: (0, j))

    def kernel(picks, left_ref, right_ref, out_ref):
        out_ref[...] = lax.dot_general(
            left_ref[...], right_ref[...], (contract, ((), ())), preferred_element_type=F32
        ).astype(out_ref.dtype)

    return grid_call(
        kernel, steps, scalars(part), (left, right), specs, [out], [(shape, dtype)], "product_" + kind
    )[0]


def product_onto(left, right, part, size, own, tile, name):
    rows, width = own.shape
    half = rows // 2

    def kernel(picks, left_ref, right_ref, own_ref, kept_ref, sent_ref):
        total = own_ref[...] + dot_nn(left_ref[...], right_ref[...])
        kept_ref[...] = total[:half]
        sent_ref[...] = total[half:].astype(BF16)

    return grid_call(
        kernel,
        width // tile,
        scalars(part),
        (left, right, own),
        [
            pl.BlockSpec(left.shape, lambda j, s: (0, 0)),
            pl.BlockSpec((size, tile), lambda j, s: (s[0], j)),
            pl.BlockSpec((rows, tile), lambda j, s: (0, j)),
        ],
        [pl.BlockSpec((half, tile), lambda j, s: (0, j))] * 2,
        [((half, width), F32), ((half, width), BF16)],
        name,
    )


def heads_forward(scaled, query_weight, key_weight, value_weight, part, dtype):
    group, features = scaled.shape
    query_part, tile = query_weight.shape[1] // 2, key_weight.shape[1] // 2
    steps = query_part // tile

    def kernel(picks, x_ref, query_ref, key_ref, value_ref, out_ref):
        step = pl.program_id(0)
        for condition, ref in (
            (step < steps, query_ref),
            (step == steps, key_ref),
            (step == steps + 1, value_ref),
        ):

            @pl.when(condition)
            def _():
                out_ref[...] = dot_nn(x_ref[...], ref[...]).astype(out_ref.dtype)

    return grid_call(
        kernel,
        steps + 2,
        scalars(part),
        (scaled, query_weight, key_weight, value_weight),
        [
            pl.BlockSpec((group, features), lambda j, s: (0, 0)),
            pl.BlockSpec(
                (features, tile), lambda j, s: (0, s[0] * steps + jnp.minimum(j, steps - 1))
            ),
            pl.BlockSpec((features, tile), lambda j, s: (0, s[0])),
            pl.BlockSpec((features, tile), lambda j, s: (0, s[0])),
        ],
        [pl.BlockSpec((group, tile), lambda j, s: (0, j))],
        [((group, query_part + 2 * tile), dtype)],
        "heads_forward",
    )[0]


def heads_backward(grads, query_weight, key_weight, value_weight, part, own=None):
    group = grads.shape[0]
    half = group // 2
    features = query_weight.shape[0]
    query_part, key_part = query_weight.shape[1] // 2, key_weight.shape[1] // 2
    tile = features // 2

    def kernel(picks, grads_ref, query_ref, key_ref, value_ref, *refs):
        total = dot_nt(grads_ref[:, :query_part], query_ref[...])
        total += dot_nt(grads_ref[:, query_part : query_part + key_part], key_ref[...])
        total += dot_nt(grads_ref[:, query_part + key_part :], value_ref[...])
        if own is None:
            refs[0][...] = total
        else:
            total += refs[0][...]
            refs[1][...] = total[:half]
            refs[2][...] = total[half:].astype(BF16)

    whole = pl.BlockSpec((group, tile), lambda j, s: (0, j))
    split = pl.BlockSpec((half, tile), lambda j, s: (0, j))
    outputs = [((group, features), F32)]
    if own is not None:
        outputs = [((half, features), F32), ((half, features), BF16)]
    return grid_call(
        kernel,
        2,
        scalars(part),
        (grads, query_weight, key_weight, value_weight) + (() if own is None else (own,)),
        [
            pl.BlockSpec(grads.shape, lambda j, s: (0, 0)),
            pl.BlockSpec((tile, query_part), lambda j, s: (j, s[0])),
            pl.BlockSpec((tile, key_part), lambda j, s: (j, s[0])),
            pl.BlockSpec((tile, key_part), lambda j, s: (j, s[0])),
        ]
        + ([] if own is None else [whole]),
        [whole] if own is None else [split, split],
        outputs,
        "heads_backward",
    )


def up_kernel(picks, mid_ref, gate_ref, up_ref, *refs):
    parts = 4
    gate_parts, up_parts = refs[:parts], refs[parts : 2 * parts]
    kept_ref, *got_refs = refs[2 * parts : -3]
    gate_grad_ref, up_grad_ref, act_ref = refs[-3:]
    features = gate_ref.shape[0]
    share = gate_parts[0].shape[0]

    def columns(own_ref, part_refs):
        total = dot_nn(mid_ref[:, :features], own_ref[...])
        for i, ref in enumerate(part_refs):
            at = pl.multiple_of(features + picks[1 + i] * share, share)
            total += dot_nn(mid_ref[:, pl.ds(at, share)], ref[...])
        return total

    gate = columns(gate_ref, gate_parts)
    up = columns(up_ref, up_parts)
    got = jnp.concatenate([ref[...] for ref in got_refs], axis=0)
    act_grad = kept_ref[...] + got.astype(F32)
    sigmoid = jax.nn.sigmoid(gate)
    silu = gate * sigmoid
    act_ref[...] = (silu * up).astype(BF16)
    gate_grad_ref[...] = (act_grad * up * sigmoid * (1.0 + gate * (1.0 - sigmoid))).astype(BF16)
    up_grad_ref[...] = (act_grad * silu).astype(BF16)


def gate_and_up(mid, gate, up, base, pieces, places, kept, got):
    rows = mid.shape[0]
    features = gate.shape[0]
    width = kept.shape[1]
    tile = width // 3
    share = pieces[0][0].shape[0]

    def columns(height, first):
        return pl.BlockSpec((height, tile), lambda j, s: (0, first + j))

    own = pl.BlockSpec((features, tile), lambda j, s: (0, 3 * s[0] + j))
    return grid_call(
        up_kernel,
        3,
        scalars(base, *places),
        (mid, gate, up, *pieces[0], *pieces[1], kept, *got),
        [pl.BlockSpec(mid.shape, lambda j, s: (0, 0)), own, own]
        + [columns(share, 0)] * (2 * len(places))
        + [columns(rows, 0)]
        + [columns(g.shape[0], 0) for g in got],
        [columns(rows, 0)] * 3,
        [((rows, width), BF16)] * 3,
        "gate_and_up",
    )


def up_back_kernel(picks, gate_grad_ref, up_grad_ref, gate_ref, up_ref, *refs):
    *pieces, out_ref = refs
    count = len(pieces) // 2
    features = gate_ref.shape[0]
    share = pieces[0].shape[0]
    gate_grad, up_grad = gate_grad_ref[...], up_grad_ref[...]
    for i in range(features // (2 * share)):
        at = slice(i * 2 * share, (i + 1) * 2 * share)
        total = dot_nt(gate_grad, gate_ref[at, :]) + dot_nt(up_grad, up_ref[at, :])
        out_ref[:, at] = total.astype(out_ref.dtype)
    for i in range(count):
        total = dot_nt(gate_grad, pieces[i][...]) + dot_nt(up_grad, pieces[count + i][...])
        at = pl.multiple_of(features + picks[1 + i] * share, share)
        out_ref[:, pl.ds(at, share)] = total.astype(out_ref.dtype)


def gate_and_up_back(gate_grad, up_grad, block, gate, up, base, pieces, places, dtype):
    rows = gate_grad.shape[0] // 2
    width = gate_grad.shape[1]
    features = gate.shape[0]
    grads = pl.BlockSpec((rows, width), lambda j, s: (block, 0))
    own = pl.BlockSpec((features, width), lambda j, s: (0, s[0]))
    pieces = (*pieces[0], *pieces[1])
    piece = pl.BlockSpec(pieces[0].shape, lambda j, s: (0, 0))
    shape = (rows, features + len(places) * pieces[0].shape[0])
    return grid_call(
        up_back_kernel,
        1,
        scalars(base, *places),
        (gate_grad, up_grad, gate, up, *pieces),
        [grads, grads, own, own] + [piece] * len(pieces),
        [pl.BlockSpec(shape, lambda j, s: (0, 0))],
        [(shape, dtype)],
        "gate_and_up_back",
    )[0]


def in_place(weight):
    return pltpu.with_memory_space_constraint(weight, pltpu.MemorySpace.HBM)


def my_bit(bit):
    return (lax.axis_index("dp") // bit) % 2


def view(shape, columns=None, **at):
    at = {int(axis[1:]): place for axis, place in at.items()}
    parts, part = columns or (1, 0)
    last = len(shape) - 1
    block = tuple(
        None if axis in at else length // (parts if axis == last else 1)
        for axis, length in enumerate(shape)
    )
    return pl.BlockSpec(
        block,
        lambda j, s: tuple(
            s[at[axis]] if axis in at else (part if axis == last else 0)
            for axis in range(len(shape))
        ),
    )


def without(shape, *axes):
    return tuple(length for axis, length in enumerate(shape) if axis not in axes)


def take(value, axis, index, columns=None):
    shape = without(value.shape, axis)
    shape = shape[:-1] + (shape[-1] // (columns or (1, 0))[0],)

    def kernel(picks, in_ref, out_ref):
        out_ref[...] = in_ref[...].astype(BF16)

    return grid_call(
        kernel,
        1,
        scalars(index),
        (value,),
        [view(value.shape, columns, **{f"a{axis}": 0})],
        [view(shape)],
        [(shape, BF16)],
        "take",
    )[0]


def start_stage(value, axis, bit):
    return swap_dp(take(value, axis, 1 - my_bit(bit)), bit)


def end_stage(value, got, axis, bit, next_axis=None, next_index=None, columns=None):
    joined = got.shape
    side = {} if axis is None else {f"a{axis}": 0}
    mine = 0 if axis is None else my_bit(bit)
    if next_axis is None:

        def kernel(picks, value_ref, got_ref, out_ref):
            out_ref[...] = value_ref[...].astype(F32) + got_ref[...].astype(F32)

        return grid_call(
            kernel,
            1,
            scalars(mine),
            (value, got),
            [view(value.shape, **side), view(joined)],
            [view(joined)],
            [(joined, F32)],
            "join",
        )[0]
    shape = without(joined, next_axis)
    behind = next_axis + (1 if axis is not None and next_axis >= axis else 0)

    def kernel(picks, keep_ref, keep_got, send_ref, send_got, kept_ref, sent_ref):
        kept_ref[...] = keep_ref[...].astype(F32) + keep_got[...].astype(F32)
        sent_ref[...] = (send_ref[...].astype(F32) + send_got[...].astype(F32)).astype(BF16)

    return grid_call(
        kernel,
        1,
        scalars(mine, next_index, 1 - next_index),
        (value, got, value, got),
        [
            view(value.shape, columns, **side, **{f"a{behind}": 1}),
            view(joined, **{f"a{next_axis}": 1}),
            view(value.shape, columns, **side, **{f"a{behind}": 2}),
            view(joined, **{f"a{next_axis}": 2}),
        ],
        [view(shape)] * 2,
        [(shape, F32), (shape, BF16)],
        "join_and_split",
    )


def add_got(kept, got):
    def kernel(kept_ref, got_ref, out_ref):
        out_ref[...] = kept_ref[...].astype(F32) + got_ref[...].astype(F32)

    return local_call(kernel, (kept, got), [(kept.shape, F32)], "add_got")[0]


def split_top(own, other, row):
    mine = my_bit(lax.axis_size("dp") // 2) == row

    def kernel(picks, own_ref, other_ref, kept_ref, sent_ref):
        for first, second, flag in ((own_ref, other_ref, 1), (other_ref, own_ref, 0)):

            @pl.when(picks[0] == flag)
            def _():
                kept_ref[...] = first[...].astype(F32)
                sent_ref[...] = second[...].astype(BF16)

    spec = view(own.shape)
    return grid_call(
        kernel,
        1,
        scalars(mine),
        (own, other),
        [spec, spec],
        [spec, spec],
        [(own.shape, F32), (own.shape, BF16)],
        "split_top",
    )


def join_core_kernel(kept_ref, got_ref, own_ref, row_ref, z_ref, row_both_ref, z_both_ref):
    half, features = own_ref.shape
    quarter = half // 2
    near = kept_ref[:half, :] + got_ref[:half, :].astype(F32)
    far = kept_ref[half:, :] + got_ref[half:, :].astype(F32)
    own_ref[...] = near[:, :features]
    row_ref[...] = near[:, features:]
    z_ref[...] = far[:, :features]
    row_both_ref[...] = far[:quarter, features:].astype(BF16)
    z_both_ref[...] = far[quarter:, features:].astype(BF16)


def join_corner_kernel(row_ref, z_ref, via_row_ref, via_z_ref, to_row_ref, to_z_ref):
    quarter = via_row_ref.shape[0]
    to_row_ref[:quarter, :] = row_ref[:quarter, :].astype(BF16)
    to_row_ref[quarter:, :] = (row_ref[quarter:, :] + via_z_ref[...].astype(F32)).astype(BF16)
    to_z_ref[:quarter, :] = (z_ref[:quarter, :] + via_row_ref[...].astype(F32)).astype(BF16)
    to_z_ref[quarter:, :] = z_ref[quarter:, :].astype(BF16)


def norm_sums_kernel(*refs):
    parts = refs[:-6]
    base_ref, inverse_ref, gain_ref, grad_ref, sums_ref, gain_grad_ref = refs[-6:]
    grad = sum(part[...].astype(F32) for part in parts)
    unit = base_ref[...].astype(F32) * column_of(inverse_ref[...])
    along = grad * unit
    grad_ref[...] = grad
    sums_ref[...] = lanes_of(jnp.sum(along * gain_ref[...], axis=1, keepdims=True))
    gain_grad_ref[...] = jnp.sum(along, axis=0, keepdims=True)


def norm_sums(parts, base, inverse, gain):
    rows, features = base.shape
    return local_call(
        norm_sums_kernel,
        (*parts, base, inverse, gain),
        [((rows, features), F32), ((8, rows), F32), ((1, features), F32)],
        "norm_sums",
    )


def norm_grad_kernel(
    grad_ref, base_ref, inverse_ref, gain_ref, sums_ref, got_sums_ref, rest_ref, *out_refs
):
    inverse = column_of(inverse_ref[...])
    unit = base_ref[...].astype(F32) * inverse
    mean = column_of(sums_ref[...] + got_sums_ref[...]) * (1.0 / D)
    out = rest_ref[...].astype(F32) + inverse * (grad_ref[...] * gain_ref[...] - unit * mean)
    for out_ref in out_refs:
        out_ref[...] = out.astype(out_ref.dtype)


def norm_grad(grad, base, inverse, gain, sums, got_sums, rest, dtypes):
    return local_call(
        norm_grad_kernel,
        (grad, base, inverse, gain, sums, got_sums, rest),
        [(grad.shape, dtype) for dtype in dtypes],
        "norm_grad",
    )


def middle_kernel(x_ref, part_ref, got_ref, mid_ref, square_ref):
    mid = x_ref[...].astype(F32) + part_ref[...] + got_ref[...].astype(F32)
    mid_ref[...] = mid
    square_ref[...] = lanes_of(jnp.sum(mid * mid, axis=1, keepdims=True))


def normed_kernel(mid_ref, square_ref, got_ref, gain_ref, normed_ref, inverse_ref):
    inverse = lax.rsqrt((square_ref[...] + got_ref[...]) * (1.0 / D) + EPSILON)
    inverse_ref[...] = inverse
    unit = mid_ref[...].astype(F32) * column_of(inverse)
    normed_ref[...] = (unit * gain_ref[...]).astype(BF16)


def scaled_kernel(own_ref, got_ref, gain_ref, x_ref, scaled_ref, square_ref):
    half = own_ref.shape[0]
    for first, ref in ((0, own_ref), (half, got_ref)):
        at = slice(first, first + half)
        values = ref[...].astype(F32)
        x_ref[at, :] = ref[...]
        scaled_ref[at, :] = (values * gain_ref[...]).astype(BF16)
        square_ref[:, at] = lanes_of(jnp.sum(values * values, axis=1, keepdims=True))


def normed_in_kernel(x_ref, inverse_ref, gain_ref, normed_ref):
    unit = x_ref[...].astype(F32) * column_of(inverse_ref[...])
    normed_ref[...] = (unit * gain_ref[...]).astype(BF16)


def block_of(weight, block_row, block_column, shape):
    def kernel(picks, in_ref, out_ref):
        out_ref[...] = in_ref[...]

    return grid_call(
        kernel,
        1,
        scalars(block_row, block_column),
        (weight,),
        [pl.BlockSpec(shape, lambda j, s: (s[0], s[1]))],
        [pl.BlockSpec(shape, lambda j, s: (0, 0))],
        [(shape, BF16)],
        "block_of",
    )[0]


def side_kernel(*refs):
    kept_ref, sent_ref = refs[-2:]
    parts = (len(refs) - 2) // 2
    width = refs[0].shape[-1]
    for i in range(parts):
        total = refs[i][...].astype(F32) + refs[parts + i][...].astype(F32)
        at = slice(i * width, (i + 1) * width)
        kept_ref[:, :, at] = total[0]
        sent_ref[:, :, at] = total[1].astype(BF16)


def layer_out_kernel(mid_ref, kept_ref, got_ref, out_ref):
    out_ref[...] = (mid_ref[...] + kept_ref[...] + got_ref[...].astype(F32)).astype(BF16)


def out_near_kernel(kept_ref, got_ref, near_ref, far_ref):
    half = near_ref.shape[0]
    near_ref[...] = kept_ref[:half, :] + got_ref[:half, :].astype(F32)
    far_ref[...] = (kept_ref[half:, :] + got_ref[half:, :].astype(F32)).astype(BF16)


def turn(values, cosine, sine):
    return values * cosine + pltpu.roll(values, HEAD_SIZE // 2, 1) * sine


def unit_of(raw):
    inverse = lax.rsqrt(jnp.mean(raw * raw, axis=-1, keepdims=True) + EPSILON)
    return raw * inverse, inverse


def scores_to_prob(query_rot, key_rot, allowed):
    scores = dot_nt(query_rot, key_rot) * (1.0 / math.sqrt(HEAD_SIZE))
    scores = jnp.where(allowed, scores, NEGATIVE)
    exps = jnp.exp(scores - jnp.max(scores, axis=-1, keepdims=True))
    return exps * (1.0 / jnp.sum(exps, axis=-1, keepdims=True))


def head_inputs(own, got, inverse_in, width):
    raw = (own[...] + got[...].astype(F32)) * inverse_in
    return [raw[:, i * HEAD_SIZE : (i + 1) * HEAD_SIZE] for i in range(width // HEAD_SIZE)]


def attend_kernel(
    query_own, query_got, key_own, key_got, value_own, value_got, inverse_ref, cosine_ref,
    sine_ref, slot_ref, start_ref, across_ref, query_gain_ref, key_gain_ref, out_ref,
):
    inverse_in = column_of(inverse_ref[...])
    cosine, sine = cosine_ref[...], sine_ref[...]
    across = across_ref[...]
    (key_raw,) = head_inputs(key_own, key_got, inverse_in, HEAD_SIZE)
    (value,) = head_inputs(value_own, value_got, inverse_in, HEAD_SIZE)
    key_rot = turn(unit_of(key_raw)[0] * key_gain_ref[...], cosine, sine).astype(BF16)
    value = value.astype(BF16)
    slots, first = column_of(slot_ref[...]), column_of(start_ref[...])
    rows = out_ref.shape[0] // 2

    for block in range(2):
        at = slice(block * rows, (block + 1) * rows)
        allowed = (across <= slots[at]) & (across >= first[at])
        for i in range(query_own.shape[1] // HEAD_SIZE):
            head = slice(i * HEAD_SIZE, (i + 1) * HEAD_SIZE)
            raw = (query_own[at, head] + query_got[at, head].astype(F32)) * inverse_in[at]
            pre = unit_of(raw)[0] * query_gain_ref[...]
            query_rot = turn(pre, cosine_ref[at, :], sine_ref[at, :]).astype(BF16)
            prob = scores_to_prob(query_rot, key_rot, allowed).astype(BF16)
            out_ref[at, head] = dot_nn(prob, value).astype(BF16)


def attend_back_kernel(
    query_own, query_got, key_own, key_got, value_own, value_got, inverse_ref, cosine_ref,
    sine_ref, slot_ref, start_ref, across_ref, query_gain_ref, key_gain_ref, grad_own, grad_got,
    out_ref, gain_ref,
):
    step = pl.program_id(0)
    repeat = query_own.shape[1] // HEAD_SIZE
    kv_heads = out_ref.shape[1] // (query_own.shape[1] + 2 * HEAD_SIZE)
    scale = 1.0 / math.sqrt(HEAD_SIZE)
    inverse_in = column_of(inverse_ref[...])
    cosine, sine = cosine_ref[...], sine_ref[...]
    across = across_ref[...]
    allowed = (across <= column_of(slot_ref[...])) & (across >= column_of(start_ref[...]))
    query_gain, key_gain = query_gain_ref[...], key_gain_ref[...]

    @pl.when(step == 0)
    def _():
        gain_ref[...] = jnp.zeros_like(gain_ref)

    (key_raw,) = head_inputs(key_own, key_got, inverse_in, HEAD_SIZE)
    (value,) = head_inputs(value_own, value_got, inverse_in, HEAD_SIZE)
    key_unit, key_inverse = unit_of(key_raw)
    key_rot = turn(key_unit * key_gain, cosine, sine).astype(BF16)
    value = value.astype(BF16)

    def norm_back(rot_grad, unit, inverse, gain, at):
        pre = rot_grad * cosine - pltpu.roll(rot_grad, HEAD_SIZE // 2, 1) * sine
        gain_ref[at : at + 1, :] += jnp.sum(pre * unit, axis=0, keepdims=True)
        scaled = pre * gain
        return inverse * (scaled - unit * jnp.mean(scaled * unit, axis=-1, keepdims=True))

    key_grad = jnp.zeros(key_raw.shape, F32)
    value_grad = jnp.zeros(key_raw.shape, F32)
    for i, query_raw in enumerate(
        head_inputs(query_own, query_got, inverse_in, query_own.shape[1])
    ):
        at = slice(i * HEAD_SIZE, (i + 1) * HEAD_SIZE)
        query_unit, query_inverse = unit_of(query_raw)
        query_rot = turn(query_unit * query_gain, cosine, sine).astype(BF16)
        prob = scores_to_prob(query_rot, key_rot, allowed)
        grad_out = (grad_own[:, at] + grad_got[:, at].astype(F32)).astype(BF16)
        prob_grad = dot_nt(grad_out, value)
        centre = jnp.sum(prob * prob_grad, axis=-1, keepdims=True)
        score_grad = (prob * (prob_grad - centre)).astype(BF16)
        value_grad += dot_tn(prob.astype(BF16), grad_out)
        key_grad += dot_tn(score_grad, query_rot)
        query_grad = norm_back(
            dot_nn(score_grad, key_rot) * scale, query_unit, query_inverse, query_gain, 0
        )
        column = pl.multiple_of((step * repeat + i) * HEAD_SIZE, HEAD_SIZE)
        out_ref[:, pl.ds(column, HEAD_SIZE)] = query_grad.astype(BF16)
    key_grad = norm_back(key_grad * scale, key_unit, key_inverse, key_gain, 1)
    column = pl.multiple_of((kv_heads * repeat + step) * HEAD_SIZE, HEAD_SIZE)
    out_ref[:, pl.ds(column, HEAD_SIZE)] = key_grad.astype(BF16)
    column = pl.multiple_of((kv_heads * (repeat + 1) + step) * HEAD_SIZE, HEAD_SIZE)
    out_ref[:, pl.ds(column, HEAD_SIZE)] = value_grad.astype(BF16)


def attention_specs(group, kv_heads, repeat):
    def block(width, first):
        return pl.BlockSpec((group, width), lambda j: (0, first + j))

    def whole(rows, columns):
        return pl.BlockSpec((rows, columns), lambda j: (0, 0))

    query = block(repeat * HEAD_SIZE, 0)
    key = block(HEAD_SIZE, kv_heads * repeat)
    value = block(HEAD_SIZE, kv_heads * (repeat + 1))
    return [query, query, key, key, value, value] + [
        whole(8, group),
        whole(group, HEAD_SIZE),
        whole(group, HEAD_SIZE),
        whole(8, group),
        whole(8, group),
        whole(1, group),
        whole(1, HEAD_SIZE),
        whole(1, HEAD_SIZE),
    ]


def attend(own, got, shared, kv_heads, repeat):
    group = own.shape[0]
    width = kv_heads * repeat * HEAD_SIZE
    return pl.pallas_call(
        attend_kernel,
        grid=(kv_heads,),
        in_specs=attention_specs(group, kv_heads, repeat),
        out_specs=pl.BlockSpec((group, repeat * HEAD_SIZE), lambda j: (0, j)),
        out_shape=jax.ShapeDtypeStruct((group, width), BF16),
        compiler_params=pltpu.CompilerParams(vmem_limit_bytes=VMEM_LIMIT),
        cost_estimate=light("attend"),
        name="attend",
    )(own, got, own, got, own, got, *shared)


def attend_back(own, got, shared, grad_own, grad_got, kv_heads, repeat):
    group, width = own.shape
    grad_block = pl.BlockSpec((group, repeat * HEAD_SIZE), lambda j: (0, j))
    return pl.pallas_call(
        attend_back_kernel,
        grid=(kv_heads,),
        in_specs=attention_specs(group, kv_heads, repeat) + [grad_block, grad_block],
        out_specs=[
            pl.BlockSpec((group, width), lambda j: (0, 0)),
            pl.BlockSpec((2, HEAD_SIZE), lambda j: (0, 0)),
        ],
        out_shape=[
            jax.ShapeDtypeStruct((group, width), BF16),
            jax.ShapeDtypeStruct((2, HEAD_SIZE), F32),
        ],
        compiler_params=pltpu.CompilerParams(vmem_limit_bytes=VMEM_LIMIT),
        cost_estimate=light("attend_back"),
        name="attend_back",
    )(own, got, own, got, own, got, *shared, grad_own, grad_got)

def shards(
    tokens,
    cotangent,
    seq_lengths,
    balance_order,
    attention_gain,
    query_weight,
    key_weight,
    value_projection,
    query_gain,
    key_norm_gain,
    output_weight,
    feedforward_gain,
    gate_weight,
    up_weight,
    down_weight,
):
    count = lax.axis_size("dp")
    levels = count.bit_length() - 1
    row = lax.axis_index("row")
    col = lax.axis_index("col")
    xbit, zbit, wbit = my_bit(1), my_bit(2), my_bit(4)
    half = tokens.shape[0]
    quarter = half // 2
    group = 2 * half
    pair = 2 * group
    features = tokens.shape[1]
    query_part = query_weight.shape[1] // 2
    key_part = key_weight.shape[1] // 2
    heads = query_part // HEAD_SIZE
    kv_heads = key_part // HEAD_SIZE
    repeat = heads // kv_heads
    ff_half = gate_weight.shape[1]
    runs = count // 8
    projections = tuple(map(in_place, (query_weight, key_weight, value_projection)))
    output_weight = in_place(output_weight)
    if runs == 1:
        gate_weight, up_weight, down_weight = map(in_place, (gate_weight, up_weight, down_weight))
    run = 2 * ff_half // count
    ff_part = ff_half // 4
    all_bits = high_bits(count)[::-1]

    def ff_block(weight, part, axis):
        if runs == 1:
            return weight, part * 2 + zbit
        pieces = [
            lax.dynamic_slice_in_dim(weight, ((part * runs + i) * 2 + zbit) * run, run, axis)
            for i in range(runs)
        ]
        return jnp.concatenate(pieces, axis=axis), 0

    moved_in = exchange(tokens)
    share = features // 4
    gate_far, far_base = ff_block(gate_weight, 1 - row, 1)
    up_far, _ = ff_block(up_weight, 1 - row, 1)
    gate_sent, up_sent = (
        block_of(weight, wbit * 2 + xbit, far_base, (share, ff_part))
        for weight in (gate_far, up_far)
    )
    got_gate, got_up = swap_row(gate_sent), swap_row(up_sent)

    base_ids = jnp.arange(half, dtype=jnp.int32)
    local_ids = jnp.concatenate([col * half + base_ids, (1 - col) * half + base_ids])
    slot_ids = jnp.arange(group, dtype=jnp.int32)
    slot = jnp.sum(
        jnp.where(balance_order[0][None, :] == local_ids[:, None], slot_ids[None, :], 0), axis=1
    )
    lengths = seq_lengths[0]
    seq_ends = jnp.cumsum(lengths)
    starts = seq_ends - lengths
    segment = jnp.sum((slot[:, None] >= seq_ends[None, :]).astype(jnp.int32), axis=1)
    hits = segment[:, None] == jnp.arange(lengths.shape[0], dtype=jnp.int32)[None, :]
    start = jnp.sum(jnp.where(hits, starts[None, :], 0), axis=1)
    cosine, sine = rotary_tables(slot - start)
    slot_lanes = jnp.broadcast_to(slot.astype(F32)[None], (8, group))
    start_lanes = jnp.broadcast_to(start.astype(F32)[None], (8, group))
    moved_in, cosine, sine, slot_lanes, start_lanes, got_gate, got_up = together(
        moved_in, cosine, sine, slot_lanes, start_lanes, got_gate, got_up
    )

    gain_in = attention_gain.astype(F32)[None]
    gain_mid = feedforward_gain.astype(F32)[None]
    x_low, scaled_in, square = local_call(
        scaled_kernel,
        (moved_in, swap_col(moved_in), gain_in),
        [((group, features), BF16), ((group, features), BF16), ((8, group), F32)],
        "scaled",
    )
    moved_grad = exchange(after(cotangent, moved_in))
    heads_sent = heads_forward(after(scaled_in, got_gate, got_up), *projections, 1 - row, BF16)
    got_square = swap_row(square)
    got_heads = swap_row(heads_sent)
    kept_heads = heads_forward(after(scaled_in, heads_sent), *projections, row, F32)
    got_gate, got_up = together(got_gate, got_up, heads_sent)[:2]
    got_gate_x, got_up_x = swap_dp(got_gate, 1), swap_dp(got_up, 1)
    got_gate_w, got_up_w = swap_dp(got_gate, 4), swap_dp(got_up, 4)

    down_own, own_at = ff_block(down_weight, row, 0)
    down_other, other_at = ff_block(down_weight, 1 - row, 0)

    def act_back(rows_of, weight, at, dtype):
        return product(rows_of, weight, "nt", dtype, ff_part // 3, at, ff_part)

    moved_grad = after(moved_grad, kept_heads)
    grad_z = swap_z(moved_grad)
    grad_near = swap_col(moved_grad)
    act_sent = [
        act_back(rows_of, down_other, other_at, BF16) for rows_of in (moved_grad, grad_near)
    ]
    got_heads, kept_heads, got_square, got_gate_x, got_gate_w, grad_z, *act_sent = together(
        got_heads, kept_heads, got_square, got_gate_x, got_gate_w, grad_z, *act_sent
    )
    inverse_in = lax.rsqrt((square + got_square) / D + EPSILON)
    shared = (
        inverse_in,
        cosine,
        sine,
        slot_lanes,
        start_lanes,
        slot_lanes[:1],
        query_gain.astype(F32)[None],
        key_norm_gain.astype(F32)[None],
    )
    got_act = [swap_row(act_sent[0])]
    got_gate_wx = swap_dp(got_gate_w, 1)
    grad_far = swap_col(grad_z)
    attention = attend(kept_heads, got_heads, shared, kv_heads, repeat)
    attention, got_act[0], grad_far = together(attention, got_act[0], grad_far)
    attention_other = swap_row(attention)
    got_act.append(swap_row(after(act_sent[1], attention)))
    out_own = product(attention, output_weight, "nn", F32, features // 2, row, query_part)
    far_sent = [
        act_back(after(rows_of, out_own), down_other, other_at, BF16)
        for rows_of in (grad_z, grad_far)
    ]
    attention_other, got_act[1], got_gate_wx, got_up_x, got_up_w, out_own, *far_sent = together(
        attention_other, got_act[1], got_gate_wx, got_up_x, got_up_w, out_own, *far_sent
    )
    got_up_wx = swap_dp(got_up_w, 1)
    out_kept, out_sent = product_onto(
        attention_other, output_weight, 1 - row, query_part, out_own, features // 2, "out_proj"
    )
    out_got = swap_col(out_sent)
    stream_mid, square_mid = local_call(
        middle_kernel,
        (moved_in, out_kept, out_got),
        [((half, features), F32), ((8, half), F32)],
        "middle",
    )
    got_square = swap_row(square_mid)
    grad_all = assemble(
        (pair, features),
        [
            (0, 0, moved_grad),
            (half, 0, grad_z),
            (group, 0, grad_near),
            (group + half, 0, after(grad_far, square_mid)),
        ],
        "grad_all",
    )
    normed_mid, inverse_mid = local_call(
        normed_kernel,
        (stream_mid, square_mid, got_square, gain_mid),
        [((half, features), BF16), ((8, half), F32)],
        "normed",
    )

    by_row = swap_row(normed_mid)
    by_z = swap_z(normed_mid)
    act_kept = act_back(after(grad_all, normed_mid), down_own, own_at, F32)
    by_row, by_z, act_kept, got_up_wx = together(by_row, by_z, act_kept, got_up_wx)
    corner_a = swap_row(by_z[:quarter])
    corner_b = swap_z(by_row[quarter:])
    got_act.extend(swap_row(after(sent, by_row)) for sent in far_sent)
    near = [
        (0, 0, normed_mid),
        (0, features, by_row),
        (half, 0, by_z),
        (half, features, corner_a),
        (half + quarter, features, corner_b),
    ]
    crossed = [(group + first, at, swap_col(piece)) for first, at, piece in near]
    mid_all = assemble((pair, 2 * features), near + crossed, "mid_all")

    gate_own, own_base = ff_block(gate_weight, row, 1)
    up_own, _ = ff_block(up_weight, row, 1)
    places = (
        wbit * 2 + xbit,
        wbit * 2 + 1 - xbit,
        (1 - wbit) * 2 + xbit,
        (1 - wbit) * 2 + 1 - xbit,
    )
    pieces = (
        (got_gate, got_gate_x, got_gate_w, got_gate_wx),
        (got_up, got_up_x, got_up_w, got_up_wx),
    )
    up_weights = (gate_own, up_own, own_base, pieces, places)
    gate_grad, up_grad, activated = gate_and_up(
        mid_all, *up_weights, act_kept, (got_act[0], got_act[2], got_act[1], got_act[3])
    )

    quarters = [activated[i * half : (i + 1) * half] for i in range(4)]
    others = [swap_row(quarters[0])]
    line = Line(activated)
    top_bit, lower_bits = all_bits[0], all_bits[1:]

    def up_rows(grad_part):
        whole = product(mid_all, grad_part, "tn", BF16, features // 2)
        return whole.reshape((2,) * (levels + 1) + (features // count, ff_part))

    def down_part(part, rows_of):
        whole = product(part, rows_of, "tn", BF16, ff_part // 2)
        return split_rows(whole, levels - 2)

    def first_stage(value, axis, bit):
        sent = line.passed(take(value, axis, 1 - my_bit(bit)))
        return swap_dp(sent, bit)

    def late_stage(value, got, axis, bit, next_axis, next_bit):
        kept, sent = end_stage(value, line.hold(got), axis, bit, next_axis, my_bit(next_bit))
        return kept, swap_dp(line.passed(sent), next_bit)

    mid_sent = line.passed(gate_and_up_back(gate_grad, up_grad, 1, *up_weights, BF16))
    got_mid = swap_col(mid_sent)
    gate_grad, others[0] = line.hold(gate_grad, others[0])
    gate_rows = up_rows(gate_grad)
    gate_got = first_stage(gate_rows, levels, 1)
    mid_kept = gate_and_up_back(line.hold(gate_grad), up_grad, 0, *up_weights, F32)
    block = (half, features)
    mid_own, to_row, to_z, row_both, z_both = local_call(
        join_core_kernel,
        (mid_kept, got_mid),
        [(block, F32)] * 3 + [((quarter, features), BF16)] * 2,
        "join_core",
    )
    via_row = swap_row(row_both)
    via_z = swap_z(z_both)
    line.passed(row_both)
    up_cols = up_rows(line.hold(up_grad))
    up_got = first_stage(up_cols, levels, 1)
    via_row, via_z = line.hold(via_row, via_z)
    to_row, to_z = local_call(
        join_corner_kernel,
        (to_row, to_z, via_row, via_z),
        [(block, BF16), (block, BF16)],
        "join_corner",
    )
    got_row, got_z = swap_row(to_row), swap_z(to_z)
    line.passed(to_row)
    down_first = down_part(activated, line.hold(grad_all))
    down_got = first_stage(down_first, down_first.ndim - 3, 1)
    got_row, got_z = line.hold(got_row, got_z)
    normed_mid_grad, mid_sum, feedforward_part = norm_sums(
        (mid_own, got_row, got_z), stream_mid, inverse_mid, gain_mid
    )
    got_sum = swap_row(line.passed(mid_sum))
    others.append(swap_row(line.hold(quarters[1])))
    got_sum, gate_got = line.hold(got_sum, gate_got)
    stream_mid_grad, branch_low = norm_grad(
        normed_mid_grad, stream_mid, inverse_mid, gain_mid, mid_sum, got_sum, moved_grad, (F32, BF16)
    )
    line.passed(branch_low)
    branch_got = swap_col(branch_low)
    gate_rows, gate_got = late_stage(gate_rows, gate_got, levels, 1, 1, top_bit)
    branch = assemble(
        (group, features), [(0, 0, branch_low), (half, 0, line.hold(branch_got))], "branch"
    )
    attention_sent = product(branch, output_weight, "nt", BF16, query_part, 1 - row, query_part)
    attention_sent, others[1] = together(attention_sent, others[1])
    got_attention = swap_row(attention_sent)
    line.passed(attention_sent)

    others.extend(swap_row(line.hold(part)) for part in quarters[2:])
    attention_kept = line.passed(
        product(line.hold(branch), output_weight, "nt", F32, query_part, row, query_part)
    )
    output_first, output_sent = [], []
    for part in (attention, attention_other):
        whole = product(line.hold(part), branch, "tn", BF16, query_part // 2)
        whole = split_rows(whole, levels - 1)
        output_sent.append(line.passed(take(whole, whole.ndim - 4, 1 - zbit)))
        output_first.append(whole)
    got_attention, *output_sent = line.hold(got_attention, *output_sent)
    line.passed(got_attention)
    output_got = [swap_dp(sent, 2) for sent in output_sent]
    projected_grad, head_gains = attend_back(
        kept_heads, got_heads, shared, attention_kept, line.hold(got_attention), kv_heads, repeat
    )
    projected_grad, others[2], others[3], gate_got, up_got, down_got = together(
        projected_grad, others[2], others[3], gate_got, up_got, down_got
    )
    projected_other = swap_row(projected_grad)
    line.passed(projected_grad)
    up_cols, up_got = late_stage(up_cols, up_got, levels, 1, 1, top_bit)

    (normed_in,) = local_call(
        normed_in_kernel,
        (x_low, line.hold(inverse_in), gain_in),
        [((group, features), BF16)],
        "normed_in",
    )

    def projection_rows(part):
        whole = split_rows(product(normed_in, part, "tn", BF16, features // 2), levels)
        return whole, first_stage(whole, levels - 2, 2)

    heads_first, heads_got = projection_rows(line.hold(projected_grad))
    activated_other = assemble(
        (pair, ff_part),
        [(i * half, 0, other) for i, other in enumerate(line.hold(*others))],
        "activated_other",
    )
    down_second = down_part(activated_other, grad_all)
    down_got_other = first_stage(down_second, down_second.ndim - 3, 1)
    in_own = line.passed(heads_backward(line.hold(projected_grad), *projections, row)[0])
    out_own = line.passed(
        product(line.hold(activated), down_own, "nn", F32, features // 2, own_at, ff_part)
    )
    out_kept, out_sent = product_onto(
        line.hold(activated_other),
        down_other,
        other_at,
        ff_part,
        out_own,
        features // 2,
        "down_proj",
    )
    out_got = swap_col(line.passed(out_sent))
    out_near, out_far = local_call(
        out_near_kernel, (out_kept, line.hold(out_got)), [(block, F32), (block, BF16)], "out_near"
    )
    line.passed(out_far)
    projected_other, in_own, out_far, down_got_other, *output_got = line.hold(
        projected_other, in_own, out_far, down_got_other, *output_got
    )
    layer_z = swap_z(out_far)
    line.passed(projected_other)
    in_kept, in_sent = heads_backward(projected_other, *projections, 1 - row, in_own)
    in_got = swap_col(line.passed(in_sent))
    down_rows = []
    for v, got in ((down_first, down_got), (down_second, down_got_other)):
        down_rows.append(line.passed(end_stage(v, line.hold(got), v.ndim - 3, 1)))
    down_kept, down_sent = split_top(*down_rows, row)
    down_got = swap_dp(line.passed(down_sent), top_bit)
    in_values = (moved_in, inverse_in[:, :half], gain_in)
    normed_in_grad, in_sum, attention_part = norm_sums(
        (in_kept, line.hold(in_got)), *in_values
    )
    got_sum = swap_row(line.passed(in_sum))
    output_rows, output_got = zip(
        *(
            late_stage(v, got, v.ndim - 4, 2, v.ndim - 4, 1)
            for v, got in zip(output_first, output_got)
        )
    )
    heads_second, heads_got_other = projection_rows(line.hold(projected_other))
    got_sum, up_got, heads_got, layer_z = line.hold(got_sum, up_got, heads_got, layer_z)
    (stream_grad,) = norm_grad(
        normed_in_grad, *in_values, in_sum, got_sum, stream_mid_grad, (BF16,)
    )
    (layer_out,) = local_call(
        layer_out_kernel, (stream_mid, out_near, line.hold(layer_z)), [(block, BF16)], "layer_out"
    )
    rows = two_rows(attention_part[0]) + two_rows(feedforward_part[0])
    rows += two_rows(head_gains.reshape(-1))
    back = exchange(line.passed(with_rows((stream_grad, layer_out), rows)))

    output_rows = [
        line.passed(add_got(kept, line.hold(got))) for kept, got in zip(output_rows, output_got)
    ]
    output_kept, output_sent = split_top(*output_rows, row)
    output_got = swap_dp(line.passed(output_sent), top_bit)
    heads_own, heads_got = late_stage(heads_first, heads_got, levels - 2, 2, levels - 2, 1)
    for bit in lower_bits:
        gate_rows, gate_got = late_stage(gate_rows, gate_got, None, None, 1, bit)
        up_cols, up_got = late_stage(up_cols, up_got, None, None, 1, bit)
    shape = gate_rows.shape[1:-1] + (2 * ff_part,)
    side_own, side_sent = local_call(
        side_kernel,
        (gate_rows, up_cols, *line.hold(gate_got, up_got)),
        [(shape, F32), (shape, BF16)],
        "side",
    )
    side_got = swap_row(line.passed(side_sent))
    back, side_got, heads_got, heads_got_other, down_got = line.hold(
        back, side_got, heads_got, heads_got_other, down_got
    )
    line.passed(side_got)
    heads_own, heads_got = late_stage(heads_own, heads_got, None, None, 0, top_bit)
    heads_other, heads_got_other = late_stage(
        heads_second, heads_got_other, levels - 2, 2, levels - 2, 1
    )
    side_got = line.hold(side_got)
    sent = jnp.stack([pick(part, 1 - zbit, 0).astype(BF16) for part in (side_own, side_got)])
    side_z = swap_z(line.passed(sent))
    output_got, heads_got, heads_got_other, side_z = line.hold(
        output_got, heads_got, heads_got_other, side_z
    )
    line.passed(heads_got)
    heads_other, heads_got_other = late_stage(heads_other, heads_got_other, None, None, 0, top_bit)

    def finish(kept, got):
        value = line.passed(add_got(kept, line.hold(got)))
        for bit in lower_bits:
            value = pick(value, my_bit(bit), 0) + swap_dp(
                pick(value, 1 - my_bit(bit), 0).astype(BF16), bit
            ).astype(F32)
        return value

    output_weight_grad = finish(output_kept, output_got)
    down_grad = finish(down_kept, down_got)
    heads_grad_own = finish(heads_own, heads_got)

    def up_columns(at):
        columns = slice(at, at + ff_part)
        keep = [pick(part[..., columns], zbit, 0) for part in (side_own, side_got.astype(F32))]
        swapped = side_z[..., columns].astype(F32)
        table = [
            by_half(zbit, near_piece, far_piece)
            for near_piece, far_piece in zip(
                by_half(row, keep[0], keep[1]), by_half(row, swapped[0], swapped[1])
            )
        ]
        return jnp.concatenate(
            [
                table[part][z][:, i * run : (i + 1) * run]
                for part in range(2)
                for i in range(runs)
                for z in range(2)
            ],
            axis=1,
        )

    gate_weight_grad = line.passed(up_columns(0))
    up_weight_grad = up_columns(ff_part)
    heads_grad_other = finish(heads_other, heads_got_other)

    def head_grad(start, width):
        own = heads_grad_own[:, start : start + width]
        other = heads_grad_other[:, start : start + width]
        return jnp.concatenate(by_half(row, own, other), axis=1)

    query_weight_grad = head_grad(0, query_part)
    key_weight_grad = head_grad(query_part, key_part)
    value_weight_grad = head_grad(query_part + key_part, key_part)

    back = back.reshape(count, -1, features).astype(F32)
    share = half // count
    grad_back = back[:, :share].reshape(half, features)
    out_back = back[:, share : 2 * share].reshape(half, features)
    totals = jnp.sum(back[:, 2 * share :], axis=0)
    gains = jnp.concatenate([totals[i] + totals[i + 1] for i in (0, 2, 4)])[None]
    gains = gains + swap_col(gains)
    gain_low, gain_high = (part[0] for part in by_half(row, gains, swap_row(gains)))
    attention_total = jnp.concatenate([gain_low[:features], gain_high[:features]])
    feedforward_total = jnp.concatenate(
        [gain_low[features : 2 * features], gain_high[features : 2 * features]]
    )
    head_totals = (gain_low + gain_high)[2 * features :]
    return (
        out_back,
        grad_back,
        attention_total,
        query_weight_grad,
        key_weight_grad,
        value_weight_grad,
        head_totals[:HEAD_SIZE],
        head_totals[HEAD_SIZE : 2 * HEAD_SIZE],
        output_weight_grad,
        feedforward_total,
        gate_weight_grad,
        up_weight_grad,
        down_grad,
    )


def solution(mesh):
    placed = (
        P(("dp", "col"), "row"),
        P(("dp", "col"), "row"),
        P("dp", None),
        P("dp", None),
        P("row"),
        P("row", "col"),
        P("row", "col"),
        P("row", "col"),
        P(),
        P(),
        P("col", "row"),
        P("row"),
        P("row", "col"),
        P("row", "col"),
        P("col", "row"),
    )
    return jax.shard_map(
        shards,
        mesh=mesh,
        in_specs=placed,
        out_specs=(
            P(("dp", "col"), "row"),
            P(("dp", "col"), "row"),
            P(),
            P(("row", "dp"), "col"),
            P(("row", "dp"), "col"),
            P(("row", "dp"), "col"),
            P(),
            P(),
            P(("col", "dp"), "row"),
            P(),
            P(("row", "dp"), "col"),
            P(("row", "dp"), "col"),
            P(("col", "dp"), "row"),
        ),
        check_vma=False,
    )
```

```python
import math

import jax
import jax.numpy as jnp
from jax import lax
from jax.experimental import pallas as pl
from jax.experimental.pallas import tpu as pltpu
from jax.sharding import PartitionSpec as P

D = 2048
HEAD_SIZE = 128
EPSILON = 1e-06
ROPE_BASE = 1000000.0
NEGATIVE = -1e30
EXTRA = 8
VMEM_LIMIT = 40 << 20
BF16 = jnp.bfloat16
F32 = jnp.float32


def dot_nn(left, right):
    return jnp.dot(left, right, preferred_element_type=F32)


def dot_nt(left, right):
    return lax.dot_general(left, right, (((1,), (1,)), ((), ())), preferred_element_type=F32)


def dot_tn(left, right):
    return lax.dot_general(left, right, (((0,), (0,)), ((), ())), preferred_element_type=F32)


def swap_row(value):
    return lax.ppermute(value, "row", [(0, 1), (1, 0)])


def swap_col(value):
    return lax.ppermute(value, "col", [(0, 1), (1, 0)])


def swap_dp(value, bit):
    count = lax.axis_size("dp")
    return lax.ppermute(value, "dp", [(i, i ^ bit) for i in range(count)])


def swap_z(value):
    return swap_dp(value, 2)


def rotary_tables(position):
    half = HEAD_SIZE // 2
    frequency = ROPE_BASE ** (-2.0 * jnp.arange(half, dtype=F32) / HEAD_SIZE)
    angles = position.astype(F32)[:, None] * frequency[None, :]
    cosine, sine = jnp.cos(angles), jnp.sin(angles)
    return jnp.concatenate([cosine, cosine], axis=1), jnp.concatenate([-sine, sine], axis=1)


def pick(value, index, axis):
    return lax.dynamic_index_in_dim(value, index, axis, keepdims=False)


def high_bits(count):
    bits, bit = [], 4
    while bit < count:
        bits.append(bit)
        bit *= 2
    return bits


def split_rows(value, levels):
    return value.reshape((2,) * levels + (value.shape[0] >> levels,) + value.shape[1:])


def exchange(value):
    return lax.all_to_all(value, "dp", split_axis=0, concat_axis=0, tiled=True)


def after(value, *earlier):
    return lax.optimization_barrier((value,) + earlier)[0]


def together(*values):
    return lax.optimization_barrier(values)


class Line:
    def __init__(self, value):
        self.last = value

    def hold(self, *values):
        held = together(*values, self.last)[:-1]
        return held[0] if len(held) == 1 else held

    def passed(self, value):
        self.last = value
        return value


def by_half(index, own, other):
    first = index == 0
    return jnp.where(first, own, other), jnp.where(first, other, own)


WINDOWS = {
    "heads_kept": 6.0,
    "attend": 2.0,
    "out_own": 3.0,
    "act_kept": 3.0,
    "gate_and_up": 3.0,
    "mid_sent": 3.0,
    "mid_kept": 1.5,
    "up_rows": 2.5,
    "down_first": 3.0,
    "attention_kept": 3.5,
    "attend_back": 2.0,
    "normed_in": 6.5,
    "heads_second": 2.0,
}


def light(name):
    amount = WINDOWS.get(name, 0.05) * 0.1
    return pl.CostEstimate(
        flops=int(amount * 1.15e9), bytes_accessed=int(amount * 3.69e6), transcendentals=0
    )


def params(grid_axes=1):
    return pltpu.CompilerParams(vmem_limit_bytes=VMEM_LIMIT)


def scalars(*values):
    return jnp.stack([jnp.asarray(v, jnp.int32) for v in values])


def lanes_of(sums):
    return jnp.broadcast_to(sums, (sums.shape[0], HEAD_SIZE)).T[:8]


def column_of(lanes):
    return lanes.T[:, :1]


def local_call(kernel, inputs, outputs, name):
    return pl.pallas_call(
        kernel,
        out_shape=[jax.ShapeDtypeStruct(shape, dtype) for shape, dtype in outputs],
        compiler_params=params(),
        cost_estimate=light(name),
        name=name,
    )(*inputs)


def grid_call(kernel, grid, picks, inputs, in_specs, out_specs, outputs, name):
    return pl.pallas_call(
        kernel,
        grid_spec=pltpu.PrefetchScalarGridSpec(
            num_scalar_prefetch=1, grid=(grid,), in_specs=in_specs, out_specs=out_specs
        ),
        out_shape=[jax.ShapeDtypeStruct(shape, dtype) for shape, dtype in outputs],
        compiler_params=params(),
        cost_estimate=light(name),
        name=name,
    )(picks, *inputs)


def assemble(shape, pieces, name):
    def kernel(*refs):
        for (first, column, piece), ref in zip(pieces, refs):
            rows, columns = piece.shape
            refs[-1][first : first + rows, column : column + columns] = ref[...]

    values = [piece for _, _, piece in pieces]
    return local_call(kernel, values, [(shape, values[0].dtype)], name)[0]


def product(
    left, right, kind, dtype, tile, part=0, size=None, block=0, rows=None, name=None
):
    contract = {"nn": ((1,), (0,)), "nt": ((1,), (1,)), "tn": ((0,), (0,))}[kind]
    size = right.shape[0] if size is None else size
    rows = left.shape[0] if rows is None else rows
    if kind == "tn":
        shape, steps = (left.shape[1], right.shape[1]), left.shape[1] // tile
        specs = [
            pl.BlockSpec((rows, tile), lambda j, s: (block, j)),
            pl.BlockSpec((size, right.shape[1]), lambda j, s: (s[0], 0)),
        ]
        out = pl.BlockSpec((tile, shape[1]), lambda j, s: (j, 0))
    else:
        width = right.shape[1] if kind == "nn" else size
        shape, steps = (rows, width), width // tile
        if kind == "nn":
            right_spec = pl.BlockSpec((size, tile), lambda j, s: (s[0], j))
        else:
            right_spec = pl.BlockSpec(
                (tile, right.shape[1]), lambda j, s: (s[0] * (size // tile) + j, 0)
            )
        specs = [pl.BlockSpec((rows, left.shape[1]), lambda j, s: (block, 0)), right_spec]
        out = pl.BlockSpec((rows, tile), lambda j, s: (0, j))

    def kernel(picks, left_ref, right_ref, out_ref):
        out_ref[...] = lax.dot_general(
            left_ref[...], right_ref[...], (contract, ((), ())), preferred_element_type=F32
        ).astype(out_ref.dtype)

    return grid_call(
        kernel,
        steps,
        scalars(part),
        (left, right),
        specs,
        [out],
        [(shape, dtype)],
        name or "product_" + kind,
    )[0]


def product_onto(left, right, part, size, own, tile, name):
    rows, width = own.shape
    half = rows // 2

    def kernel(picks, left_ref, right_ref, own_ref, kept_ref, sent_ref):
        total = own_ref[...] + dot_nn(left_ref[...], right_ref[...])
        kept_ref[...] = total[:half]
        sent_ref[...] = total[half:].astype(BF16)

    return grid_call(
        kernel,
        width // tile,
        scalars(part),
        (left, right, own),
        [
            pl.BlockSpec(left.shape, lambda j, s: (0, 0)),
            pl.BlockSpec((size, tile), lambda j, s: (s[0], j)),
            pl.BlockSpec((rows, tile), lambda j, s: (0, j)),
        ],
        [pl.BlockSpec((half, tile), lambda j, s: (0, j))] * 2,
        [((half, width), F32), ((half, width), BF16)],
        name,
    )


def down_product(act_all, down_own, down_other, own_at, other_at, tile):
    rows, width = act_all.shape
    half, size, features = rows // 2, width // 2, down_own.shape[1]
    quarter = half // 2

    def kernel(picks, act_ref, own_ref, other_ref, kept_ref, near_ref, far_ref):
        total = dot_nn(act_ref[:, :size], own_ref[...]) + dot_nn(act_ref[:, size:], other_ref[...])
        kept_ref[...] = total[:half]
        near_ref[...] = total[half : half + quarter].astype(BF16)
        far_ref[...] = total[half + quarter :].astype(BF16)

    return grid_call(
        kernel,
        features // tile,
        scalars(own_at, other_at),
        (act_all, down_own, down_other),
        [
            pl.BlockSpec(act_all.shape, lambda j, s: (0, 0)),
            pl.BlockSpec((size, tile), lambda j, s: (s[0], j)),
            pl.BlockSpec((size, tile), lambda j, s: (s[1], j)),
        ],
        [pl.BlockSpec((half, tile), lambda j, s: (0, j))]
        + [pl.BlockSpec((quarter, tile), lambda j, s: (0, j))] * 2,
        [((half, features), F32), ((quarter, features), BF16), ((quarter, features), BF16)],
        "down_proj",
    )


def heads_forward(scaled, query_weight, key_weight, value_weight, part, dtype, name):
    group, features = scaled.shape
    query_part, tile = query_weight.shape[1] // 2, key_weight.shape[1] // 2
    steps = query_part // tile

    def kernel(picks, x_ref, query_ref, key_ref, value_ref, out_ref):
        step = pl.program_id(0)
        for condition, ref in (
            (step < steps, query_ref),
            (step == steps, key_ref),
            (step == steps + 1, value_ref),
        ):

            @pl.when(condition)
            def _():
                out_ref[...] = dot_nn(x_ref[...], ref[...]).astype(out_ref.dtype)

    return grid_call(
        kernel,
        steps + 2,
        scalars(part),
        (scaled, query_weight, key_weight, value_weight),
        [
            pl.BlockSpec((group, features), lambda j, s: (0, 0)),
            pl.BlockSpec(
                (features, tile), lambda j, s: (0, s[0] * steps + jnp.minimum(j, steps - 1))
            ),
            pl.BlockSpec((features, tile), lambda j, s: (0, s[0])),
            pl.BlockSpec((features, tile), lambda j, s: (0, s[0])),
        ],
        [pl.BlockSpec((group, tile), lambda j, s: (0, j))],
        [((group, query_part + 2 * tile), dtype)],
        name,
    )[0]


def heads_backward(grads, query_weight, key_weight, value_weight, part, own=None):
    group = grads.shape[0]
    half = group // 2
    features = query_weight.shape[0]
    query_part, key_part = query_weight.shape[1] // 2, key_weight.shape[1] // 2
    tile = features // 2

    def kernel(picks, grads_ref, query_ref, key_ref, value_ref, *refs):
        total = dot_nt(grads_ref[:, :query_part], query_ref[...])
        total += dot_nt(grads_ref[:, query_part : query_part + key_part], key_ref[...])
        total += dot_nt(grads_ref[:, query_part + key_part :], value_ref[...])
        if own is None:
            refs[0][...] = total
        else:
            total += refs[0][...]
            refs[1][...] = total[:half]
            refs[2][...] = total[half:].astype(BF16)

    whole = pl.BlockSpec((group, tile), lambda j, s: (0, j))
    split = pl.BlockSpec((half, tile), lambda j, s: (0, j))
    outputs = [((group, features), F32)]
    if own is not None:
        outputs = [((half, features), F32), ((half, features), BF16)]
    return grid_call(
        kernel,
        2,
        scalars(part),
        (grads, query_weight, key_weight, value_weight) + (() if own is None else (own,)),
        [
            pl.BlockSpec(grads.shape, lambda j, s: (0, 0)),
            pl.BlockSpec((tile, query_part), lambda j, s: (j, s[0])),
            pl.BlockSpec((tile, key_part), lambda j, s: (j, s[0])),
            pl.BlockSpec((tile, key_part), lambda j, s: (j, s[0])),
        ]
        + ([] if own is None else [whole]),
        [whole] if own is None else [split, split],
        outputs,
        "heads_backward",
    )


def up_kernel(picks, mid_ref, gate_ref, up_ref, *refs):
    parts = 4
    gate_parts, up_parts = refs[:parts], refs[parts : 2 * parts]
    kept_ref, *got_refs = refs[2 * parts : -3]
    gate_grad_ref, up_grad_ref, act_ref = refs[-3:]
    features = gate_ref.shape[0]
    share = gate_parts[0].shape[0]

    def columns(own_ref, part_refs):
        total = dot_nn(mid_ref[:, :features], own_ref[...])
        for i, ref in enumerate(part_refs):
            at = pl.multiple_of(features + picks[1 + i] * share, share)
            total += dot_nn(mid_ref[:, pl.ds(at, share)], ref[...])
        return total

    gate = columns(gate_ref, gate_parts)
    up = columns(up_ref, up_parts)
    got = jnp.concatenate([ref[...] for ref in got_refs], axis=0)
    act_grad = kept_ref[...] + got.astype(F32)
    sigmoid = jax.nn.sigmoid(gate)
    silu = gate * sigmoid
    act_ref[...] = (silu * up).astype(BF16)
    gate_grad_ref[...] = (act_grad * up * sigmoid * (1.0 + gate * (1.0 - sigmoid))).astype(BF16)
    up_grad_ref[...] = (act_grad * silu).astype(BF16)


def gate_and_up(mid, gate, up, base, pieces, places, kept, got):
    rows = mid.shape[0]
    features = gate.shape[0]
    width = kept.shape[1]
    tile = width // 3
    share = pieces[0][0].shape[0]

    def columns(height, first):
        return pl.BlockSpec((height, tile), lambda j, s: (0, first + j))

    own = pl.BlockSpec((features, tile), lambda j, s: (0, 3 * s[0] + j))
    return grid_call(
        up_kernel,
        3,
        scalars(base, *places),
        (mid, gate, up, *pieces[0], *pieces[1], kept, *got),
        [pl.BlockSpec(mid.shape, lambda j, s: (0, 0)), own, own]
        + [columns(share, 0)] * (2 * len(places))
        + [columns(rows, 0)]
        + [columns(g.shape[0], 0) for g in got],
        [columns(rows, 0)] * 3,
        [((rows, width), BF16)] * 3,
        "gate_and_up",
    )


def up_back_kernel(picks, gate_grad_ref, up_grad_ref, gate_ref, up_ref, *refs):
    *pieces, near_ref, far_ref = refs
    count = len(pieces) // 2
    features = gate_ref.shape[0]
    share = pieces[0].shape[0]
    gate_grad, up_grad = gate_grad_ref[...], up_grad_ref[...]
    for i in range(features // (2 * share)):
        at = slice(i * 2 * share, (i + 1) * 2 * share)
        total = dot_nt(gate_grad, gate_ref[at, :]) + dot_nt(up_grad, up_ref[at, :])
        near_ref[:, at] = total.astype(near_ref.dtype)
    for i in range(count):
        total = dot_nt(gate_grad, pieces[i][...]) + dot_nt(up_grad, pieces[count + i][...])
        at = pl.multiple_of(picks[1 + i] * share, share)
        far_ref[:, pl.ds(at, share)] = total.astype(far_ref.dtype)


def gate_and_up_back(gate_grad, up_grad, block, gate, up, base, pieces, places, dtype, name):
    rows = gate_grad.shape[0] // 2
    width = gate_grad.shape[1]
    features = gate.shape[0]
    grads = pl.BlockSpec((rows, width), lambda j, s: (block, 0))
    own = pl.BlockSpec((features, width), lambda j, s: (0, s[0]))
    pieces = (*pieces[0], *pieces[1])
    piece = pl.BlockSpec(pieces[0].shape, lambda j, s: (0, 0))
    shape = (rows, features)
    return grid_call(
        up_back_kernel,
        1,
        scalars(base, *places),
        (gate_grad, up_grad, gate, up, *pieces),
        [grads, grads, own, own] + [piece] * len(pieces),
        [pl.BlockSpec(shape, lambda j, s: (0, 0))] * 2,
        [(shape, dtype)] * 2,
        name,
    )


def in_place(weight):
    return pltpu.with_memory_space_constraint(weight, pltpu.MemorySpace.HBM)


def my_bit(bit):
    return (lax.axis_index("dp") // bit) % 2


def view(shape, columns=None, **at):
    at = {int(axis[1:]): place for axis, place in at.items()}
    parts, part = columns or (1, 0)
    last = len(shape) - 1
    block = tuple(
        None if axis in at else length // (parts if axis == last else 1)
        for axis, length in enumerate(shape)
    )
    return pl.BlockSpec(
        block,
        lambda j, s: tuple(
            s[at[axis]] if axis in at else (part if axis == last else 0)
            for axis in range(len(shape))
        ),
    )


def without(shape, *axes):
    return tuple(length for axis, length in enumerate(shape) if axis not in axes)


def take(value, axis, index, columns=None):
    shape = without(value.shape, axis)
    shape = shape[:-1] + (shape[-1] // (columns or (1, 0))[0],)

    def kernel(picks, in_ref, out_ref):
        out_ref[...] = in_ref[...].astype(BF16)

    return grid_call(
        kernel,
        1,
        scalars(index),
        (value,),
        [view(value.shape, columns, **{f"a{axis}": 0})],
        [view(shape)],
        [(shape, BF16)],
        "take",
    )[0]


def start_stage(value, axis, bit):
    return swap_dp(take(value, axis, 1 - my_bit(bit)), bit)


def end_stage(value, got, axis, bit, next_axis=None, next_index=None, columns=None):
    joined = got.shape
    side = {} if axis is None else {f"a{axis}": 0}
    mine = 0 if axis is None else my_bit(bit)
    if next_axis is None:

        def kernel(picks, value_ref, got_ref, out_ref):
            out_ref[...] = value_ref[...].astype(F32) + got_ref[...].astype(F32)

        return grid_call(
            kernel,
            1,
            scalars(mine),
            (value, got),
            [view(value.shape, **side), view(joined)],
            [view(joined)],
            [(joined, F32)],
            "join",
        )[0]
    shape = without(joined, next_axis)
    behind = next_axis + (1 if axis is not None and next_axis >= axis else 0)

    def kernel(picks, keep_ref, keep_got, send_ref, send_got, kept_ref, sent_ref):
        kept_ref[...] = keep_ref[...].astype(F32) + keep_got[...].astype(F32)
        sent_ref[...] = (send_ref[...].astype(F32) + send_got[...].astype(F32)).astype(BF16)

    return grid_call(
        kernel,
        1,
        scalars(mine, next_index, 1 - next_index),
        (value, got, value, got),
        [
            view(value.shape, columns, **side, **{f"a{behind}": 1}),
            view(joined, **{f"a{next_axis}": 1}),
            view(value.shape, columns, **side, **{f"a{behind}": 2}),
            view(joined, **{f"a{next_axis}": 2}),
        ],
        [view(shape)] * 2,
        [(shape, F32), (shape, BF16)],
        "join_and_split",
    )


def add_got(kept, got):
    def kernel(kept_ref, got_ref, out_ref):
        out_ref[...] = kept_ref[...].astype(F32) + got_ref[...].astype(F32)

    return local_call(kernel, (kept, got), [(kept.shape, F32)], "add_got")[0]


def split_top(own, other, row):
    mine = my_bit(lax.axis_size("dp") // 2) == row

    def kernel(picks, own_ref, other_ref, kept_ref, sent_ref):
        for first, second, flag in ((own_ref, other_ref, 1), (other_ref, own_ref, 0)):

            @pl.when(picks[0] == flag)
            def _():
                kept_ref[...] = first[...].astype(F32)
                sent_ref[...] = second[...].astype(BF16)

    spec = view(own.shape)
    return grid_call(
        kernel,
        1,
        scalars(mine),
        (own, other),
        [spec, spec],
        [spec, spec],
        [(own.shape, F32), (own.shape, BF16)],
        "split_top",
    )


def join_core_kernel(
    near_ref, far_ref, got_near, got_far, own_ref, row_ref, z_ref, row_both_ref, z_both_ref
):
    half = own_ref.shape[0]
    quarter = half // 2
    near = near_ref[...] + got_near[...].astype(F32)
    far = far_ref[...] + got_far[...].astype(F32)
    own_ref[...] = near[:half]
    row_ref[...] = far[:half]
    z_ref[...] = near[half:]
    row_both_ref[...] = far[half : half + quarter].astype(BF16)
    z_both_ref[...] = far[half + quarter :].astype(BF16)


def join_corner_kernel(row_ref, z_ref, via_row_ref, via_z_ref, to_row_ref, to_z_ref):
    quarter = via_row_ref.shape[0]
    to_row_ref[:quarter, :] = row_ref[:quarter, :].astype(BF16)
    to_row_ref[quarter:, :] = (row_ref[quarter:, :] + via_z_ref[...].astype(F32)).astype(BF16)
    to_z_ref[:quarter, :] = (z_ref[:quarter, :] + via_row_ref[...].astype(F32)).astype(BF16)
    to_z_ref[quarter:, :] = z_ref[quarter:, :].astype(BF16)


def norm_sums_kernel(*refs):
    parts = refs[:-6]
    base_ref, inverse_ref, gain_ref, grad_ref, sums_ref, gain_grad_ref = refs[-6:]
    grad = sum(part[...].astype(F32) for part in parts)
    unit = base_ref[...].astype(F32) * column_of(inverse_ref[...])
    along = grad * unit
    grad_ref[...] = grad
    sums_ref[...] = lanes_of(jnp.sum(along * gain_ref[...], axis=1, keepdims=True))
    gain_grad_ref[...] = jnp.sum(along, axis=0, keepdims=True)


def norm_sums(parts, base, inverse, gain):
    rows, features = base.shape
    return local_call(
        norm_sums_kernel,
        (*parts, base, inverse, gain),
        [((rows, features), F32), ((8, rows), F32), ((1, features), F32)],
        "norm_sums",
    )


def norm_grad_kernel(
    grad_ref, base_ref, inverse_ref, gain_ref, sums_ref, got_sums_ref, rest_ref, *out_refs
):
    inverse = column_of(inverse_ref[...])
    unit = base_ref[...].astype(F32) * inverse
    mean = column_of(sums_ref[...] + got_sums_ref[...]) * (1.0 / D)
    out = rest_ref[...].astype(F32) + inverse * (grad_ref[...] * gain_ref[...] - unit * mean)
    for out_ref in out_refs:
        out_ref[...] = out.astype(out_ref.dtype)


def norm_grad(grad, base, inverse, gain, sums, got_sums, rest, dtypes):
    return local_call(
        norm_grad_kernel,
        (grad, base, inverse, gain, sums, got_sums, rest),
        [(grad.shape, dtype) for dtype in dtypes],
        "norm_grad",
    )


def middle_kernel(x_ref, part_ref, got_ref, mid_ref, square_ref):
    mid = x_ref[...].astype(F32) + part_ref[...] + got_ref[...].astype(F32)
    mid_ref[...] = mid
    square_ref[...] = lanes_of(jnp.sum(mid * mid, axis=1, keepdims=True))


def normed_kernel(mid_ref, square_ref, got_ref, gain_ref, normed_ref, inverse_ref):
    inverse = lax.rsqrt((square_ref[...] + got_ref[...]) * (1.0 / D) + EPSILON)
    inverse_ref[...] = inverse
    unit = mid_ref[...].astype(F32) * column_of(inverse)
    normed_ref[...] = (unit * gain_ref[...]).astype(BF16)


def scaled_kernel(own_ref, got_ref, gain_ref, x_ref, scaled_ref, square_ref):
    half = own_ref.shape[0]
    for first, ref in ((0, own_ref), (half, got_ref)):
        at = slice(first, first + half)
        values = ref[...].astype(F32)
        x_ref[at, :] = ref[...]
        scaled_ref[at, :] = (values * gain_ref[...]).astype(BF16)
        square_ref[:, at] = lanes_of(jnp.sum(values * values, axis=1, keepdims=True))


def normed_in_kernel(x_ref, inverse_ref, gain_ref, normed_ref):
    unit = x_ref[...].astype(F32) * column_of(inverse_ref[...])
    normed_ref[...] = (unit * gain_ref[...]).astype(BF16)


def block_of(weight, block_row, block_column, shape):
    def kernel(picks, in_ref, out_ref):
        out_ref[...] = in_ref[...]

    return grid_call(
        kernel,
        1,
        scalars(block_row, block_column),
        (weight,),
        [pl.BlockSpec(shape, lambda j, s: (s[0], s[1]))],
        [pl.BlockSpec(shape, lambda j, s: (0, 0))],
        [(shape, BF16)],
        "block_of",
    )[0]


def side_kernel(*refs):
    kept_ref, sent_ref = refs[-2:]
    parts = (len(refs) - 2) // 2
    width = refs[0].shape[-1]
    for i in range(parts):
        total = refs[i][...].astype(F32) + refs[parts + i][...].astype(F32)
        at = slice(i * width, (i + 1) * width)
        kept_ref[:, :, at] = total[0]
        sent_ref[:, :, at] = total[1].astype(BF16)


def pack_back(grad, attention_part, feedforward_part, head_gains, count):
    rows, features = grad.shape
    share = rows // count

    def kernel(grad_ref, attention_ref, feedforward_ref, heads_ref, out_ref):
        rest = jnp.zeros((1, features - 2 * HEAD_SIZE), F32)
        heads = jnp.concatenate([heads_ref[:1, :], heads_ref[1:, :], rest], axis=1)
        values = jnp.concatenate([attention_ref[...], feedforward_ref[...], heads, heads], axis=0)
        high = values.astype(BF16)
        low = (values - high.astype(F32)).astype(BF16)
        extra = jnp.concatenate([high.astype(F32), low.astype(F32)], axis=0).astype(BF16)
        for i in range(count):
            out_ref[i, :share, :] = grad_ref[i * share : (i + 1) * share, :]
            out_ref[i, share:, :] = extra

    return local_call(
        kernel,
        (grad, attention_part, feedforward_part, head_gains),
        [((count, share + EXTRA, features), BF16)],
        "pack_back",
    )[0]


def layer_out_kernel(mid_ref, kept_ref, got_ref, out_ref):
    out_ref[...] = (mid_ref[...] + kept_ref[...] + got_ref[...].astype(F32)).astype(BF16)


def out_near_kernel(kept_ref, got_near, got_far, near_ref, far_ref):
    half = near_ref.shape[0]
    near_ref[...] = kept_ref[:half, :] + got_near[...].astype(F32)
    far_ref[...] = (kept_ref[half:, :] + got_far[...].astype(F32)).astype(BF16)


def turn(values, cosine, sine):
    return values * cosine + pltpu.roll(values, HEAD_SIZE // 2, 1) * sine


def unit_of(raw):
    inverse = lax.rsqrt(jnp.mean(raw * raw, axis=-1, keepdims=True) + EPSILON)
    return raw * inverse, inverse


def scores_to_prob(query_rot, key_rot, allowed):
    scores = dot_nt(query_rot, key_rot) * (1.0 / math.sqrt(HEAD_SIZE))
    scores = jnp.where(allowed, scores, NEGATIVE)
    exps = jnp.exp(scores - jnp.max(scores, axis=-1, keepdims=True))
    return exps * (1.0 / jnp.sum(exps, axis=-1, keepdims=True))


def head_inputs(own, got, inverse_in, width):
    raw = (own[...] + got[...].astype(F32)) * inverse_in
    return [raw[:, i * HEAD_SIZE : (i + 1) * HEAD_SIZE] for i in range(width // HEAD_SIZE)]


def attend_kernel(
    query_own, query_got, key_own, key_got, value_own, value_got, inverse_ref, cosine_ref,
    sine_ref, slot_ref, start_ref, across_ref, query_gain_ref, key_gain_ref, out_ref,
):
    inverse_in = column_of(inverse_ref[...])
    cosine, sine = cosine_ref[...], sine_ref[...]
    across = across_ref[...]
    (key_raw,) = head_inputs(key_own, key_got, inverse_in, HEAD_SIZE)
    (value,) = head_inputs(value_own, value_got, inverse_in, HEAD_SIZE)
    key_rot = turn(unit_of(key_raw)[0] * key_gain_ref[...], cosine, sine).astype(BF16)
    value = value.astype(BF16)
    slots, first = column_of(slot_ref[...]), column_of(start_ref[...])
    rows = out_ref.shape[0] // 2

    for block in range(2):
        at = slice(block * rows, (block + 1) * rows)
        allowed = (across <= slots[at]) & (across >= first[at])
        for i in range(query_own.shape[1] // HEAD_SIZE):
            head = slice(i * HEAD_SIZE, (i + 1) * HEAD_SIZE)
            raw = (query_own[at, head] + query_got[at, head].astype(F32)) * inverse_in[at]
            pre = unit_of(raw)[0] * query_gain_ref[...]
            query_rot = turn(pre, cosine_ref[at, :], sine_ref[at, :]).astype(BF16)
            prob = scores_to_prob(query_rot, key_rot, allowed).astype(BF16)
            out_ref[at, head] = dot_nn(prob, value).astype(BF16)


def attend_back_kernel(
    query_own, query_got, key_own, key_got, value_own, value_got, inverse_ref, cosine_ref,
    sine_ref, slot_ref, start_ref, across_ref, query_gain_ref, key_gain_ref, grad_own, grad_got,
    out_ref, gain_ref,
):
    step = pl.program_id(0)
    repeat = query_own.shape[1] // HEAD_SIZE
    kv_heads = out_ref.shape[1] // (query_own.shape[1] + 2 * HEAD_SIZE)
    scale = 1.0 / math.sqrt(HEAD_SIZE)
    inverse_in = column_of(inverse_ref[...])
    cosine, sine = cosine_ref[...], sine_ref[...]
    across = across_ref[...]
    allowed = (across <= column_of(slot_ref[...])) & (across >= column_of(start_ref[...]))
    query_gain, key_gain = query_gain_ref[...], key_gain_ref[...]

    @pl.when(step == 0)
    def _():
        gain_ref[...] = jnp.zeros_like(gain_ref)

    (key_raw,) = head_inputs(key_own, key_got, inverse_in, HEAD_SIZE)
    (value,) = head_inputs(value_own, value_got, inverse_in, HEAD_SIZE)
    key_unit, key_inverse = unit_of(key_raw)
    key_rot = turn(key_unit * key_gain, cosine, sine).astype(BF16)
    value = value.astype(BF16)

    def norm_back(rot_grad, unit, inverse, gain, at):
        pre = rot_grad * cosine - pltpu.roll(rot_grad, HEAD_SIZE // 2, 1) * sine
        gain_ref[at : at + 1, :] += jnp.sum(pre * unit, axis=0, keepdims=True)
        scaled = pre * gain
        return inverse * (scaled - unit * jnp.mean(scaled * unit, axis=-1, keepdims=True))

    key_grad = jnp.zeros(key_raw.shape, F32)
    value_grad = jnp.zeros(key_raw.shape, F32)
    for i, query_raw in enumerate(
        head_inputs(query_own, query_got, inverse_in, query_own.shape[1])
    ):
        at = slice(i * HEAD_SIZE, (i + 1) * HEAD_SIZE)
        query_unit, query_inverse = unit_of(query_raw)
        query_rot = turn(query_unit * query_gain, cosine, sine).astype(BF16)
        prob = scores_to_prob(query_rot, key_rot, allowed)
        grad_out = (grad_own[:, at] + grad_got[:, at].astype(F32)).astype(BF16)
        prob_grad = dot_nt(grad_out, value)
        centre = jnp.sum(prob * prob_grad, axis=-1, keepdims=True)
        score_grad = (prob * (prob_grad - centre)).astype(BF16)
        value_grad += dot_tn(prob.astype(BF16), grad_out)
        key_grad += dot_tn(score_grad, query_rot)
        query_grad = norm_back(
            dot_nn(score_grad, key_rot) * scale, query_unit, query_inverse, query_gain, 0
        )
        column = pl.multiple_of((step * repeat + i) * HEAD_SIZE, HEAD_SIZE)
        out_ref[:, pl.ds(column, HEAD_SIZE)] = query_grad.astype(BF16)
    key_grad = norm_back(key_grad * scale, key_unit, key_inverse, key_gain, 1)
    column = pl.multiple_of((kv_heads * repeat + step) * HEAD_SIZE, HEAD_SIZE)
    out_ref[:, pl.ds(column, HEAD_SIZE)] = key_grad.astype(BF16)
    column = pl.multiple_of((kv_heads * (repeat + 1) + step) * HEAD_SIZE, HEAD_SIZE)
    out_ref[:, pl.ds(column, HEAD_SIZE)] = value_grad.astype(BF16)


def attention_specs(group, kv_heads, repeat):
    def block(width, first):
        return pl.BlockSpec((group, width), lambda j: (0, first + j))

    def whole(rows, columns):
        return pl.BlockSpec((rows, columns), lambda j: (0, 0))

    query = block(repeat * HEAD_SIZE, 0)
    key = block(HEAD_SIZE, kv_heads * repeat)
    value = block(HEAD_SIZE, kv_heads * (repeat + 1))
    return [query, query, key, key, value, value] + [
        whole(8, group),
        whole(group, HEAD_SIZE),
        whole(group, HEAD_SIZE),
        whole(8, group),
        whole(8, group),
        whole(1, group),
        whole(1, HEAD_SIZE),
        whole(1, HEAD_SIZE),
    ]


def attend(own, got, shared, kv_heads, repeat):
    group = own.shape[0]
    width = kv_heads * repeat * HEAD_SIZE
    return pl.pallas_call(
        attend_kernel,
        grid=(kv_heads,),
        in_specs=attention_specs(group, kv_heads, repeat),
        out_specs=pl.BlockSpec((group, repeat * HEAD_SIZE), lambda j: (0, j)),
        out_shape=jax.ShapeDtypeStruct((group, width), BF16),
        compiler_params=pltpu.CompilerParams(vmem_limit_bytes=VMEM_LIMIT),
        cost_estimate=light("attend"),
        name="attend",
    )(own, got, own, got, own, got, *shared)


def attend_back(own, got, shared, grad_own, grad_got, kv_heads, repeat):
    group, width = own.shape
    grad_block = pl.BlockSpec((group, repeat * HEAD_SIZE), lambda j: (0, j))
    return pl.pallas_call(
        attend_back_kernel,
        grid=(kv_heads,),
        in_specs=attention_specs(group, kv_heads, repeat) + [grad_block, grad_block],
        out_specs=[
            pl.BlockSpec((group, width), lambda j: (0, 0)),
            pl.BlockSpec((2, HEAD_SIZE), lambda j: (0, 0)),
        ],
        out_shape=[
            jax.ShapeDtypeStruct((group, width), BF16),
            jax.ShapeDtypeStruct((2, HEAD_SIZE), F32),
        ],
        compiler_params=pltpu.CompilerParams(vmem_limit_bytes=VMEM_LIMIT),
        cost_estimate=light("attend_back"),
        name="attend_back",
    )(own, got, own, got, own, got, *shared, grad_own, grad_got)

def shards(
    tokens,
    cotangent,
    seq_lengths,
    balance_order,
    attention_gain,
    query_weight,
    key_weight,
    value_projection,
    query_gain,
    key_norm_gain,
    output_weight,
    feedforward_gain,
    gate_weight,
    up_weight,
    down_weight,
):
    count = lax.axis_size("dp")
    levels = count.bit_length() - 1
    row = lax.axis_index("row")
    col = lax.axis_index("col")
    xbit, zbit, wbit = my_bit(1), my_bit(2), my_bit(4)
    half = tokens.shape[0]
    quarter = half // 2
    group = 2 * half
    pair = 2 * group
    features = tokens.shape[1]
    query_part = query_weight.shape[1] // 2
    key_part = key_weight.shape[1] // 2
    heads = query_part // HEAD_SIZE
    kv_heads = key_part // HEAD_SIZE
    repeat = heads // kv_heads
    ff_half = gate_weight.shape[1]
    runs = count // 8
    projections = tuple(map(in_place, (query_weight, key_weight, value_projection)))
    output_weight = in_place(output_weight)
    if runs == 1:
        gate_weight, up_weight, down_weight = map(in_place, (gate_weight, up_weight, down_weight))
    run = 2 * ff_half // count
    ff_part = ff_half // 4
    all_bits = high_bits(count)[::-1]

    def ff_block(weight, part, axis):
        if runs == 1:
            return weight, part * 2 + zbit
        pieces = [
            lax.dynamic_slice_in_dim(weight, ((part * runs + i) * 2 + zbit) * run, run, axis)
            for i in range(runs)
        ]
        return jnp.concatenate(pieces, axis=axis), 0

    moved_in = exchange(tokens)
    share = features // 4
    gate_far, far_base = ff_block(gate_weight, 1 - row, 1)
    up_far, _ = ff_block(up_weight, 1 - row, 1)
    gate_sent, up_sent = (
        block_of(weight, wbit * 2 + xbit, far_base, (share, ff_part))
        for weight in (gate_far, up_far)
    )
    got_gate, got_up = swap_row(gate_sent), swap_row(up_sent)

    base_ids = jnp.arange(half, dtype=jnp.int32)
    local_ids = jnp.concatenate([col * half + base_ids, (1 - col) * half + base_ids])
    slot_ids = jnp.arange(group, dtype=jnp.int32)
    slot = jnp.sum(
        jnp.where(balance_order[0][None, :] == local_ids[:, None], slot_ids[None, :], 0), axis=1
    )
    lengths = seq_lengths[0]
    seq_ends = jnp.cumsum(lengths)
    starts = seq_ends - lengths
    segment = jnp.sum((slot[:, None] >= seq_ends[None, :]).astype(jnp.int32), axis=1)
    hits = segment[:, None] == jnp.arange(lengths.shape[0], dtype=jnp.int32)[None, :]
    start = jnp.sum(jnp.where(hits, starts[None, :], 0), axis=1)
    cosine, sine = rotary_tables(slot - start)
    slot_lanes = jnp.broadcast_to(slot.astype(F32)[None], (8, group))
    start_lanes = jnp.broadcast_to(start.astype(F32)[None], (8, group))
    moved_in, cosine, sine, slot_lanes, start_lanes, got_gate, got_up = together(
        moved_in, cosine, sine, slot_lanes, start_lanes, got_gate, got_up
    )

    gain_in = attention_gain.astype(F32)[None]
    gain_mid = feedforward_gain.astype(F32)[None]
    x_low, scaled_in, square = local_call(
        scaled_kernel,
        (moved_in, swap_col(moved_in), gain_in),
        [((group, features), BF16), ((group, features), BF16), ((8, group), F32)],
        "scaled",
    )
    moved_grad = exchange(after(cotangent, moved_in))
    heads_sent = heads_forward(after(scaled_in, got_gate, got_up), *projections, 1 - row, BF16, "heads_sent")
    got_square = swap_row(square)
    got_heads = swap_row(heads_sent)
    kept_heads = heads_forward(
        after(scaled_in, heads_sent), *projections, row, F32, "heads_kept"
    )
    got_gate, got_up = together(got_gate, got_up, heads_sent)[:2]
    got_gate_x, got_up_x = swap_dp(got_gate, 1), swap_dp(got_up, 1)
    got_gate_w, got_up_w = swap_dp(got_gate, 4), swap_dp(got_up, 4)

    down_own, own_at = ff_block(down_weight, row, 0)
    down_other, other_at = ff_block(down_weight, 1 - row, 0)

    def act_back(rows_of, weight, at, dtype, name="act_sent"):
        return product(rows_of, weight, "nt", dtype, ff_part // 3, at, ff_part, name=name)

    moved_grad = after(moved_grad, kept_heads)
    grad_z = swap_z(moved_grad)
    grad_near = swap_col(moved_grad)
    act_sent = [
        act_back(rows_of, down_other, other_at, BF16) for rows_of in (moved_grad, grad_near)
    ]
    got_heads, kept_heads, got_square, got_gate_x, got_gate_w, grad_z, *act_sent = together(
        got_heads, kept_heads, got_square, got_gate_x, got_gate_w, grad_z, *act_sent
    )
    inverse_in = lax.rsqrt((square + got_square) / D + EPSILON)
    shared = (
        inverse_in,
        cosine,
        sine,
        slot_lanes,
        start_lanes,
        slot_lanes[:1],
        query_gain.astype(F32)[None],
        key_norm_gain.astype(F32)[None],
    )
    got_act = [swap_row(act_sent[0])]
    got_gate_wx = swap_dp(got_gate_w, 1)
    grad_far = swap_col(grad_z)
    attention = attend(kept_heads, got_heads, shared, kv_heads, repeat)
    attention, got_act[0], grad_far = together(attention, got_act[0], grad_far)
    attention_other = swap_row(attention)
    got_act.append(swap_row(after(act_sent[1], attention)))
    out_own = product(
        attention, output_weight, "nn", F32, features // 2, row, query_part, name="out_own"
    )
    far_sent = [
        act_back(after(rows_of, out_own), down_other, other_at, BF16)
        for rows_of in (grad_z, grad_far)
    ]
    attention_other, got_act[1], got_gate_wx, got_up_x, got_up_w, out_own, *far_sent = together(
        attention_other, got_act[1], got_gate_wx, got_up_x, got_up_w, out_own, *far_sent
    )
    got_up_wx = swap_dp(got_up_w, 1)
    out_kept, out_sent = product_onto(
        attention_other, output_weight, 1 - row, query_part, out_own, features // 2, "out_proj"
    )
    out_got = swap_col(out_sent)
    stream_mid, square_mid = local_call(
        middle_kernel,
        (moved_in, out_kept, out_got),
        [((half, features), F32), ((8, half), F32)],
        "middle",
    )
    got_square = swap_row(square_mid)
    grad_all = assemble(
        (pair, features),
        [
            (0, 0, moved_grad),
            (half, 0, grad_z),
            (group, 0, grad_near),
            (group + half, 0, after(grad_far, square_mid)),
        ],
        "grad_all",
    )
    normed_mid, inverse_mid = local_call(
        normed_kernel,
        (stream_mid, square_mid, got_square, gain_mid),
        [((half, features), BF16), ((8, half), F32)],
        "normed",
    )

    by_row = swap_row(normed_mid)
    by_z = swap_z(normed_mid)
    act_kept = act_back(after(grad_all, normed_mid), down_own, own_at, F32, "act_kept")
    by_row, by_z, act_kept, got_up_wx = together(by_row, by_z, act_kept, got_up_wx)
    corner_a = swap_row(by_z[:quarter])
    corner_b = swap_z(by_row[quarter:])
    got_act.extend(swap_row(after(sent, by_row)) for sent in far_sent)
    near = [
        (0, 0, normed_mid),
        (0, features, by_row),
        (half, 0, by_z),
        (half, features, corner_a),
        (half + quarter, features, corner_b),
    ]
    crossed = [(group + first, at, swap_col(piece)) for first, at, piece in near]
    mid_all = assemble((pair, 2 * features), near + crossed, "mid_all")

    gate_own, own_base = ff_block(gate_weight, row, 1)
    up_own, _ = ff_block(up_weight, row, 1)
    places = (
        wbit * 2 + xbit,
        wbit * 2 + 1 - xbit,
        (1 - wbit) * 2 + xbit,
        (1 - wbit) * 2 + 1 - xbit,
    )
    pieces = (
        (got_gate, got_gate_x, got_gate_w, got_gate_wx),
        (got_up, got_up_x, got_up_w, got_up_wx),
    )
    up_weights = (gate_own, up_own, own_base, pieces, places)
    gate_grad, up_grad, activated = gate_and_up(
        mid_all, *up_weights, act_kept, (got_act[0], got_act[2], got_act[1], got_act[3])
    )

    act_got = swap_row(activated)
    line = Line(activated)
    top_bit, lower_bits = all_bits[0], all_bits[1:]
    top_place = jnp.where(my_bit(top_bit) == row, 0, 1)

    def up_rows(grad_part, name):
        whole = product(mid_all, grad_part, "tn", BF16, features // 2, name=name)
        return whole.reshape((2,) * (levels + 1) + (features // count, ff_part))

    def first_stage(value, axis, bit):
        sent = line.passed(take(value, axis, 1 - my_bit(bit)))
        return swap_dp(sent, bit)

    def late_stage(value, got, axis, bit, next_axis, next_bit, place=None):
        place = my_bit(next_bit) if place is None else place
        kept, sent = end_stage(value, line.hold(got), axis, bit, next_axis, place)
        return kept, swap_dp(line.passed(sent), next_bit)

    mid_sent = gate_and_up_back(gate_grad, up_grad, 1, *up_weights, BF16, "mid_sent")
    line.passed(mid_sent[0])
    got_mid = [swap_col(sent) for sent in mid_sent]
    gate_rows = up_rows(line.hold(gate_grad), "gate_rows")
    gate_got = first_stage(gate_rows, levels, 1)
    mid_kept = gate_and_up_back(line.hold(gate_grad), up_grad, 0, *up_weights, F32, "mid_kept")
    *got_mid, kept_near, act_got = together(*got_mid, mid_kept[0], act_got)
    block = (half, features)
    mid_own, to_row, to_z, row_both, z_both = local_call(
        join_core_kernel,
        (kept_near, mid_kept[1], *got_mid),
        [(block, F32)] * 3 + [((quarter, features), BF16)] * 2,
        "join_core",
    )
    via_row = swap_row(row_both)
    via_z = swap_z(z_both)
    line.passed(row_both)
    up_cols = up_rows(line.hold(up_grad), "up_rows")
    up_sent = line.passed(take(up_cols, levels, 1 - xbit))
    via_row, via_z, up_sent = line.hold(via_row, via_z, up_sent)
    to_row, to_z = local_call(
        join_corner_kernel,
        (to_row, to_z, via_row, via_z),
        [(block, BF16), (block, BF16)],
        "join_corner",
    )
    got_row, got_z = swap_row(to_row), swap_z(to_z)
    up_got = swap_dp(up_sent, 1)
    line.passed(to_row)
    act_all = assemble(
        (pair, 2 * ff_part), [(0, 0, activated), (0, ff_part, line.hold(act_got))], "act_all"
    )
    down_rows = product(act_all, grad_all, "tn", BF16, ff_part // 2, name="down_first")
    down_rows = split_rows(down_rows, levels - 1)
    down_sent = line.passed(take(down_rows, levels - 2, 1 - xbit))
    got_row, got_z, down_sent = line.hold(got_row, got_z, down_sent)
    normed_mid_grad, mid_sum, feedforward_part = norm_sums(
        (mid_own, got_row, got_z), stream_mid, inverse_mid, gain_mid
    )
    got_sum = swap_row(line.passed(mid_sum))
    down_got = swap_dp(down_sent, 1)
    got_sum, gate_got = line.hold(got_sum, gate_got)
    stream_mid_grad, branch_low = norm_grad(
        normed_mid_grad, stream_mid, inverse_mid, gain_mid, mid_sum, got_sum, moved_grad, (F32, BF16)
    )
    line.passed(branch_low)
    branch_got = swap_col(branch_low)
    gate_rows, gate_got = late_stage(gate_rows, gate_got, levels, 1, 1, top_bit)
    branch = assemble(
        (group, features), [(0, 0, branch_low), (half, 0, line.hold(branch_got))], "branch"
    )
    attention_sent = product(branch, output_weight, "nt", BF16, query_part, 1 - row, query_part)
    got_attention = swap_row(attention_sent)
    line.passed(attention_sent)

    attention_kept = line.passed(
        product(
            line.hold(branch),
            output_weight,
            "nt",
            F32,
            query_part,
            row,
            query_part,
            name="attention_kept",
        )
    )
    attention_all = assemble(
        (group, 2 * query_part),
        [(0, 0, line.hold(attention)), (0, query_part, attention_other)],
        "attention_all",
    )
    output_rows = product(attention_all, branch, "tn", BF16, query_part, name="output_rows")
    output_rows = split_rows(output_rows, levels)
    output_sent = line.passed(take(output_rows, levels - 2, 1 - zbit))
    output_got = swap_dp(output_sent, 2)
    out_kept, *out_sent = down_product(
        line.hold(act_all), down_own, down_other, own_at, other_at, features // 2
    )
    line.passed(out_kept)
    out_got = [swap_col(sent) for sent in out_sent]
    got_attention, out_kept = line.hold(got_attention, out_kept)
    line.passed(got_attention)
    projected_grad, head_gains = attend_back(
        kept_heads, got_heads, shared, attention_kept, line.hold(got_attention), kv_heads, repeat
    )
    projected_grad, up_got, gate_got, output_got, *out_got = together(
        projected_grad, up_got, gate_got, output_got, *out_got
    )
    projected_other = swap_row(projected_grad)
    line.passed(projected_grad)
    up_cols, up_got = late_stage(up_cols, up_got, levels, 1, 1, top_bit)

    (normed_in,) = local_call(
        normed_in_kernel,
        (x_low, line.hold(inverse_in), gain_in),
        [((group, features), BF16)],
        "normed_in",
    )

    def projection_rows(part, name):
        whole = product(normed_in, part, "tn", BF16, features // 2, name=name)
        whole = split_rows(whole, levels)
        return whole, line.passed(take(whole, levels - 2, 1 - zbit))

    heads_first, heads_sent_own = projection_rows(line.hold(projected_grad), "heads_first")
    in_own = line.passed(heads_backward(line.hold(projected_grad), *projections, row)[0])
    heads_got = swap_dp(heads_sent_own, 2)
    out_near, out_far = local_call(
        out_near_kernel, (out_kept, *line.hold(*out_got)), [(block, F32), (block, BF16)], "out_near"
    )
    layer_z = swap_z(line.passed(out_far))
    projected_other, in_own, down_got = line.hold(projected_other, in_own, down_got)
    line.passed(projected_other)
    in_kept, in_sent = heads_backward(projected_other, *projections, 1 - row, in_own)
    in_got = swap_col(line.passed(in_sent))
    down_rows, down_got = late_stage(down_rows, down_got, levels - 2, 1, 0, top_bit, top_place)
    in_values = (moved_in, inverse_in[:, :half], gain_in)
    normed_in_grad, in_sum, attention_part = norm_sums(
        (in_kept, line.hold(in_got)), *in_values
    )
    got_sum = swap_row(line.passed(in_sum))
    output_rows, output_got = late_stage(
        output_rows, output_got, levels - 2, 2, levels - 2, 1
    )
    heads_second, heads_sent_other = projection_rows(line.hold(projected_other), "heads_second")
    got_sum, up_got, heads_got, heads_sent_other = line.hold(
        got_sum, up_got, heads_got, heads_sent_other
    )
    heads_got_other = swap_dp(heads_sent_other, 2)
    (stream_grad,) = norm_grad(
        normed_in_grad, *in_values, in_sum, got_sum, stream_mid_grad, (BF16,)
    )
    grad_back = exchange(
        line.passed(pack_back(stream_grad, attention_part, feedforward_part, head_gains, count))
    )

    for bit in lower_bits:
        gate_rows, gate_got = late_stage(gate_rows, gate_got, None, None, 1, bit)
        up_cols, up_got = late_stage(up_cols, up_got, None, None, 1, bit)
    shape = gate_rows.shape[1:-1] + (2 * ff_part,)
    side_own, side_sent = local_call(
        side_kernel,
        (gate_rows, up_cols, *line.hold(gate_got, up_got)),
        [(shape, F32), (shape, BF16)],
        "side",
    )
    side_got = swap_row(line.passed(side_sent))
    heads_own, heads_got = late_stage(heads_first, heads_got, levels - 2, 2, levels - 2, 1)
    (layer_out,) = local_call(
        layer_out_kernel, (stream_mid, out_near, line.hold(layer_z)), [(block, BF16)], "layer_out"
    )
    line.passed(layer_out)
    output_got, side_got, heads_got, layer_out = line.hold(
        output_got, side_got, heads_got, layer_out
    )
    line.passed(side_got)
    output_rows, output_got = late_stage(
        output_rows, output_got, None, None, 0, top_bit, top_place
    )
    heads_own, heads_got = late_stage(heads_own, heads_got, None, None, 0, top_bit)
    sent = jnp.stack([pick(part, 1 - zbit, 0).astype(BF16) for part in (side_own, side_got)])
    side_z = swap_z(line.passed(sent))
    grad_back, layer_out = line.hold(grad_back, layer_out)
    line.passed(grad_back)
    out_back = exchange(layer_out)
    heads_got_other, down_got = line.hold(heads_got_other, down_got)
    line.passed(down_got)
    heads_other, heads_got_other = late_stage(
        heads_second, heads_got_other, levels - 2, 2, levels - 2, 1
    )

    def finish(kept, got):
        value = line.passed(add_got(kept, line.hold(got)))
        for bit in lower_bits:
            value = pick(value, my_bit(bit), 0) + swap_dp(
                pick(value, 1 - my_bit(bit), 0).astype(BF16), bit
            ).astype(F32)
        return value

    down_grad = finish(down_rows, down_got)
    heads_other, heads_got_other = late_stage(heads_other, heads_got_other, None, None, 0, top_bit)
    output_weight_grad = finish(output_rows, output_got)
    side_z = line.hold(side_z)

    def up_columns(at):
        columns = slice(at, at + ff_part)
        keep = [pick(part[..., columns], zbit, 0) for part in (side_own, side_got.astype(F32))]
        swapped = side_z[..., columns].astype(F32)
        table = [
            by_half(zbit, near_piece, far_piece)
            for near_piece, far_piece in zip(
                by_half(row, keep[0], keep[1]), by_half(row, swapped[0], swapped[1])
            )
        ]
        return jnp.concatenate(
            [
                table[part][z][:, i * run : (i + 1) * run]
                for part in range(2)
                for i in range(runs)
                for z in range(2)
            ],
            axis=1,
        )

    gate_weight_grad = up_columns(0)
    up_weight_grad = line.passed(up_columns(ff_part))
    heads_grad_own = finish(heads_own, heads_got)
    out_back = line.passed(line.hold(out_back))
    heads_grad_other = finish(heads_other, heads_got_other)

    def head_grad(start, width):
        own = heads_grad_own[:, start : start + width]
        other = heads_grad_other[:, start : start + width]
        return jnp.concatenate(by_half(row, own, other), axis=1)

    query_weight_grad = head_grad(0, query_part)
    key_weight_grad = head_grad(query_part, key_part)
    value_weight_grad = head_grad(query_part + key_part, key_part)

    back = grad_back.reshape(count, -1, features).astype(F32)
    grad_back = back[:, :-EXTRA].reshape(half, features)
    totals = jnp.sum(back[:, -EXTRA:], axis=0)
    out_back = out_back.astype(F32)
    gains = jnp.concatenate([totals[i] + totals[i + 4] for i in range(3)])[None]
    gains = gains + swap_col(gains)
    gain_low, gain_high = (part[0] for part in by_half(row, gains, swap_row(gains)))
    attention_total = jnp.concatenate([gain_low[:features], gain_high[:features]])
    feedforward_total = jnp.concatenate(
        [gain_low[features : 2 * features], gain_high[features : 2 * features]]
    )
    head_totals = (gain_low + gain_high)[2 * features :]
    return (
        out_back,
        grad_back,
        attention_total,
        query_weight_grad,
        key_weight_grad,
        value_weight_grad,
        head_totals[:HEAD_SIZE],
        head_totals[HEAD_SIZE : 2 * HEAD_SIZE],
        output_weight_grad,
        feedforward_total,
        gate_weight_grad,
        up_weight_grad,
        down_grad,
    )


def solution(mesh):
    placed = (
        P(("dp", "col"), "row"),
        P(("dp", "col"), "row"),
        P("dp", None),
        P("dp", None),
        P("row"),
        P("row", "col"),
        P("row", "col"),
        P("row", "col"),
        P(),
        P(),
        P("col", "row"),
        P("row"),
        P("row", "col"),
        P("row", "col"),
        P("col", "row"),
    )
    return jax.shard_map(
        shards,
        mesh=mesh,
        in_specs=placed,
        out_specs=(
            P(("dp", "col"), "row"),
            P(("dp", "col"), "row"),
            P(),
            P(("row", "dp"), "col"),
            P(("row", "dp"), "col"),
            P(("row", "dp"), "col"),
            P(),
            P(),
            P(("col", "dp"), "row"),
            P(),
            P(("row", "dp"), "col"),
            P(("row", "dp"), "col"),
            P(("col", "dp"), "row"),
        ),
        check_vma=False,
    )
```

```python
import math

import jax
import jax.numpy as jnp
from jax import lax
from jax.experimental import pallas as pl
from jax.experimental.pallas import tpu as pltpu
from jax.sharding import PartitionSpec as P

D = 2048
HEAD_SIZE = 128
EPSILON = 1e-06
ROPE_BASE = 1000000.0
NEGATIVE = -1e30
EXTRA = 8
VMEM_LIMIT = 28 << 20
BF16 = jnp.bfloat16
F32 = jnp.float32


def dot_nn(left, right):
    return jnp.dot(left, right, preferred_element_type=F32)


def dot_nt(left, right):
    return lax.dot_general(left, right, (((1,), (1,)), ((), ())), preferred_element_type=F32)


def dot_tn(left, right):
    return lax.dot_general(left, right, (((0,), (0,)), ((), ())), preferred_element_type=F32)


def swap_row(value):
    return lax.ppermute(value, "row", [(0, 1), (1, 0)])


def swap_col(value):
    return lax.ppermute(value, "col", [(0, 1), (1, 0)])


def swap_dp(value, bit):
    count = lax.axis_size("dp")
    return lax.ppermute(value, "dp", [(i, i ^ bit) for i in range(count)])


def swap_z(value):
    return swap_dp(value, 2)


def rotary_tables(position):
    half = HEAD_SIZE // 2
    frequency = ROPE_BASE ** (-2.0 * jnp.arange(half, dtype=F32) / HEAD_SIZE)
    angles = position.astype(F32)[:, None] * frequency[None, :]
    cosine, sine = jnp.cos(angles), jnp.sin(angles)
    return jnp.concatenate([cosine, cosine], axis=1), jnp.concatenate([-sine, sine], axis=1)


def pick(value, index, axis):
    return lax.dynamic_index_in_dim(value, index, axis, keepdims=False)


def high_bits(count):
    bits, bit = [], 4
    while bit < count:
        bits.append(bit)
        bit *= 2
    return bits


def split_rows(value, levels):
    return value.reshape((2,) * levels + (value.shape[0] >> levels,) + value.shape[1:])


def exchange(value):
    return lax.all_to_all(value, "dp", split_axis=0, concat_axis=0, tiled=True)


def after(value, *earlier):
    return lax.optimization_barrier((value,) + earlier)[0]


def together(*values):
    return lax.optimization_barrier(values)


class Line:
    def __init__(self, value):
        self.last = value

    def hold(self, *values):
        held = together(*values, self.last)[:-1]
        return held[0] if len(held) == 1 else held

    def passed(self, value):
        self.last = value
        return value


def by_half(index, own, other):
    first = index == 0
    return jnp.where(first, own, other), jnp.where(first, other, own)


WINDOWS = {
    "heads_kept": 6.0,
    "attend": 2.0,
    "out_own": 3.0,
    "act_kept": 3.0,
    "gate_and_up": 3.0,
    "mid_sent": 3.0,
    "mid_kept": 1.5,
    "up_rows": 2.5,
    "down_first": 3.0,
    "attention_kept": 3.5,
    "attend_back": 2.0,
    "normed_in": 6.5,
    "heads_second": 2.0,
}


def light(name):
    amount = WINDOWS.get(name, 0.05) * 0.1
    return pl.CostEstimate(
        flops=int(amount * 1.15e9), bytes_accessed=int(amount * 3.69e6), transcendentals=0
    )


def params(grid_axes=1):
    return pltpu.CompilerParams(vmem_limit_bytes=VMEM_LIMIT)


def scalars(*values):
    return jnp.stack([jnp.asarray(v, jnp.int32) for v in values])


def lanes_of(sums):
    return jnp.broadcast_to(sums, (sums.shape[0], HEAD_SIZE)).T[:8]


def column_of(lanes):
    return lanes.T[:, :1]


def local_call(kernel, inputs, outputs, name):
    return pl.pallas_call(
        kernel,
        out_shape=[jax.ShapeDtypeStruct(shape, dtype) for shape, dtype in outputs],
        compiler_params=params(),
        cost_estimate=light(name),
        name=name,
    )(*inputs)


def grid_call(kernel, grid, picks, inputs, in_specs, out_specs, outputs, name):
    return pl.pallas_call(
        kernel,
        grid_spec=pltpu.PrefetchScalarGridSpec(
            num_scalar_prefetch=1, grid=(grid,), in_specs=in_specs, out_specs=out_specs
        ),
        out_shape=[jax.ShapeDtypeStruct(shape, dtype) for shape, dtype in outputs],
        compiler_params=params(),
        cost_estimate=light(name),
        name=name,
    )(picks, *inputs)


def assemble(shape, pieces, name):
    def kernel(*refs):
        for (first, column, piece), ref in zip(pieces, refs):
            rows, columns = piece.shape
            refs[-1][first : first + rows, column : column + columns] = ref[...]

    values = [piece for _, _, piece in pieces]
    return local_call(kernel, values, [(shape, values[0].dtype)], name)[0]


def product(
    left, right, kind, dtype, tile, part=0, size=None, block=0, rows=None, name=None
):
    contract = {"nn": ((1,), (0,)), "nt": ((1,), (1,)), "tn": ((0,), (0,))}[kind]
    size = right.shape[0] if size is None else size
    rows = left.shape[0] if rows is None else rows
    if kind == "tn":
        shape, steps = (left.shape[1], right.shape[1]), left.shape[1] // tile
        specs = [
            pl.BlockSpec((rows, tile), lambda j, s: (block, j)),
            pl.BlockSpec((size, right.shape[1]), lambda j, s: (s[0], 0)),
        ]
        out = pl.BlockSpec((tile, shape[1]), lambda j, s: (j, 0))
    else:
        width = right.shape[1] if kind == "nn" else size
        shape, steps = (rows, width), width // tile
        if kind == "nn":
            right_spec = pl.BlockSpec((size, tile), lambda j, s: (s[0], j))
        else:
            right_spec = pl.BlockSpec(
                (tile, right.shape[1]), lambda j, s: (s[0] * (size // tile) + j, 0)
            )
        specs = [pl.BlockSpec((rows, left.shape[1]), lambda j, s: (block, 0)), right_spec]
        out = pl.BlockSpec((rows, tile), lambda j, s: (0, j))

    def kernel(picks, left_ref, right_ref, out_ref):
        out_ref[...] = lax.dot_general(
            left_ref[...], right_ref[...], (contract, ((), ())), preferred_element_type=F32
        ).astype(out_ref.dtype)

    return grid_call(
        kernel,
        steps,
        scalars(part),
        (left, right),
        specs,
        [out],
        [(shape, dtype)],
        name or "product_" + kind,
    )[0]


def product_onto(left, right, part, size, own, tile, name):
    rows, width = own.shape
    half = rows // 2

    def kernel(picks, left_ref, right_ref, own_ref, kept_ref, sent_ref):
        total = own_ref[...] + dot_nn(left_ref[...], right_ref[...])
        kept_ref[...] = total[:half]
        sent_ref[...] = total[half:].astype(BF16)

    return grid_call(
        kernel,
        width // tile,
        scalars(part),
        (left, right, own),
        [
            pl.BlockSpec(left.shape, lambda j, s: (0, 0)),
            pl.BlockSpec((size, tile), lambda j, s: (s[0], j)),
            pl.BlockSpec((rows, tile), lambda j, s: (0, j)),
        ],
        [pl.BlockSpec((half, tile), lambda j, s: (0, j))] * 2,
        [((half, width), F32), ((half, width), BF16)],
        name,
    )


def down_product(act_all, down_own, down_other, own_at, other_at, tile):
    rows, width = act_all.shape
    half, size, features = rows // 2, width // 2, down_own.shape[1]
    quarter = half // 2

    def kernel(picks, act_ref, own_ref, other_ref, kept_ref, near_ref, far_ref):
        total = dot_nn(act_ref[:, :size], own_ref[...]) + dot_nn(act_ref[:, size:], other_ref[...])
        kept_ref[...] = total[:half]
        near_ref[...] = total[half : half + quarter].astype(BF16)
        far_ref[...] = total[half + quarter :].astype(BF16)

    return grid_call(
        kernel,
        features // tile,
        scalars(own_at, other_at),
        (act_all, down_own, down_other),
        [
            pl.BlockSpec(act_all.shape, lambda j, s: (0, 0)),
            pl.BlockSpec((size, tile), lambda j, s: (s[0], j)),
            pl.BlockSpec((size, tile), lambda j, s: (s[1], j)),
        ],
        [pl.BlockSpec((half, tile), lambda j, s: (0, j))]
        + [pl.BlockSpec((quarter, tile), lambda j, s: (0, j))] * 2,
        [((half, features), F32), ((quarter, features), BF16), ((quarter, features), BF16)],
        "down_proj",
    )


def heads_forward(scaled, query_weight, key_weight, value_weight, part, dtype, name):
    group, features = scaled.shape
    query_part, tile = query_weight.shape[1] // 2, key_weight.shape[1] // 2
    steps = query_part // tile

    def kernel(picks, x_ref, query_ref, key_ref, value_ref, out_ref):
        step = pl.program_id(0)
        for condition, ref in (
            (step < steps, query_ref),
            (step == steps, key_ref),
            (step == steps + 1, value_ref),
        ):

            @pl.when(condition)
            def _():
                out_ref[...] = dot_nn(x_ref[...], ref[...]).astype(out_ref.dtype)

    return grid_call(
        kernel,
        steps + 2,
        scalars(part),
        (scaled, query_weight, key_weight, value_weight),
        [
            pl.BlockSpec((group, features), lambda j, s: (0, 0)),
            pl.BlockSpec(
                (features, tile), lambda j, s: (0, s[0] * steps + jnp.minimum(j, steps - 1))
            ),
            pl.BlockSpec((features, tile), lambda j, s: (0, s[0])),
            pl.BlockSpec((features, tile), lambda j, s: (0, s[0])),
        ],
        [pl.BlockSpec((group, tile), lambda j, s: (0, j))],
        [((group, query_part + 2 * tile), dtype)],
        name,
    )[0]


def heads_backward(grads, query_weight, key_weight, value_weight, part, own=None):
    group = grads.shape[0]
    half = group // 2
    features = query_weight.shape[0]
    query_part, key_part = query_weight.shape[1] // 2, key_weight.shape[1] // 2
    tile = features // 2

    def kernel(picks, grads_ref, query_ref, key_ref, value_ref, *refs):
        total = dot_nt(grads_ref[:, :query_part], query_ref[...])
        total += dot_nt(grads_ref[:, query_part : query_part + key_part], key_ref[...])
        total += dot_nt(grads_ref[:, query_part + key_part :], value_ref[...])
        if own is None:
            refs[0][...] = total
        else:
            total += refs[0][...]
            refs[1][...] = total[:half]
            refs[2][...] = total[half:].astype(BF16)

    whole = pl.BlockSpec((group, tile), lambda j, s: (0, j))
    split = pl.BlockSpec((half, tile), lambda j, s: (0, j))
    outputs = [((group, features), F32)]
    if own is not None:
        outputs = [((half, features), F32), ((half, features), BF16)]
    return grid_call(
        kernel,
        2,
        scalars(part),
        (grads, query_weight, key_weight, value_weight) + (() if own is None else (own,)),
        [
            pl.BlockSpec(grads.shape, lambda j, s: (0, 0)),
            pl.BlockSpec((tile, query_part), lambda j, s: (j, s[0])),
            pl.BlockSpec((tile, key_part), lambda j, s: (j, s[0])),
            pl.BlockSpec((tile, key_part), lambda j, s: (j, s[0])),
        ]
        + ([] if own is None else [whole]),
        [whole] if own is None else [split, split],
        outputs,
        "heads_backward",
    )


def up_kernel(picks, mid_ref, gate_ref, up_ref, *refs):
    parts = 2
    gate_parts, up_parts = refs[:parts], refs[parts : 2 * parts]
    kept_ref, *got_refs = refs[2 * parts : -3]
    gate_grad_ref, up_grad_ref, act_ref = refs[-3:]
    features = gate_ref.shape[0]
    share = gate_parts[0].shape[0]

    def columns(own_ref, part_refs):
        total = dot_nn(mid_ref[:, :features], own_ref[...])
        for i, ref in enumerate(part_refs):
            at = pl.multiple_of(features + picks[1 + i] * share, share)
            total += dot_nn(mid_ref[:, pl.ds(at, share)], ref[...])
        return total

    gate = columns(gate_ref, gate_parts)
    up = columns(up_ref, up_parts)
    got = jnp.concatenate([ref[...] for ref in got_refs], axis=0)
    act_grad = kept_ref[...] + got.astype(F32)
    sigmoid = jax.nn.sigmoid(gate)
    silu = gate * sigmoid
    act_ref[...] = (silu * up).astype(BF16)
    gate_grad_ref[...] = (act_grad * up * sigmoid * (1.0 + gate * (1.0 - sigmoid))).astype(BF16)
    up_grad_ref[...] = (act_grad * silu).astype(BF16)


def gate_and_up(mid, gate, up, base, pieces, places, kept, got):
    rows = mid.shape[0]
    features = gate.shape[0]
    width = kept.shape[1]
    tile = width // 3
    share = pieces[0][0].shape[0]

    def columns(height, first):
        return pl.BlockSpec((height, tile), lambda j, s: (0, first + j))

    own = pl.BlockSpec((features, tile), lambda j, s: (0, 3 * s[0] + j))
    return grid_call(
        up_kernel,
        3,
        scalars(base, *places),
        (mid, gate, up, *pieces[0], *pieces[1], kept, *got),
        [pl.BlockSpec(mid.shape, lambda j, s: (0, 0)), own, own]
        + [columns(share, 0)] * (2 * len(places))
        + [columns(rows, 0)]
        + [columns(g.shape[0], 0) for g in got],
        [columns(rows, 0)] * 3,
        [((rows, width), BF16)] * 3,
        "gate_and_up",
    )


def up_back_kernel(picks, gate_grad_ref, up_grad_ref, gate_ref, up_ref, *refs):
    *pieces, near_ref, far_ref = refs
    count = len(pieces) // 2
    features = gate_ref.shape[0]
    share = pieces[0].shape[0]
    gate_grad, up_grad = gate_grad_ref[...], up_grad_ref[...]
    for i in range(features // share):
        at = slice(i * share, (i + 1) * share)
        total = dot_nt(gate_grad, gate_ref[at, :]) + dot_nt(up_grad, up_ref[at, :])
        near_ref[:, at] = total.astype(near_ref.dtype)
    for i in range(count):
        total = dot_nt(gate_grad, pieces[i][...]) + dot_nt(up_grad, pieces[count + i][...])
        at = pl.multiple_of(picks[1 + i] * share, share)
        far_ref[:, pl.ds(at, share)] = total.astype(far_ref.dtype)


def gate_and_up_back(gate_grad, up_grad, block, gate, up, base, pieces, places, dtype, name):
    rows = gate_grad.shape[0] // 2
    width = gate_grad.shape[1]
    features = gate.shape[0]
    grads = pl.BlockSpec((rows, width), lambda j, s: (block, 0))
    own = pl.BlockSpec((features, width), lambda j, s: (0, s[0]))
    pieces = (*pieces[0], *pieces[1])
    piece = pl.BlockSpec(pieces[0].shape, lambda j, s: (0, 0))
    shape = (rows, features)
    return grid_call(
        up_back_kernel,
        1,
        scalars(base, *places),
        (gate_grad, up_grad, gate, up, *pieces),
        [grads, grads, own, own] + [piece] * len(pieces),
        [pl.BlockSpec(shape, lambda j, s: (0, 0))] * 2,
        [(shape, dtype)] * 2,
        name,
    )


def in_place(weight):
    return pltpu.with_memory_space_constraint(weight, pltpu.MemorySpace.HBM)


def my_bit(bit):
    return (lax.axis_index("dp") // bit) % 2


def view(shape, columns=None, **at):
    at = {int(axis[1:]): place for axis, place in at.items()}
    parts, part = columns or (1, 0)
    last = len(shape) - 1
    block = tuple(
        None if axis in at else length // (parts if axis == last else 1)
        for axis, length in enumerate(shape)
    )
    return pl.BlockSpec(
        block,
        lambda j, s: tuple(
            s[at[axis]] if axis in at else (part if axis == last else 0)
            for axis in range(len(shape))
        ),
    )


def without(shape, *axes):
    return tuple(length for axis, length in enumerate(shape) if axis not in axes)


def take(value, axis, index, columns=None):
    shape = without(value.shape, axis)
    shape = shape[:-1] + (shape[-1] // (columns or (1, 0))[0],)

    def kernel(picks, in_ref, out_ref):
        out_ref[...] = in_ref[...].astype(BF16)

    return grid_call(
        kernel,
        1,
        scalars(index),
        (value,),
        [view(value.shape, columns, **{f"a{axis}": 0})],
        [view(shape)],
        [(shape, BF16)],
        "take",
    )[0]


def start_stage(value, axis, bit):
    return swap_dp(take(value, axis, 1 - my_bit(bit)), bit)


def end_stage(value, got, axis, bit, next_axis=None, next_index=None, columns=None):
    joined = got.shape
    side = {} if axis is None else {f"a{axis}": 0}
    mine = 0 if axis is None else my_bit(bit)
    if next_axis is None:

        def kernel(picks, value_ref, got_ref, out_ref):
            out_ref[...] = value_ref[...].astype(F32) + got_ref[...].astype(F32)

        return grid_call(
            kernel,
            1,
            scalars(mine),
            (value, got),
            [view(value.shape, **side), view(joined)],
            [view(joined)],
            [(joined, F32)],
            "join",
        )[0]
    shape = without(joined, next_axis)
    behind = next_axis + (1 if axis is not None and next_axis >= axis else 0)

    def kernel(picks, keep_ref, keep_got, send_ref, send_got, kept_ref, sent_ref):
        kept_ref[...] = keep_ref[...].astype(F32) + keep_got[...].astype(F32)
        sent_ref[...] = (send_ref[...].astype(F32) + send_got[...].astype(F32)).astype(BF16)

    return grid_call(
        kernel,
        1,
        scalars(mine, next_index, 1 - next_index),
        (value, got, value, got),
        [
            view(value.shape, columns, **side, **{f"a{behind}": 1}),
            view(joined, **{f"a{next_axis}": 1}),
            view(value.shape, columns, **side, **{f"a{behind}": 2}),
            view(joined, **{f"a{next_axis}": 2}),
        ],
        [view(shape)] * 2,
        [(shape, F32), (shape, BF16)],
        "join_and_split",
    )


def add_got(kept, got):
    def kernel(kept_ref, got_ref, out_ref):
        out_ref[...] = kept_ref[...].astype(F32) + got_ref[...].astype(F32)

    return local_call(kernel, (kept, got), [(kept.shape, F32)], "add_got")[0]


def split_top(own, other, row):
    mine = my_bit(lax.axis_size("dp") // 2) == row

    def kernel(picks, own_ref, other_ref, kept_ref, sent_ref):
        for first, second, flag in ((own_ref, other_ref, 1), (other_ref, own_ref, 0)):

            @pl.when(picks[0] == flag)
            def _():
                kept_ref[...] = first[...].astype(F32)
                sent_ref[...] = second[...].astype(BF16)

    spec = view(own.shape)
    return grid_call(
        kernel,
        1,
        scalars(mine),
        (own, other),
        [spec, spec],
        [spec, spec],
        [(own.shape, F32), (own.shape, BF16)],
        "split_top",
    )


def join_core_kernel(
    near_ref, far_ref, got_near, got_far, own_ref, row_ref, z_ref, row_both_ref, z_both_ref
):
    half = own_ref.shape[0]
    quarter = half // 2
    near = near_ref[...] + got_near[...].astype(F32)
    far = far_ref[...] + got_far[...].astype(F32)
    own_ref[...] = near[:half]
    row_ref[...] = far[:half]
    z_ref[...] = near[half:]
    row_both_ref[...] = far[half : half + quarter].astype(BF16)
    z_both_ref[...] = far[half + quarter :].astype(BF16)


def join_corner_kernel(row_ref, z_ref, via_row_ref, via_z_ref, to_row_ref, to_z_ref):
    quarter = via_row_ref.shape[0]
    to_row_ref[:quarter, :] = row_ref[:quarter, :].astype(BF16)
    to_row_ref[quarter:, :] = (row_ref[quarter:, :] + via_z_ref[...].astype(F32)).astype(BF16)
    to_z_ref[:quarter, :] = (z_ref[:quarter, :] + via_row_ref[...].astype(F32)).astype(BF16)
    to_z_ref[quarter:, :] = z_ref[quarter:, :].astype(BF16)


def norm_sums_kernel(*refs):
    parts = refs[:-6]
    base_ref, inverse_ref, gain_ref, grad_ref, sums_ref, gain_grad_ref = refs[-6:]
    grad = sum(part[...].astype(F32) for part in parts)
    unit = base_ref[...].astype(F32) * column_of(inverse_ref[...])
    along = grad * unit
    grad_ref[...] = grad
    sums_ref[...] = lanes_of(jnp.sum(along * gain_ref[...], axis=1, keepdims=True))
    gain_grad_ref[...] = jnp.sum(along, axis=0, keepdims=True)


def norm_sums(parts, base, inverse, gain):
    rows, features = base.shape
    return local_call(
        norm_sums_kernel,
        (*parts, base, inverse, gain),
        [((rows, features), F32), ((8, rows), F32), ((1, features), F32)],
        "norm_sums",
    )


def norm_grad_kernel(
    grad_ref, base_ref, inverse_ref, gain_ref, sums_ref, got_sums_ref, rest_ref, *out_refs
):
    inverse = column_of(inverse_ref[...])
    unit = base_ref[...].astype(F32) * inverse
    mean = column_of(sums_ref[...] + got_sums_ref[...]) * (1.0 / D)
    out = rest_ref[...].astype(F32) + inverse * (grad_ref[...] * gain_ref[...] - unit * mean)
    for out_ref in out_refs:
        out_ref[...] = out.astype(out_ref.dtype)


def norm_grad(grad, base, inverse, gain, sums, got_sums, rest, dtypes):
    return local_call(
        norm_grad_kernel,
        (grad, base, inverse, gain, sums, got_sums, rest),
        [(grad.shape, dtype) for dtype in dtypes],
        "norm_grad",
    )


def middle_kernel(x_ref, part_ref, got_ref, mid_ref, square_ref):
    mid = x_ref[...].astype(F32) + part_ref[...] + got_ref[...].astype(F32)
    mid_ref[...] = mid
    square_ref[...] = lanes_of(jnp.sum(mid * mid, axis=1, keepdims=True))


def normed_kernel(mid_ref, square_ref, got_ref, gain_ref, normed_ref, inverse_ref):
    inverse = lax.rsqrt((square_ref[...] + got_ref[...]) * (1.0 / D) + EPSILON)
    inverse_ref[...] = inverse
    unit = mid_ref[...].astype(F32) * column_of(inverse)
    normed_ref[...] = (unit * gain_ref[...]).astype(BF16)


def scaled_kernel(own_ref, got_ref, gain_ref, x_ref, scaled_ref, square_ref):
    half = own_ref.shape[0]
    for first, ref in ((0, own_ref), (half, got_ref)):
        at = slice(first, first + half)
        values = ref[...].astype(F32)
        x_ref[at, :] = ref[...]
        scaled_ref[at, :] = (values * gain_ref[...]).astype(BF16)
        square_ref[:, at] = lanes_of(jnp.sum(values * values, axis=1, keepdims=True))


def normed_in_kernel(x_ref, inverse_ref, gain_ref, normed_ref):
    unit = x_ref[...].astype(F32) * column_of(inverse_ref[...])
    normed_ref[...] = (unit * gain_ref[...]).astype(BF16)


def block_of(weight, block_row, block_column, shape):
    def kernel(picks, in_ref, out_ref):
        out_ref[...] = in_ref[...]

    return grid_call(
        kernel,
        1,
        scalars(block_row, block_column),
        (weight,),
        [pl.BlockSpec(shape, lambda j, s: (s[0], s[1]))],
        [pl.BlockSpec(shape, lambda j, s: (0, 0))],
        [(shape, BF16)],
        "block_of",
    )[0]


def side_kernel(*refs):
    kept_ref, sent_ref = refs[-2:]
    parts = (len(refs) - 2) // 2
    width = refs[0].shape[-1]
    for i in range(parts):
        total = refs[i][...].astype(F32) + refs[parts + i][...].astype(F32)
        at = slice(i * width, (i + 1) * width)
        kept_ref[:, :, at] = total[0]
        sent_ref[:, :, at] = total[1].astype(BF16)


def pack_back(grad, attention_part, feedforward_part, head_gains, count):
    rows, features = grad.shape
    share = rows // count

    def kernel(grad_ref, attention_ref, feedforward_ref, heads_ref, out_ref):
        rest = jnp.zeros((1, features - 2 * HEAD_SIZE), F32)
        heads = jnp.concatenate([heads_ref[:1, :], heads_ref[1:, :], rest], axis=1)
        values = jnp.concatenate([attention_ref[...], feedforward_ref[...], heads, heads], axis=0)
        high = values.astype(BF16)
        low = (values - high.astype(F32)).astype(BF16)
        extra = jnp.concatenate([high.astype(F32), low.astype(F32)], axis=0).astype(BF16)
        for i in range(count):
            out_ref[i, :share, :] = grad_ref[i * share : (i + 1) * share, :]
            out_ref[i, share:, :] = extra

    return local_call(
        kernel,
        (grad, attention_part, feedforward_part, head_gains),
        [((count, share + EXTRA, features), BF16)],
        "pack_back",
    )[0]


def layer_out_kernel(mid_ref, kept_ref, got_ref, out_ref):
    out_ref[...] = (mid_ref[...] + kept_ref[...] + got_ref[...].astype(F32)).astype(BF16)


def out_near_kernel(kept_ref, got_near, got_far, near_ref, far_ref):
    half = near_ref.shape[0]
    near_ref[...] = kept_ref[:half, :] + got_near[...].astype(F32)
    far_ref[...] = (kept_ref[half:, :] + got_far[...].astype(F32)).astype(BF16)


def turn(values, cosine, sine):
    return values * cosine + pltpu.roll(values, HEAD_SIZE // 2, 1) * sine


def unit_of(raw):
    inverse = lax.rsqrt(jnp.mean(raw * raw, axis=-1, keepdims=True) + EPSILON)
    return raw * inverse, inverse


def scores_to_prob(query_rot, key_rot, allowed):
    scores = dot_nt(query_rot, key_rot) * (1.0 / math.sqrt(HEAD_SIZE))
    scores = jnp.where(allowed, scores, NEGATIVE)
    exps = jnp.exp(scores - jnp.max(scores, axis=-1, keepdims=True))
    return exps * (1.0 / jnp.sum(exps, axis=-1, keepdims=True))


def head_inputs(own, got, inverse_in, width):
    raw = (own[...] + got[...].astype(F32)) * inverse_in
    return [raw[:, i * HEAD_SIZE : (i + 1) * HEAD_SIZE] for i in range(width // HEAD_SIZE)]


def attend_kernel(
    query_own, query_got, key_own, key_got, value_own, value_got, inverse_ref, cosine_ref,
    sine_ref, slot_ref, start_ref, across_ref, query_gain_ref, key_gain_ref, out_ref,
):
    inverse_in = column_of(inverse_ref[...])
    cosine, sine = cosine_ref[...], sine_ref[...]
    across = across_ref[...]
    (key_raw,) = head_inputs(key_own, key_got, inverse_in, HEAD_SIZE)
    (value,) = head_inputs(value_own, value_got, inverse_in, HEAD_SIZE)
    key_rot = turn(unit_of(key_raw)[0] * key_gain_ref[...], cosine, sine).astype(BF16)
    value = value.astype(BF16)
    slots, first = column_of(slot_ref[...]), column_of(start_ref[...])
    rows = out_ref.shape[0] // 2

    for block in range(2):
        at = slice(block * rows, (block + 1) * rows)
        allowed = (across <= slots[at]) & (across >= first[at])
        for i in range(query_own.shape[1] // HEAD_SIZE):
            head = slice(i * HEAD_SIZE, (i + 1) * HEAD_SIZE)
            raw = (query_own[at, head] + query_got[at, head].astype(F32)) * inverse_in[at]
            pre = unit_of(raw)[0] * query_gain_ref[...]
            query_rot = turn(pre, cosine_ref[at, :], sine_ref[at, :]).astype(BF16)
            prob = scores_to_prob(query_rot, key_rot, allowed).astype(BF16)
            out_ref[at, head] = dot_nn(prob, value).astype(BF16)


def attend_back_kernel(
    query_own, query_got, key_own, key_got, value_own, value_got, inverse_ref, cosine_ref,
    sine_ref, slot_ref, start_ref, across_ref, query_gain_ref, key_gain_ref, grad_own, grad_got,
    out_ref, gain_ref,
):
    step = pl.program_id(0)
    repeat = query_own.shape[1] // HEAD_SIZE
    kv_heads = out_ref.shape[1] // (query_own.shape[1] + 2 * HEAD_SIZE)
    scale = 1.0 / math.sqrt(HEAD_SIZE)
    inverse_in = column_of(inverse_ref[...])
    cosine, sine = cosine_ref[...], sine_ref[...]
    across = across_ref[...]
    allowed = (across <= column_of(slot_ref[...])) & (across >= column_of(start_ref[...]))
    query_gain, key_gain = query_gain_ref[...], key_gain_ref[...]

    @pl.when(step == 0)
    def _():
        gain_ref[...] = jnp.zeros_like(gain_ref)

    (key_raw,) = head_inputs(key_own, key_got, inverse_in, HEAD_SIZE)
    (value,) = head_inputs(value_own, value_got, inverse_in, HEAD_SIZE)
    key_unit, key_inverse = unit_of(key_raw)
    key_rot = turn(key_unit * key_gain, cosine, sine).astype(BF16)
    value = value.astype(BF16)

    def norm_back(rot_grad, unit, inverse, gain, at):
        pre = rot_grad * cosine - pltpu.roll(rot_grad, HEAD_SIZE // 2, 1) * sine
        gain_ref[at : at + 1, :] += jnp.sum(pre * unit, axis=0, keepdims=True)
        scaled = pre * gain
        return inverse * (scaled - unit * jnp.mean(scaled * unit, axis=-1, keepdims=True))

    key_grad = jnp.zeros(key_raw.shape, F32)
    value_grad = jnp.zeros(key_raw.shape, F32)
    for i, query_raw in enumerate(
        head_inputs(query_own, query_got, inverse_in, query_own.shape[1])
    ):
        at = slice(i * HEAD_SIZE, (i + 1) * HEAD_SIZE)
        query_unit, query_inverse = unit_of(query_raw)
        query_rot = turn(query_unit * query_gain, cosine, sine).astype(BF16)
        prob = scores_to_prob(query_rot, key_rot, allowed)
        grad_out = (grad_own[:, at] + grad_got[:, at].astype(F32)).astype(BF16)
        prob_grad = dot_nt(grad_out, value)
        centre = jnp.sum(prob * prob_grad, axis=-1, keepdims=True)
        score_grad = (prob * (prob_grad - centre)).astype(BF16)
        value_grad += dot_tn(prob.astype(BF16), grad_out)
        key_grad += dot_tn(score_grad, query_rot)
        query_grad = norm_back(
            dot_nn(score_grad, key_rot) * scale, query_unit, query_inverse, query_gain, 0
        )
        column = pl.multiple_of((step * repeat + i) * HEAD_SIZE, HEAD_SIZE)
        out_ref[:, pl.ds(column, HEAD_SIZE)] = query_grad.astype(BF16)
    key_grad = norm_back(key_grad * scale, key_unit, key_inverse, key_gain, 1)
    column = pl.multiple_of((kv_heads * repeat + step) * HEAD_SIZE, HEAD_SIZE)
    out_ref[:, pl.ds(column, HEAD_SIZE)] = key_grad.astype(BF16)
    column = pl.multiple_of((kv_heads * (repeat + 1) + step) * HEAD_SIZE, HEAD_SIZE)
    out_ref[:, pl.ds(column, HEAD_SIZE)] = value_grad.astype(BF16)


def attention_specs(group, kv_heads, repeat):
    def block(width, first):
        return pl.BlockSpec((group, width), lambda j: (0, first + j))

    def whole(rows, columns):
        return pl.BlockSpec((rows, columns), lambda j: (0, 0))

    query = block(repeat * HEAD_SIZE, 0)
    key = block(HEAD_SIZE, kv_heads * repeat)
    value = block(HEAD_SIZE, kv_heads * (repeat + 1))
    return [query, query, key, key, value, value] + [
        whole(8, group),
        whole(group, HEAD_SIZE),
        whole(group, HEAD_SIZE),
        whole(8, group),
        whole(8, group),
        whole(1, group),
        whole(1, HEAD_SIZE),
        whole(1, HEAD_SIZE),
    ]


def attend(own, got, shared, kv_heads, repeat):
    group = own.shape[0]
    width = kv_heads * repeat * HEAD_SIZE
    return pl.pallas_call(
        attend_kernel,
        grid=(kv_heads,),
        in_specs=attention_specs(group, kv_heads, repeat),
        out_specs=pl.BlockSpec((group, repeat * HEAD_SIZE), lambda j: (0, j)),
        out_shape=jax.ShapeDtypeStruct((group, width), BF16),
        compiler_params=pltpu.CompilerParams(vmem_limit_bytes=VMEM_LIMIT),
        cost_estimate=light("attend"),
        name="attend",
    )(own, got, own, got, own, got, *shared)


def attend_back(own, got, shared, grad_own, grad_got, kv_heads, repeat):
    group, width = own.shape
    grad_block = pl.BlockSpec((group, repeat * HEAD_SIZE), lambda j: (0, j))
    return pl.pallas_call(
        attend_back_kernel,
        grid=(kv_heads,),
        in_specs=attention_specs(group, kv_heads, repeat) + [grad_block, grad_block],
        out_specs=[
            pl.BlockSpec((group, width), lambda j: (0, 0)),
            pl.BlockSpec((2, HEAD_SIZE), lambda j: (0, 0)),
        ],
        out_shape=[
            jax.ShapeDtypeStruct((group, width), BF16),
            jax.ShapeDtypeStruct((2, HEAD_SIZE), F32),
        ],
        compiler_params=pltpu.CompilerParams(vmem_limit_bytes=VMEM_LIMIT),
        cost_estimate=light("attend_back"),
        name="attend_back",
    )(own, got, own, got, own, got, *shared, grad_own, grad_got)

def shards(
    tokens,
    cotangent,
    seq_lengths,
    balance_order,
    attention_gain,
    query_weight,
    key_weight,
    value_projection,
    query_gain,
    key_norm_gain,
    output_weight,
    feedforward_gain,
    gate_weight,
    up_weight,
    down_weight,
):
    count = lax.axis_size("dp")
    levels = count.bit_length() - 1
    row = lax.axis_index("row")
    col = lax.axis_index("col")
    xbit, zbit = my_bit(1), my_bit(2)
    half = tokens.shape[0]
    quarter = half // 2
    group = 2 * half
    pair = 2 * group
    features = tokens.shape[1]
    query_part = query_weight.shape[1] // 2
    key_part = key_weight.shape[1] // 2
    heads = query_part // HEAD_SIZE
    kv_heads = key_part // HEAD_SIZE
    repeat = heads // kv_heads
    ff_half = gate_weight.shape[1]
    runs = count // 8
    projections = tuple(map(in_place, (query_weight, key_weight, value_projection)))
    output_weight = in_place(output_weight)
    if runs == 1:
        gate_weight, up_weight, down_weight = map(in_place, (gate_weight, up_weight, down_weight))
    run = 2 * ff_half // count
    ff_part = ff_half // 4
    all_bits = high_bits(count)[::-1]

    def ff_block(weight, part, axis):
        if runs == 1:
            return weight, part * 2 + zbit
        pieces = [
            lax.dynamic_slice_in_dim(weight, ((part * runs + i) * 2 + zbit) * run, run, axis)
            for i in range(runs)
        ]
        return jnp.concatenate(pieces, axis=axis), 0

    moved_in = exchange(tokens)
    share = features // 2
    gate_far, far_base = ff_block(gate_weight, 1 - row, 1)
    up_far, _ = ff_block(up_weight, 1 - row, 1)
    gate_sent, up_sent = (
        block_of(weight, xbit, far_base, (share, ff_part))
        for weight in (gate_far, up_far)
    )
    got_gate, got_up = swap_row(gate_sent), swap_row(up_sent)

    base_ids = jnp.arange(half, dtype=jnp.int32)
    local_ids = jnp.concatenate([col * half + base_ids, (1 - col) * half + base_ids])
    slot_ids = jnp.arange(group, dtype=jnp.int32)
    slot = jnp.sum(
        jnp.where(balance_order[0][None, :] == local_ids[:, None], slot_ids[None, :], 0), axis=1
    )
    lengths = seq_lengths[0]
    seq_ends = jnp.cumsum(lengths)
    starts = seq_ends - lengths
    segment = jnp.sum((slot[:, None] >= seq_ends[None, :]).astype(jnp.int32), axis=1)
    hits = segment[:, None] == jnp.arange(lengths.shape[0], dtype=jnp.int32)[None, :]
    start = jnp.sum(jnp.where(hits, starts[None, :], 0), axis=1)
    cosine, sine = rotary_tables(slot - start)
    slot_lanes = jnp.broadcast_to(slot.astype(F32)[None], (8, group))
    start_lanes = jnp.broadcast_to(start.astype(F32)[None], (8, group))
    moved_in, cosine, sine, slot_lanes, start_lanes, got_gate, up_sent = together(
        moved_in, cosine, sine, slot_lanes, start_lanes, got_gate, up_sent
    )

    gain_in = attention_gain.astype(F32)[None]
    gain_mid = feedforward_gain.astype(F32)[None]
    x_low, scaled_in, square = local_call(
        scaled_kernel,
        (moved_in, swap_col(moved_in), gain_in),
        [((group, features), BF16), ((group, features), BF16), ((8, group), F32)],
        "scaled",
    )
    moved_grad = exchange(after(cotangent, moved_in))
    heads_sent = heads_forward(after(scaled_in, got_gate, got_up), *projections, 1 - row, BF16, "heads_sent")
    got_square = swap_row(square)
    got_heads = swap_row(heads_sent)
    kept_heads = heads_forward(
        after(scaled_in, heads_sent), *projections, row, F32, "heads_kept"
    )
    got_gate, got_up = together(got_gate, got_up, heads_sent)[:2]
    got_gate_x, got_up_x = swap_dp(got_gate, 1), swap_dp(got_up, 1)

    down_own, own_at = ff_block(down_weight, row, 0)
    down_other, other_at = ff_block(down_weight, 1 - row, 0)

    def act_back(rows_of, weight, at, dtype, name="act_sent"):
        return product(rows_of, weight, "nt", dtype, ff_part // 3, at, ff_part, name=name)

    moved_grad = after(moved_grad, kept_heads)
    grad_z = swap_z(moved_grad)
    grad_near = swap_col(moved_grad)
    act_sent = [
        act_back(rows_of, down_other, other_at, BF16) for rows_of in (moved_grad, grad_near)
    ]
    got_heads, kept_heads, got_square, grad_z, *act_sent = together(
        got_heads, kept_heads, got_square, grad_z, *act_sent
    )
    inverse_in = lax.rsqrt((square + got_square) / D + EPSILON)
    shared = (
        inverse_in,
        cosine,
        sine,
        slot_lanes,
        start_lanes,
        slot_lanes[:1],
        query_gain.astype(F32)[None],
        key_norm_gain.astype(F32)[None],
    )
    got_act = [swap_row(act_sent[0])]
    grad_far = swap_col(grad_z)
    attention = attend(kept_heads, got_heads, shared, kv_heads, repeat)
    attention, got_act[0], grad_far = together(attention, got_act[0], grad_far)
    attention_other = swap_row(attention)
    got_act.append(swap_row(after(act_sent[1], attention)))
    out_own = product(
        attention, output_weight, "nn", F32, features // 2, row, query_part, name="out_own"
    )
    far_sent = [
        act_back(after(rows_of, out_own), down_other, other_at, BF16)
        for rows_of in (grad_z, grad_far)
    ]
    attention_other, got_act[1], got_gate_x, out_own, *far_sent = together(
        attention_other, got_act[1], got_gate_x, out_own, *far_sent
    )
    out_kept, out_sent = product_onto(
        attention_other, output_weight, 1 - row, query_part, out_own, features // 2, "out_proj"
    )
    out_got = swap_col(out_sent)
    stream_mid, square_mid = local_call(
        middle_kernel,
        (moved_in, out_kept, out_got),
        [((half, features), F32), ((8, half), F32)],
        "middle",
    )
    got_square = swap_row(square_mid)
    grad_all = assemble(
        (pair, features),
        [
            (0, 0, moved_grad),
            (half, 0, grad_z),
            (group, 0, grad_near),
            (group + half, 0, after(grad_far, square_mid)),
        ],
        "grad_all",
    )
    normed_mid, inverse_mid = local_call(
        normed_kernel,
        (stream_mid, square_mid, got_square, gain_mid),
        [((half, features), BF16), ((8, half), F32)],
        "normed",
    )

    by_row = swap_row(normed_mid)
    by_z = swap_z(normed_mid)
    act_kept = act_back(after(grad_all, normed_mid), down_own, own_at, F32, "act_kept")
    by_row, by_z, act_kept, got_up_x = together(by_row, by_z, act_kept, got_up_x)
    corner_a = swap_row(by_z[:quarter])
    corner_b = swap_z(by_row[quarter:])
    got_act.extend(swap_row(after(sent, by_row)) for sent in far_sent)
    near = [
        (0, 0, normed_mid),
        (0, features, by_row),
        (half, 0, by_z),
        (half, features, corner_a),
        (half + quarter, features, corner_b),
    ]
    crossed = [(group + first, at, swap_col(piece)) for first, at, piece in near]
    mid_all = assemble((pair, 2 * features), near + crossed, "mid_all")

    gate_own, own_base = ff_block(gate_weight, row, 1)
    up_own, _ = ff_block(up_weight, row, 1)
    places = (xbit, 1 - xbit)
    pieces = ((got_gate, got_gate_x), (got_up, got_up_x))
    up_weights = (gate_own, up_own, own_base, pieces, places)
    gate_grad, up_grad, activated = gate_and_up(
        mid_all, *up_weights, act_kept, (got_act[0], got_act[2], got_act[1], got_act[3])
    )

    act_got = swap_row(activated)
    line = Line(activated)
    top_bit, lower_bits = all_bits[0], all_bits[1:]
    top_place = jnp.where(my_bit(top_bit) == row, 0, 1)

    def up_rows(grad_part, name):
        whole = product(mid_all, grad_part, "tn", BF16, features // 2, name=name)
        return whole.reshape((2,) * (levels + 1) + (features // count, ff_part))

    def first_stage(value, axis, bit):
        sent = line.passed(take(value, axis, 1 - my_bit(bit)))
        return swap_dp(sent, bit)

    def late_stage(value, got, axis, bit, next_axis, next_bit, place=None):
        place = my_bit(next_bit) if place is None else place
        kept, sent = end_stage(value, line.hold(got), axis, bit, next_axis, place)
        return kept, swap_dp(line.passed(sent), next_bit)

    mid_sent = gate_and_up_back(gate_grad, up_grad, 1, *up_weights, BF16, "mid_sent")
    line.passed(mid_sent[0])
    got_mid = [swap_col(sent) for sent in mid_sent]
    gate_rows = up_rows(line.hold(gate_grad), "gate_rows")
    gate_got = first_stage(gate_rows, levels, 1)
    mid_kept = gate_and_up_back(line.hold(gate_grad), up_grad, 0, *up_weights, F32, "mid_kept")
    *got_mid, kept_near, act_got = together(*got_mid, mid_kept[0], act_got)
    block = (half, features)
    mid_own, to_row, to_z, row_both, z_both = local_call(
        join_core_kernel,
        (kept_near, mid_kept[1], *got_mid),
        [(block, F32)] * 3 + [((quarter, features), BF16)] * 2,
        "join_core",
    )
    via_row = swap_row(row_both)
    via_z = swap_z(z_both)
    line.passed(row_both)
    up_cols = up_rows(line.hold(up_grad), "up_rows")
    up_sent = line.passed(take(up_cols, levels, 1 - xbit))
    via_row, via_z, up_sent = line.hold(via_row, via_z, up_sent)
    to_row, to_z = local_call(
        join_corner_kernel,
        (to_row, to_z, via_row, via_z),
        [(block, BF16), (block, BF16)],
        "join_corner",
    )
    got_row, got_z = swap_row(to_row), swap_z(to_z)
    up_got = swap_dp(up_sent, 1)
    line.passed(to_row)
    act_all = assemble(
        (pair, 2 * ff_part), [(0, 0, activated), (0, ff_part, line.hold(act_got))], "act_all"
    )
    down_rows = product(act_all, grad_all, "tn", BF16, ff_part // 2, name="down_first")
    down_rows = split_rows(down_rows, levels - 1)
    down_sent = line.passed(take(down_rows, levels - 2, 1 - xbit))
    got_row, got_z, down_sent = line.hold(got_row, got_z, down_sent)
    normed_mid_grad, mid_sum, feedforward_part = norm_sums(
        (mid_own, got_row, got_z), stream_mid, inverse_mid, gain_mid
    )
    got_sum = swap_row(line.passed(mid_sum))
    down_got = swap_dp(down_sent, 1)
    got_sum, gate_got = line.hold(got_sum, gate_got)
    stream_mid_grad, branch_low = norm_grad(
        normed_mid_grad, stream_mid, inverse_mid, gain_mid, mid_sum, got_sum, moved_grad, (F32, BF16)
    )
    line.passed(branch_low)
    branch_got = swap_col(branch_low)
    gate_rows, gate_got = late_stage(gate_rows, gate_got, levels, 1, 1, top_bit)
    branch = assemble(
        (group, features), [(0, 0, branch_low), (half, 0, line.hold(branch_got))], "branch"
    )
    attention_sent = product(branch, output_weight, "nt", BF16, query_part, 1 - row, query_part)
    got_attention = swap_row(attention_sent)
    line.passed(attention_sent)

    attention_kept = line.passed(
        product(
            line.hold(branch),
            output_weight,
            "nt",
            F32,
            query_part,
            row,
            query_part,
            name="attention_kept",
        )
    )
    attention_all = assemble(
        (group, 2 * query_part),
        [(0, 0, line.hold(attention)), (0, query_part, attention_other)],
        "attention_all",
    )
    output_rows = product(attention_all, branch, "tn", BF16, query_part, name="output_rows")
    output_rows = split_rows(output_rows, levels)
    output_sent = line.passed(take(output_rows, levels - 2, 1 - zbit))
    output_got = swap_dp(output_sent, 2)
    out_kept, *out_sent = down_product(
        line.hold(act_all), down_own, down_other, own_at, other_at, features // 2
    )
    line.passed(out_kept)
    out_got = [swap_col(sent) for sent in out_sent]
    got_attention, out_kept = line.hold(got_attention, out_kept)
    line.passed(got_attention)
    projected_grad, head_gains = attend_back(
        kept_heads, got_heads, shared, attention_kept, line.hold(got_attention), kv_heads, repeat
    )
    projected_grad, up_got, gate_got, output_got, *out_got = together(
        projected_grad, up_got, gate_got, output_got, *out_got
    )
    projected_other = swap_row(projected_grad)
    line.passed(projected_grad)
    up_cols, up_got = late_stage(up_cols, up_got, levels, 1, 1, top_bit)

    (normed_in,) = local_call(
        normed_in_kernel,
        (x_low, line.hold(inverse_in), gain_in),
        [((group, features), BF16)],
        "normed_in",
    )

    def projection_rows(part, name):
        whole = product(normed_in, part, "tn", BF16, features // 2, name=name)
        whole = split_rows(whole, levels)
        return whole, line.passed(take(whole, levels - 2, 1 - zbit))

    heads_first, heads_sent_own = projection_rows(line.hold(projected_grad), "heads_first")
    in_own = line.passed(heads_backward(line.hold(projected_grad), *projections, row)[0])
    heads_got = swap_dp(heads_sent_own, 2)
    out_near, out_far = local_call(
        out_near_kernel, (out_kept, *line.hold(*out_got)), [(block, F32), (block, BF16)], "out_near"
    )
    layer_z = swap_z(line.passed(out_far))
    projected_other, in_own, down_got = line.hold(projected_other, in_own, down_got)
    line.passed(projected_other)
    in_kept, in_sent = heads_backward(projected_other, *projections, 1 - row, in_own)
    in_got = swap_col(line.passed(in_sent))
    down_rows, down_got = late_stage(down_rows, down_got, levels - 2, 1, 0, top_bit, top_place)
    in_values = (moved_in, inverse_in[:, :half], gain_in)
    normed_in_grad, in_sum, attention_part = norm_sums(
        (in_kept, line.hold(in_got)), *in_values
    )
    got_sum = swap_row(line.passed(in_sum))
    output_rows, output_got = late_stage(
        output_rows, output_got, levels - 2, 2, levels - 2, 1
    )
    heads_second, heads_sent_other = projection_rows(line.hold(projected_other), "heads_second")
    got_sum, up_got, heads_got, heads_sent_other = line.hold(
        got_sum, up_got, heads_got, heads_sent_other
    )
    heads_got_other = swap_dp(heads_sent_other, 2)
    (stream_grad,) = norm_grad(
        normed_in_grad, *in_values, in_sum, got_sum, stream_mid_grad, (BF16,)
    )
    grad_back = exchange(
        line.passed(pack_back(stream_grad, attention_part, feedforward_part, head_gains, count))
    )

    for bit in lower_bits:
        gate_rows, gate_got = late_stage(gate_rows, gate_got, None, None, 1, bit)
        up_cols, up_got = late_stage(up_cols, up_got, None, None, 1, bit)
    shape = gate_rows.shape[1:-1] + (2 * ff_part,)
    side_own, side_sent = local_call(
        side_kernel,
        (gate_rows, up_cols, *line.hold(gate_got, up_got)),
        [(shape, F32), (shape, BF16)],
        "side",
    )
    side_got = swap_row(line.passed(side_sent))
    heads_own, heads_got = late_stage(heads_first, heads_got, levels - 2, 2, levels - 2, 1)
    (layer_out,) = local_call(
        layer_out_kernel, (stream_mid, out_near, line.hold(layer_z)), [(block, BF16)], "layer_out"
    )
    line.passed(layer_out)
    output_got, side_got, heads_got, layer_out = line.hold(
        output_got, side_got, heads_got, layer_out
    )
    line.passed(side_got)
    output_rows, output_got = late_stage(
        output_rows, output_got, None, None, 0, top_bit, top_place
    )
    heads_own, heads_got = late_stage(heads_own, heads_got, None, None, 0, top_bit)
    sent = jnp.stack([pick(part, 1 - zbit, 0).astype(BF16) for part in (side_own, side_got)])
    side_z = swap_z(line.passed(sent))
    grad_back, layer_out = line.hold(grad_back, layer_out)
    line.passed(grad_back)
    out_back = exchange(layer_out)
    heads_got_other, down_got = line.hold(heads_got_other, down_got)
    line.passed(down_got)
    heads_other, heads_got_other = late_stage(
        heads_second, heads_got_other, levels - 2, 2, levels - 2, 1
    )

    def finish(kept, got):
        value = line.passed(add_got(kept, line.hold(got)))
        for bit in lower_bits:
            value = pick(value, my_bit(bit), 0) + swap_dp(
                pick(value, 1 - my_bit(bit), 0).astype(BF16), bit
            ).astype(F32)
        return value

    down_grad = finish(down_rows, down_got)
    heads_other, heads_got_other = late_stage(heads_other, heads_got_other, None, None, 0, top_bit)
    output_weight_grad = finish(output_rows, output_got)
    side_z = line.hold(side_z)

    def up_columns(at):
        columns = slice(at, at + ff_part)
        keep = [pick(part[..., columns], zbit, 0) for part in (side_own, side_got.astype(F32))]
        swapped = side_z[..., columns].astype(F32)
        table = [
            by_half(zbit, near_piece, far_piece)
            for near_piece, far_piece in zip(
                by_half(row, keep[0], keep[1]), by_half(row, swapped[0], swapped[1])
            )
        ]
        return jnp.concatenate(
            [
                table[part][z][:, i * run : (i + 1) * run]
                for part in range(2)
                for i in range(runs)
                for z in range(2)
            ],
            axis=1,
        )

    gate_weight_grad = up_columns(0)
    up_weight_grad = line.passed(up_columns(ff_part))
    heads_grad_own = finish(heads_own, heads_got)
    out_back = line.passed(line.hold(out_back))
    heads_grad_other = finish(heads_other, heads_got_other)

    def head_grad(start, width):
        own = heads_grad_own[:, start : start + width]
        other = heads_grad_other[:, start : start + width]
        return jnp.concatenate(by_half(row, own, other), axis=1)

    query_weight_grad = head_grad(0, query_part)
    key_weight_grad = head_grad(query_part, key_part)
    value_weight_grad = head_grad(query_part + key_part, key_part)

    back = grad_back.reshape(count, -1, features).astype(F32)
    grad_back = back[:, :-EXTRA].reshape(half, features)
    totals = jnp.sum(back[:, -EXTRA:], axis=0)
    out_back = out_back.astype(F32)
    gains = jnp.concatenate([totals[i] + totals[i + 4] for i in range(3)])[None]
    gains = gains + swap_col(gains)
    gain_low, gain_high = (part[0] for part in by_half(row, gains, swap_row(gains)))
    attention_total = jnp.concatenate([gain_low[:features], gain_high[:features]])
    feedforward_total = jnp.concatenate(
        [gain_low[features : 2 * features], gain_high[features : 2 * features]]
    )
    head_totals = (gain_low + gain_high)[2 * features :]
    return (
        out_back,
        grad_back,
        attention_total,
        query_weight_grad,
        key_weight_grad,
        value_weight_grad,
        head_totals[:HEAD_SIZE],
        head_totals[HEAD_SIZE : 2 * HEAD_SIZE],
        output_weight_grad,
        feedforward_total,
        gate_weight_grad,
        up_weight_grad,
        down_grad,
    )


def solution(mesh):
    placed = (
        P(("dp", "col"), "row"),
        P(("dp", "col"), "row"),
        P("dp", None),
        P("dp", None),
        P("row"),
        P("row", "col"),
        P("row", "col"),
        P("row", "col"),
        P(),
        P(),
        P("col", "row"),
        P("row"),
        P("row", "col"),
        P("row", "col"),
        P("col", "row"),
    )
    return jax.shard_map(
        shards,
        mesh=mesh,
        in_specs=placed,
        out_specs=(
            P(("dp", "col"), "row"),
            P(("dp", "col"), "row"),
            P(),
            P(("row", "dp"), "col"),
            P(("row", "dp"), "col"),
            P(("row", "dp"), "col"),
            P(),
            P(),
            P(("col", "dp"), "row"),
            P(),
            P(("row", "dp"), "col"),
            P(("row", "dp"), "col"),
            P(("col", "dp"), "row"),
        ),
        check_vma=False,
    )
```

```python
import math

import jax
import jax.numpy as jnp
from jax import lax
from jax.experimental import pallas as pl
from jax.experimental.pallas import tpu as pltpu
from jax.sharding import PartitionSpec as P

D = 2048
HEAD_SIZE = 128
EPSILON = 1e-06
ROPE_BASE = 1000000.0
NEGATIVE = -1e30
EXTRA = 8
VMEM_LIMIT = 28 << 20
BF16 = jnp.bfloat16
F32 = jnp.float32


def dot_nn(left, right):
    return jnp.dot(left, right, preferred_element_type=F32)


def dot_nt(left, right):
    return lax.dot_general(left, right, (((1,), (1,)), ((), ())), preferred_element_type=F32)


def dot_tn(left, right):
    return lax.dot_general(left, right, (((0,), (0,)), ((), ())), preferred_element_type=F32)


def swap_row(value):
    return lax.ppermute(value, "row", [(0, 1), (1, 0)])


def swap_col(value):
    return lax.ppermute(value, "col", [(0, 1), (1, 0)])


def swap_dp(value, bit):
    count = lax.axis_size("dp")
    return lax.ppermute(value, "dp", [(i, i ^ bit) for i in range(count)])


def swap_z(value):
    return swap_dp(value, 2)


def rotary_tables(position):
    half = HEAD_SIZE // 2
    frequency = ROPE_BASE ** (-2.0 * jnp.arange(half, dtype=F32) / HEAD_SIZE)
    angles = position.astype(F32)[:, None] * frequency[None, :]
    cosine, sine = jnp.cos(angles), jnp.sin(angles)
    return jnp.concatenate([cosine, cosine], axis=1), jnp.concatenate([-sine, sine], axis=1)


def pick(value, index, axis):
    return lax.dynamic_index_in_dim(value, index, axis, keepdims=False)


def high_bits(count):
    bits, bit = [], 4
    while bit < count:
        bits.append(bit)
        bit *= 2
    return bits


def split_rows(value, levels):
    return value.reshape((2,) * levels + (value.shape[0] >> levels,) + value.shape[1:])


def exchange(value):
    return lax.all_to_all(value, "dp", split_axis=0, concat_axis=0, tiled=True)


def after(value, *earlier):
    return lax.optimization_barrier((value,) + earlier)[0]


def together(*values):
    return lax.optimization_barrier(values)


class Line:
    def __init__(self, value):
        self.last = value

    def hold(self, *values):
        held = together(*values, self.last)[:-1]
        return held[0] if len(held) == 1 else held

    def passed(self, value):
        self.last = value
        return value


def by_half(index, own, other):
    first = index == 0
    return jnp.where(first, own, other), jnp.where(first, other, own)


WINDOWS = {
    "heads_kept": 6.0,
    "attend": 2.0,
    "out_own": 3.0,
    "act_kept": 3.0,
    "gate_and_up": 3.0,
    "mid_sent": 3.0,
    "mid_kept": 1.5,
    "up_rows": 2.5,
    "down_first": 3.0,
    "attention_kept": 3.5,
    "attend_back": 2.0,
    "normed_in": 6.5,
    "heads_second": 2.0,
}


def light(name):
    amount = WINDOWS.get(name, 0.05) * 1.0
    return pl.CostEstimate(
        flops=int(amount * 1.15e9), bytes_accessed=int(amount * 3.69e6), transcendentals=0
    )


def params(grid_axes=1):
    return pltpu.CompilerParams(vmem_limit_bytes=VMEM_LIMIT)


def scalars(*values):
    return jnp.stack([jnp.asarray(v, jnp.int32) for v in values])


def lanes_of(sums):
    return jnp.broadcast_to(sums, (sums.shape[0], HEAD_SIZE)).T[:8]


def column_of(lanes):
    return lanes.T[:, :1]


def local_call(kernel, inputs, outputs, name):
    return pl.pallas_call(
        kernel,
        out_shape=[jax.ShapeDtypeStruct(shape, dtype) for shape, dtype in outputs],
        compiler_params=params(),
        cost_estimate=light(name),
        name=name,
    )(*inputs)


def grid_call(kernel, grid, picks, inputs, in_specs, out_specs, outputs, name):
    return pl.pallas_call(
        kernel,
        grid_spec=pltpu.PrefetchScalarGridSpec(
            num_scalar_prefetch=1, grid=(grid,), in_specs=in_specs, out_specs=out_specs
        ),
        out_shape=[jax.ShapeDtypeStruct(shape, dtype) for shape, dtype in outputs],
        compiler_params=params(),
        cost_estimate=light(name),
        name=name,
    )(picks, *inputs)


def assemble(shape, pieces, name):
    def kernel(*refs):
        for (first, column, piece), ref in zip(pieces, refs):
            rows, columns = piece.shape
            refs[-1][first : first + rows, column : column + columns] = ref[...]

    values = [piece for _, _, piece in pieces]
    return local_call(kernel, values, [(shape, values[0].dtype)], name)[0]


def product(
    left, right, kind, dtype, tile, part=0, size=None, block=0, rows=None, name=None
):
    contract = {"nn": ((1,), (0,)), "nt": ((1,), (1,)), "tn": ((0,), (0,))}[kind]
    size = right.shape[0] if size is None else size
    rows = left.shape[0] if rows is None else rows
    if kind == "tn":
        shape, steps = (left.shape[1], right.shape[1]), left.shape[1] // tile
        specs = [
            pl.BlockSpec((rows, tile), lambda j, s: (block, j)),
            pl.BlockSpec((size, right.shape[1]), lambda j, s: (s[0], 0)),
        ]
        out = pl.BlockSpec((tile, shape[1]), lambda j, s: (j, 0))
    else:
        width = right.shape[1] if kind == "nn" else size
        shape, steps = (rows, width), width // tile
        if kind == "nn":
            right_spec = pl.BlockSpec((size, tile), lambda j, s: (s[0], j))
        else:
            right_spec = pl.BlockSpec(
                (tile, right.shape[1]), lambda j, s: (s[0] * (size // tile) + j, 0)
            )
        specs = [pl.BlockSpec((rows, left.shape[1]), lambda j, s: (block, 0)), right_spec]
        out = pl.BlockSpec((rows, tile), lambda j, s: (0, j))

    def kernel(picks, left_ref, right_ref, out_ref):
        out_ref[...] = lax.dot_general(
            left_ref[...], right_ref[...], (contract, ((), ())), preferred_element_type=F32
        ).astype(out_ref.dtype)

    return grid_call(
        kernel,
        steps,
        scalars(part),
        (left, right),
        specs,
        [out],
        [(shape, dtype)],
        name or "product_" + kind,
    )[0]


def product_onto(left, right, part, size, own, tile, name):
    rows, width = own.shape
    half = rows // 2

    def kernel(picks, left_ref, right_ref, own_ref, kept_ref, sent_ref):
        total = own_ref[...] + dot_nn(left_ref[...], right_ref[...])
        kept_ref[...] = total[:half]
        sent_ref[...] = total[half:].astype(BF16)

    return grid_call(
        kernel,
        width // tile,
        scalars(part),
        (left, right, own),
        [
            pl.BlockSpec(left.shape, lambda j, s: (0, 0)),
            pl.BlockSpec((size, tile), lambda j, s: (s[0], j)),
            pl.BlockSpec((rows, tile), lambda j, s: (0, j)),
        ],
        [pl.BlockSpec((half, tile), lambda j, s: (0, j))] * 2,
        [((half, width), F32), ((half, width), BF16)],
        name,
    )


def down_product(act_all, down_own, down_other, own_at, other_at, tile):
    rows, width = act_all.shape
    half, size, features = rows // 2, width // 2, down_own.shape[1]
    quarter = half // 2

    def kernel(picks, act_ref, own_ref, other_ref, kept_ref, near_ref, far_ref):
        total = dot_nn(act_ref[:, :size], own_ref[...]) + dot_nn(act_ref[:, size:], other_ref[...])
        kept_ref[...] = total[:half]
        near_ref[...] = total[half : half + quarter].astype(BF16)
        far_ref[...] = total[half + quarter :].astype(BF16)

    return grid_call(
        kernel,
        features // tile,
        scalars(own_at, other_at),
        (act_all, down_own, down_other),
        [
            pl.BlockSpec(act_all.shape, lambda j, s: (0, 0)),
            pl.BlockSpec((size, tile), lambda j, s: (s[0], j)),
            pl.BlockSpec((size, tile), lambda j, s: (s[1], j)),
        ],
        [pl.BlockSpec((half, tile), lambda j, s: (0, j))]
        + [pl.BlockSpec((quarter, tile), lambda j, s: (0, j))] * 2,
        [((half, features), F32), ((quarter, features), BF16), ((quarter, features), BF16)],
        "down_proj",
    )


def heads_forward(scaled, query_weight, key_weight, value_weight, part, dtype, name):
    group, features = scaled.shape
    query_part, tile = query_weight.shape[1] // 2, key_weight.shape[1] // 2
    steps = query_part // tile

    def kernel(picks, x_ref, query_ref, key_ref, value_ref, out_ref):
        step = pl.program_id(0)
        for condition, ref in (
            (step < steps, query_ref),
            (step == steps, key_ref),
            (step == steps + 1, value_ref),
        ):

            @pl.when(condition)
            def _():
                out_ref[...] = dot_nn(x_ref[...], ref[...]).astype(out_ref.dtype)

    return grid_call(
        kernel,
        steps + 2,
        scalars(part),
        (scaled, query_weight, key_weight, value_weight),
        [
            pl.BlockSpec((group, features), lambda j, s: (0, 0)),
            pl.BlockSpec(
                (features, tile), lambda j, s: (0, s[0] * steps + jnp.minimum(j, steps - 1))
            ),
            pl.BlockSpec((features, tile), lambda j, s: (0, s[0])),
            pl.BlockSpec((features, tile), lambda j, s: (0, s[0])),
        ],
        [pl.BlockSpec((group, tile), lambda j, s: (0, j))],
        [((group, query_part + 2 * tile), dtype)],
        name,
    )[0]


def heads_backward(grads, query_weight, key_weight, value_weight, part, own=None):
    group = grads.shape[0]
    half = group // 2
    features = query_weight.shape[0]
    query_part, key_part = query_weight.shape[1] // 2, key_weight.shape[1] // 2
    tile = features // 2

    def kernel(picks, grads_ref, query_ref, key_ref, value_ref, *refs):
        total = dot_nt(grads_ref[:, :query_part], query_ref[...])
        total += dot_nt(grads_ref[:, query_part : query_part + key_part], key_ref[...])
        total += dot_nt(grads_ref[:, query_part + key_part :], value_ref[...])
        if own is None:
            refs[0][...] = total
        else:
            total += refs[0][...]
            refs[1][...] = total[:half]
            refs[2][...] = total[half:].astype(BF16)

    whole = pl.BlockSpec((group, tile), lambda j, s: (0, j))
    split = pl.BlockSpec((half, tile), lambda j, s: (0, j))
    outputs = [((group, features), F32)]
    if own is not None:
        outputs = [((half, features), F32), ((half, features), BF16)]
    return grid_call(
        kernel,
        2,
        scalars(part),
        (grads, query_weight, key_weight, value_weight) + (() if own is None else (own,)),
        [
            pl.BlockSpec(grads.shape, lambda j, s: (0, 0)),
            pl.BlockSpec((tile, query_part), lambda j, s: (j, s[0])),
            pl.BlockSpec((tile, key_part), lambda j, s: (j, s[0])),
            pl.BlockSpec((tile, key_part), lambda j, s: (j, s[0])),
        ]
        + ([] if own is None else [whole]),
        [whole] if own is None else [split, split],
        outputs,
        "heads_backward",
    )


def up_kernel(picks, mid_ref, gate_ref, up_ref, *refs):
    parts = 2
    gate_parts, up_parts = refs[:parts], refs[parts : 2 * parts]
    kept_ref, *got_refs = refs[2 * parts : -3]
    gate_grad_ref, up_grad_ref, act_ref = refs[-3:]
    features = gate_ref.shape[0]
    share = gate_parts[0].shape[0]

    def columns(own_ref, part_refs):
        total = dot_nn(mid_ref[:, :features], own_ref[...])
        for i, ref in enumerate(part_refs):
            at = pl.multiple_of(features + picks[1 + i] * share, share)
            total += dot_nn(mid_ref[:, pl.ds(at, share)], ref[...])
        return total

    gate = columns(gate_ref, gate_parts)
    up = columns(up_ref, up_parts)
    got = jnp.concatenate([ref[...] for ref in got_refs], axis=0)
    act_grad = kept_ref[...] + got.astype(F32)
    sigmoid = jax.nn.sigmoid(gate)
    silu = gate * sigmoid
    act_ref[...] = (silu * up).astype(BF16)
    gate_grad_ref[...] = (act_grad * up * sigmoid * (1.0 + gate * (1.0 - sigmoid))).astype(BF16)
    up_grad_ref[...] = (act_grad * silu).astype(BF16)


def gate_and_up(mid, gate, up, base, pieces, places, kept, got):
    rows = mid.shape[0]
    features = gate.shape[0]
    width = kept.shape[1]
    tile = width // 3
    share = pieces[0][0].shape[0]

    def columns(height, first):
        return pl.BlockSpec((height, tile), lambda j, s: (0, first + j))

    own = pl.BlockSpec((features, tile), lambda j, s: (0, 3 * s[0] + j))
    return grid_call(
        up_kernel,
        3,
        scalars(base, *places),
        (mid, gate, up, *pieces[0], *pieces[1], kept, *got),
        [pl.BlockSpec(mid.shape, lambda j, s: (0, 0)), own, own]
        + [columns(share, 0)] * (2 * len(places))
        + [columns(rows, 0)]
        + [columns(g.shape[0], 0) for g in got],
        [columns(rows, 0)] * 3,
        [((rows, width), BF16)] * 3,
        "gate_and_up",
    )


def up_back_kernel(picks, gate_grad_ref, up_grad_ref, gate_ref, up_ref, *refs):
    *pieces, near_ref, far_ref = refs
    count = len(pieces) // 2
    features = gate_ref.shape[0]
    share = pieces[0].shape[0]
    gate_grad, up_grad = gate_grad_ref[...], up_grad_ref[...]
    for i in range(features // share):
        at = slice(i * share, (i + 1) * share)
        total = dot_nt(gate_grad, gate_ref[at, :]) + dot_nt(up_grad, up_ref[at, :])
        near_ref[:, at] = total.astype(near_ref.dtype)
    for i in range(count):
        total = dot_nt(gate_grad, pieces[i][...]) + dot_nt(up_grad, pieces[count + i][...])
        at = pl.multiple_of(picks[1 + i] * share, share)
        far_ref[:, pl.ds(at, share)] = total.astype(far_ref.dtype)


def gate_and_up_back(gate_grad, up_grad, block, gate, up, base, pieces, places, dtype, name):
    rows = gate_grad.shape[0] // 2
    width = gate_grad.shape[1]
    features = gate.shape[0]
    grads = pl.BlockSpec((rows, width), lambda j, s: (block, 0))
    own = pl.BlockSpec((features, width), lambda j, s: (0, s[0]))
    pieces = (*pieces[0], *pieces[1])
    piece = pl.BlockSpec(pieces[0].shape, lambda j, s: (0, 0))
    shape = (rows, features)
    return grid_call(
        up_back_kernel,
        1,
        scalars(base, *places),
        (gate_grad, up_grad, gate, up, *pieces),
        [grads, grads, own, own] + [piece] * len(pieces),
        [pl.BlockSpec(shape, lambda j, s: (0, 0))] * 2,
        [(shape, dtype)] * 2,
        name,
    )


def in_place(weight):
    return pltpu.with_memory_space_constraint(weight, pltpu.MemorySpace.HBM)


def my_bit(bit):
    return (lax.axis_index("dp") // bit) % 2


def view(shape, columns=None, **at):
    at = {int(axis[1:]): place for axis, place in at.items()}
    parts, part = columns or (1, 0)
    last = len(shape) - 1
    block = tuple(
        None if axis in at else length // (parts if axis == last else 1)
        for axis, length in enumerate(shape)
    )
    return pl.BlockSpec(
        block,
        lambda j, s: tuple(
            s[at[axis]] if axis in at else (part if axis == last else 0)
            for axis in range(len(shape))
        ),
    )


def without(shape, *axes):
    return tuple(length for axis, length in enumerate(shape) if axis not in axes)


def take(value, axis, index, columns=None):
    shape = without(value.shape, axis)
    shape = shape[:-1] + (shape[-1] // (columns or (1, 0))[0],)

    def kernel(picks, in_ref, out_ref):
        out_ref[...] = in_ref[...].astype(BF16)

    return grid_call(
        kernel,
        1,
        scalars(index),
        (value,),
        [view(value.shape, columns, **{f"a{axis}": 0})],
        [view(shape)],
        [(shape, BF16)],
        "take",
    )[0]


def start_stage(value, axis, bit):
    return swap_dp(take(value, axis, 1 - my_bit(bit)), bit)


def end_stage(value, got, axis, bit, next_axis=None, next_index=None, columns=None):
    joined = got.shape
    side = {} if axis is None else {f"a{axis}": 0}
    mine = 0 if axis is None else my_bit(bit)
    if next_axis is None:

        def kernel(picks, value_ref, got_ref, out_ref):
            out_ref[...] = value_ref[...].astype(F32) + got_ref[...].astype(F32)

        return grid_call(
            kernel,
            1,
            scalars(mine),
            (value, got),
            [view(value.shape, **side), view(joined)],
            [view(joined)],
            [(joined, F32)],
            "join",
        )[0]
    shape = without(joined, next_axis)
    behind = next_axis + (1 if axis is not None and next_axis >= axis else 0)

    def kernel(picks, keep_ref, keep_got, send_ref, send_got, kept_ref, sent_ref):
        kept_ref[...] = keep_ref[...].astype(F32) + keep_got[...].astype(F32)
        sent_ref[...] = (send_ref[...].astype(F32) + send_got[...].astype(F32)).astype(BF16)

    return grid_call(
        kernel,
        1,
        scalars(mine, next_index, 1 - next_index),
        (value, got, value, got),
        [
            view(value.shape, columns, **side, **{f"a{behind}": 1}),
            view(joined, **{f"a{next_axis}": 1}),
            view(value.shape, columns, **side, **{f"a{behind}": 2}),
            view(joined, **{f"a{next_axis}": 2}),
        ],
        [view(shape)] * 2,
        [(shape, F32), (shape, BF16)],
        "join_and_split",
    )


def add_got(kept, got):
    def kernel(kept_ref, got_ref, out_ref):
        out_ref[...] = kept_ref[...].astype(F32) + got_ref[...].astype(F32)

    return local_call(kernel, (kept, got), [(kept.shape, F32)], "add_got")[0]


def split_top(own, other, row):
    mine = my_bit(lax.axis_size("dp") // 2) == row

    def kernel(picks, own_ref, other_ref, kept_ref, sent_ref):
        for first, second, flag in ((own_ref, other_ref, 1), (other_ref, own_ref, 0)):

            @pl.when(picks[0] == flag)
            def _():
                kept_ref[...] = first[...].astype(F32)
                sent_ref[...] = second[...].astype(BF16)

    spec = view(own.shape)
    return grid_call(
        kernel,
        1,
        scalars(mine),
        (own, other),
        [spec, spec],
        [spec, spec],
        [(own.shape, F32), (own.shape, BF16)],
        "split_top",
    )


def join_core_kernel(
    near_ref, far_ref, got_near, got_far, own_ref, row_ref, z_ref, row_both_ref, z_both_ref
):
    half = own_ref.shape[0]
    quarter = half // 2
    near = near_ref[...] + got_near[...].astype(F32)
    far = far_ref[...] + got_far[...].astype(F32)
    own_ref[...] = near[:half]
    row_ref[...] = far[:half]
    z_ref[...] = near[half:]
    row_both_ref[...] = far[half : half + quarter].astype(BF16)
    z_both_ref[...] = far[half + quarter :].astype(BF16)


def join_corner_kernel(row_ref, z_ref, via_row_ref, via_z_ref, to_row_ref, to_z_ref):
    quarter = via_row_ref.shape[0]
    to_row_ref[:quarter, :] = row_ref[:quarter, :].astype(BF16)
    to_row_ref[quarter:, :] = (row_ref[quarter:, :] + via_z_ref[...].astype(F32)).astype(BF16)
    to_z_ref[:quarter, :] = (z_ref[:quarter, :] + via_row_ref[...].astype(F32)).astype(BF16)
    to_z_ref[quarter:, :] = z_ref[quarter:, :].astype(BF16)


def norm_sums_kernel(*refs):
    parts = refs[:-6]
    base_ref, inverse_ref, gain_ref, grad_ref, sums_ref, gain_grad_ref = refs[-6:]
    grad = sum(part[...].astype(F32) for part in parts)
    unit = base_ref[...].astype(F32) * column_of(inverse_ref[...])
    along = grad * unit
    grad_ref[...] = grad
    sums_ref[...] = lanes_of(jnp.sum(along * gain_ref[...], axis=1, keepdims=True))
    gain_grad_ref[...] = jnp.sum(along, axis=0, keepdims=True)


def norm_sums(parts, base, inverse, gain):
    rows, features = base.shape
    return local_call(
        norm_sums_kernel,
        (*parts, base, inverse, gain),
        [((rows, features), F32), ((8, rows), F32), ((1, features), F32)],
        "norm_sums",
    )


def norm_grad_kernel(
    grad_ref, base_ref, inverse_ref, gain_ref, sums_ref, got_sums_ref, rest_ref, *out_refs
):
    inverse = column_of(inverse_ref[...])
    unit = base_ref[...].astype(F32) * inverse
    mean = column_of(sums_ref[...] + got_sums_ref[...]) * (1.0 / D)
    out = rest_ref[...].astype(F32) + inverse * (grad_ref[...] * gain_ref[...] - unit * mean)
    for out_ref in out_refs:
        out_ref[...] = out.astype(out_ref.dtype)


def norm_grad(grad, base, inverse, gain, sums, got_sums, rest, dtypes):
    return local_call(
        norm_grad_kernel,
        (grad, base, inverse, gain, sums, got_sums, rest),
        [(grad.shape, dtype) for dtype in dtypes],
        "norm_grad",
    )


def middle_kernel(x_ref, part_ref, got_ref, mid_ref, square_ref):
    mid = x_ref[...].astype(F32) + part_ref[...] + got_ref[...].astype(F32)
    mid_ref[...] = mid
    square_ref[...] = lanes_of(jnp.sum(mid * mid, axis=1, keepdims=True))


def normed_kernel(mid_ref, square_ref, got_ref, gain_ref, normed_ref, inverse_ref):
    inverse = lax.rsqrt((square_ref[...] + got_ref[...]) * (1.0 / D) + EPSILON)
    inverse_ref[...] = inverse
    unit = mid_ref[...].astype(F32) * column_of(inverse)
    normed_ref[...] = (unit * gain_ref[...]).astype(BF16)


def scaled_kernel(own_ref, got_ref, gain_ref, x_ref, scaled_ref, square_ref):
    half = own_ref.shape[0]
    for first, ref in ((0, own_ref), (half, got_ref)):
        at = slice(first, first + half)
        values = ref[...].astype(F32)
        x_ref[at, :] = ref[...]
        scaled_ref[at, :] = (values * gain_ref[...]).astype(BF16)
        square_ref[:, at] = lanes_of(jnp.sum(values * values, axis=1, keepdims=True))


def normed_in_kernel(x_ref, inverse_ref, gain_ref, normed_ref):
    unit = x_ref[...].astype(F32) * column_of(inverse_ref[...])
    normed_ref[...] = (unit * gain_ref[...]).astype(BF16)


def block_of(weight, block_row, block_column, shape):
    def kernel(picks, in_ref, out_ref):
        out_ref[...] = in_ref[...]

    return grid_call(
        kernel,
        1,
        scalars(block_row, block_column),
        (weight,),
        [pl.BlockSpec(shape, lambda j, s: (s[0], s[1]))],
        [pl.BlockSpec(shape, lambda j, s: (0, 0))],
        [(shape, BF16)],
        "block_of",
    )[0]


def side_kernel(*refs):
    kept_ref, sent_ref = refs[-2:]
    parts = (len(refs) - 2) // 2
    width = refs[0].shape[-1]
    for i in range(parts):
        total = refs[i][...].astype(F32) + refs[parts + i][...].astype(F32)
        at = slice(i * width, (i + 1) * width)
        kept_ref[:, :, at] = total[0]
        sent_ref[:, :, at] = total[1].astype(BF16)


def pack_back(grad, attention_part, feedforward_part, head_gains, count):
    rows, features = grad.shape
    share = rows // count

    def kernel(grad_ref, attention_ref, feedforward_ref, heads_ref, out_ref):
        rest = jnp.zeros((1, features - 2 * HEAD_SIZE), F32)
        heads = jnp.concatenate([heads_ref[:1, :], heads_ref[1:, :], rest], axis=1)
        values = jnp.concatenate([attention_ref[...], feedforward_ref[...], heads, heads], axis=0)
        high = values.astype(BF16)
        low = (values - high.astype(F32)).astype(BF16)
        extra = jnp.concatenate([high.astype(F32), low.astype(F32)], axis=0).astype(BF16)
        for i in range(count):
            out_ref[i, :share, :] = grad_ref[i * share : (i + 1) * share, :]
            out_ref[i, share:, :] = extra

    return local_call(
        kernel,
        (grad, attention_part, feedforward_part, head_gains),
        [((count, share + EXTRA, features), BF16)],
        "pack_back",
    )[0]


def layer_out_kernel(mid_ref, kept_ref, got_ref, out_ref):
    out_ref[...] = (mid_ref[...] + kept_ref[...] + got_ref[...].astype(F32)).astype(BF16)


def out_near_kernel(kept_ref, got_near, got_far, near_ref, far_ref):
    half = near_ref.shape[0]
    near_ref[...] = kept_ref[:half, :] + got_near[...].astype(F32)
    far_ref[...] = (kept_ref[half:, :] + got_far[...].astype(F32)).astype(BF16)


def turn(values, cosine, sine):
    return values * cosine + pltpu.roll(values, HEAD_SIZE // 2, 1) * sine


def unit_of(raw):
    inverse = lax.rsqrt(jnp.mean(raw * raw, axis=-1, keepdims=True) + EPSILON)
    return raw * inverse, inverse


def scores_to_prob(query_rot, key_rot, allowed):
    scores = dot_nt(query_rot, key_rot) * (1.0 / math.sqrt(HEAD_SIZE))
    scores = jnp.where(allowed, scores, NEGATIVE)
    exps = jnp.exp(scores - jnp.max(scores, axis=-1, keepdims=True))
    return exps * (1.0 / jnp.sum(exps, axis=-1, keepdims=True))


def head_inputs(own, got, inverse_in, width):
    raw = (own[...] + got[...].astype(F32)) * inverse_in
    return [raw[:, i * HEAD_SIZE : (i + 1) * HEAD_SIZE] for i in range(width // HEAD_SIZE)]


def attend_kernel(
    query_own, query_got, key_own, key_got, value_own, value_got, inverse_ref, cosine_ref,
    sine_ref, slot_ref, start_ref, across_ref, query_gain_ref, key_gain_ref, out_ref,
):
    inverse_in = column_of(inverse_ref[...])
    cosine, sine = cosine_ref[...], sine_ref[...]
    across = across_ref[...]
    (key_raw,) = head_inputs(key_own, key_got, inverse_in, HEAD_SIZE)
    (value,) = head_inputs(value_own, value_got, inverse_in, HEAD_SIZE)
    key_rot = turn(unit_of(key_raw)[0] * key_gain_ref[...], cosine, sine).astype(BF16)
    value = value.astype(BF16)
    slots, first = column_of(slot_ref[...]), column_of(start_ref[...])
    rows = out_ref.shape[0] // 2

    for block in range(2):
        at = slice(block * rows, (block + 1) * rows)
        allowed = (across <= slots[at]) & (across >= first[at])
        for i in range(query_own.shape[1] // HEAD_SIZE):
            head = slice(i * HEAD_SIZE, (i + 1) * HEAD_SIZE)
            raw = (query_own[at, head] + query_got[at, head].astype(F32)) * inverse_in[at]
            pre = unit_of(raw)[0] * query_gain_ref[...]
            query_rot = turn(pre, cosine_ref[at, :], sine_ref[at, :]).astype(BF16)
            prob = scores_to_prob(query_rot, key_rot, allowed).astype(BF16)
            out_ref[at, head] = dot_nn(prob, value).astype(BF16)


def attend_back_kernel(
    query_own, query_got, key_own, key_got, value_own, value_got, inverse_ref, cosine_ref,
    sine_ref, slot_ref, start_ref, across_ref, query_gain_ref, key_gain_ref, grad_own, grad_got,
    out_ref, gain_ref,
):
    step = pl.program_id(0)
    repeat = query_own.shape[1] // HEAD_SIZE
    kv_heads = out_ref.shape[1] // (query_own.shape[1] + 2 * HEAD_SIZE)
    scale = 1.0 / math.sqrt(HEAD_SIZE)
    inverse_in = column_of(inverse_ref[...])
    cosine, sine = cosine_ref[...], sine_ref[...]
    across = across_ref[...]
    allowed = (across <= column_of(slot_ref[...])) & (across >= column_of(start_ref[...]))
    query_gain, key_gain = query_gain_ref[...], key_gain_ref[...]

    @pl.when(step == 0)
    def _():
        gain_ref[...] = jnp.zeros_like(gain_ref)

    (key_raw,) = head_inputs(key_own, key_got, inverse_in, HEAD_SIZE)
    (value,) = head_inputs(value_own, value_got, inverse_in, HEAD_SIZE)
    key_unit, key_inverse = unit_of(key_raw)
    key_rot = turn(key_unit * key_gain, cosine, sine).astype(BF16)
    value = value.astype(BF16)

    def norm_back(rot_grad, unit, inverse, gain, at):
        pre = rot_grad * cosine - pltpu.roll(rot_grad, HEAD_SIZE // 2, 1) * sine
        gain_ref[at : at + 1, :] += jnp.sum(pre * unit, axis=0, keepdims=True)
        scaled = pre * gain
        return inverse * (scaled - unit * jnp.mean(scaled * unit, axis=-1, keepdims=True))

    key_grad = jnp.zeros(key_raw.shape, F32)
    value_grad = jnp.zeros(key_raw.shape, F32)
    for i, query_raw in enumerate(
        head_inputs(query_own, query_got, inverse_in, query_own.shape[1])
    ):
        at = slice(i * HEAD_SIZE, (i + 1) * HEAD_SIZE)
        query_unit, query_inverse = unit_of(query_raw)
        query_rot = turn(query_unit * query_gain, cosine, sine).astype(BF16)
        prob = scores_to_prob(query_rot, key_rot, allowed)
        grad_out = (grad_own[:, at] + grad_got[:, at].astype(F32)).astype(BF16)
        prob_grad = dot_nt(grad_out, value)
        centre = jnp.sum(prob * prob_grad, axis=-1, keepdims=True)
        score_grad = (prob * (prob_grad - centre)).astype(BF16)
        value_grad += dot_tn(prob.astype(BF16), grad_out)
        key_grad += dot_tn(score_grad, query_rot)
        query_grad = norm_back(
            dot_nn(score_grad, key_rot) * scale, query_unit, query_inverse, query_gain, 0
        )
        column = pl.multiple_of((step * repeat + i) * HEAD_SIZE, HEAD_SIZE)
        out_ref[:, pl.ds(column, HEAD_SIZE)] = query_grad.astype(BF16)
    key_grad = norm_back(key_grad * scale, key_unit, key_inverse, key_gain, 1)
    column = pl.multiple_of((kv_heads * repeat + step) * HEAD_SIZE, HEAD_SIZE)
    out_ref[:, pl.ds(column, HEAD_SIZE)] = key_grad.astype(BF16)
    column = pl.multiple_of((kv_heads * (repeat + 1) + step) * HEAD_SIZE, HEAD_SIZE)
    out_ref[:, pl.ds(column, HEAD_SIZE)] = value_grad.astype(BF16)


def attention_specs(group, kv_heads, repeat):
    def block(width, first):
        return pl.BlockSpec((group, width), lambda j: (0, first + j))

    def whole(rows, columns):
        return pl.BlockSpec((rows, columns), lambda j: (0, 0))

    query = block(repeat * HEAD_SIZE, 0)
    key = block(HEAD_SIZE, kv_heads * repeat)
    value = block(HEAD_SIZE, kv_heads * (repeat + 1))
    return [query, query, key, key, value, value] + [
        whole(8, group),
        whole(group, HEAD_SIZE),
        whole(group, HEAD_SIZE),
        whole(8, group),
        whole(8, group),
        whole(1, group),
        whole(1, HEAD_SIZE),
        whole(1, HEAD_SIZE),
    ]


def attend(own, got, shared, kv_heads, repeat):
    group = own.shape[0]
    width = kv_heads * repeat * HEAD_SIZE
    return pl.pallas_call(
        attend_kernel,
        grid=(kv_heads,),
        in_specs=attention_specs(group, kv_heads, repeat),
        out_specs=pl.BlockSpec((group, repeat * HEAD_SIZE), lambda j: (0, j)),
        out_shape=jax.ShapeDtypeStruct((group, width), BF16),
        compiler_params=pltpu.CompilerParams(vmem_limit_bytes=VMEM_LIMIT),
        cost_estimate=light("attend"),
        name="attend",
    )(own, got, own, got, own, got, *shared)


def attend_back(own, got, shared, grad_own, grad_got, kv_heads, repeat):
    group, width = own.shape
    grad_block = pl.BlockSpec((group, repeat * HEAD_SIZE), lambda j: (0, j))
    return pl.pallas_call(
        attend_back_kernel,
        grid=(kv_heads,),
        in_specs=attention_specs(group, kv_heads, repeat) + [grad_block, grad_block],
        out_specs=[
            pl.BlockSpec((group, width), lambda j: (0, 0)),
            pl.BlockSpec((2, HEAD_SIZE), lambda j: (0, 0)),
        ],
        out_shape=[
            jax.ShapeDtypeStruct((group, width), BF16),
            jax.ShapeDtypeStruct((2, HEAD_SIZE), F32),
        ],
        compiler_params=pltpu.CompilerParams(vmem_limit_bytes=VMEM_LIMIT),
        cost_estimate=light("attend_back"),
        name="attend_back",
    )(own, got, own, got, own, got, *shared, grad_own, grad_got)

def shards(
    tokens,
    cotangent,
    seq_lengths,
    balance_order,
    attention_gain,
    query_weight,
    key_weight,
    value_projection,
    query_gain,
    key_norm_gain,
    output_weight,
    feedforward_gain,
    gate_weight,
    up_weight,
    down_weight,
):
    count = lax.axis_size("dp")
    levels = count.bit_length() - 1
    row = lax.axis_index("row")
    col = lax.axis_index("col")
    xbit, zbit = my_bit(1), my_bit(2)
    half = tokens.shape[0]
    quarter = half // 2
    group = 2 * half
    pair = 2 * group
    features = tokens.shape[1]
    query_part = query_weight.shape[1] // 2
    key_part = key_weight.shape[1] // 2
    heads = query_part // HEAD_SIZE
    kv_heads = key_part // HEAD_SIZE
    repeat = heads // kv_heads
    ff_half = gate_weight.shape[1]
    runs = count // 8
    projections = tuple(map(in_place, (query_weight, key_weight, value_projection)))
    output_weight = in_place(output_weight)
    if runs == 1:
        gate_weight, up_weight, down_weight = map(in_place, (gate_weight, up_weight, down_weight))
    run = 2 * ff_half // count
    ff_part = ff_half // 4
    all_bits = high_bits(count)[::-1]

    def ff_block(weight, part, axis):
        if runs == 1:
            return weight, part * 2 + zbit
        pieces = [
            lax.dynamic_slice_in_dim(weight, ((part * runs + i) * 2 + zbit) * run, run, axis)
            for i in range(runs)
        ]
        return jnp.concatenate(pieces, axis=axis), 0

    moved_in = exchange(tokens)
    share = features // 2
    gate_far, far_base = ff_block(gate_weight, 1 - row, 1)
    up_far, _ = ff_block(up_weight, 1 - row, 1)
    gate_sent, up_sent = (
        block_of(weight, xbit, far_base, (share, ff_part))
        for weight in (gate_far, up_far)
    )
    got_gate, got_up = swap_row(gate_sent), swap_row(up_sent)

    base_ids = jnp.arange(half, dtype=jnp.int32)
    local_ids = jnp.concatenate([col * half + base_ids, (1 - col) * half + base_ids])
    slot_ids = jnp.arange(group, dtype=jnp.int32)
    slot = jnp.sum(
        jnp.where(balance_order[0][None, :] == local_ids[:, None], slot_ids[None, :], 0), axis=1
    )
    lengths = seq_lengths[0]
    seq_ends = jnp.cumsum(lengths)
    starts = seq_ends - lengths
    segment = jnp.sum((slot[:, None] >= seq_ends[None, :]).astype(jnp.int32), axis=1)
    hits = segment[:, None] == jnp.arange(lengths.shape[0], dtype=jnp.int32)[None, :]
    start = jnp.sum(jnp.where(hits, starts[None, :], 0), axis=1)
    cosine, sine = rotary_tables(slot - start)
    slot_lanes = jnp.broadcast_to(slot.astype(F32)[None], (8, group))
    start_lanes = jnp.broadcast_to(start.astype(F32)[None], (8, group))
    moved_in, cosine, sine, slot_lanes, start_lanes, got_gate, up_sent = together(
        moved_in, cosine, sine, slot_lanes, start_lanes, got_gate, up_sent
    )

    gain_in = attention_gain.astype(F32)[None]
    gain_mid = feedforward_gain.astype(F32)[None]
    x_low, scaled_in, square = local_call(
        scaled_kernel,
        (moved_in, swap_col(moved_in), gain_in),
        [((group, features), BF16), ((group, features), BF16), ((8, group), F32)],
        "scaled",
    )
    moved_grad = exchange(after(cotangent, moved_in))
    heads_sent = heads_forward(after(scaled_in, got_gate, got_up), *projections, 1 - row, BF16, "heads_sent")
    got_square = swap_row(square)
    got_heads = swap_row(heads_sent)
    kept_heads = heads_forward(
        after(scaled_in, heads_sent), *projections, row, F32, "heads_kept"
    )
    got_gate, got_up = together(got_gate, got_up, heads_sent)[:2]
    got_gate_x, got_up_x = swap_dp(got_gate, 1), swap_dp(got_up, 1)

    down_own, own_at = ff_block(down_weight, row, 0)
    down_other, other_at = ff_block(down_weight, 1 - row, 0)

    def act_back(rows_of, weight, at, dtype, name="act_sent"):
        return product(rows_of, weight, "nt", dtype, ff_part // 3, at, ff_part, name=name)

    moved_grad = after(moved_grad, kept_heads)
    grad_z = swap_z(moved_grad)
    grad_near = swap_col(moved_grad)
    act_sent = [
        act_back(rows_of, down_other, other_at, BF16) for rows_of in (moved_grad, grad_near)
    ]
    got_heads, kept_heads, got_square, grad_z, *act_sent = together(
        got_heads, kept_heads, got_square, grad_z, *act_sent
    )
    inverse_in = lax.rsqrt((square + got_square) / D + EPSILON)
    shared = (
        inverse_in,
        cosine,
        sine,
        slot_lanes,
        start_lanes,
        slot_lanes[:1],
        query_gain.astype(F32)[None],
        key_norm_gain.astype(F32)[None],
    )
    got_act = [swap_row(act_sent[0])]
    grad_far = swap_col(grad_z)
    attention = attend(kept_heads, got_heads, shared, kv_heads, repeat)
    attention, got_act[0], grad_far = together(attention, got_act[0], grad_far)
    attention_other = swap_row(attention)
    got_act.append(swap_row(after(act_sent[1], attention)))
    out_own = product(
        attention, output_weight, "nn", F32, features // 2, row, query_part, name="out_own"
    )
    far_sent = [
        act_back(after(rows_of, out_own), down_other, other_at, BF16)
        for rows_of in (grad_z, grad_far)
    ]
    attention_other, got_gate_x, out_own, *far_sent = together(
        attention_other, got_gate_x, out_own, *far_sent
    )
    out_kept, out_sent = product_onto(
        attention_other, output_weight, 1 - row, query_part, out_own, features // 2, "out_proj"
    )
    out_got = swap_col(out_sent)
    stream_mid, square_mid = local_call(
        middle_kernel,
        (moved_in, out_kept, out_got),
        [((half, features), F32), ((8, half), F32)],
        "middle",
    )
    got_square = swap_row(square_mid)
    grad_all = assemble(
        (pair, features),
        [
            (0, 0, moved_grad),
            (half, 0, grad_z),
            (group, 0, grad_near),
            (group + half, 0, after(grad_far, square_mid)),
        ],
        "grad_all",
    )
    got_square, got_act[1] = together(got_square, got_act[1])
    normed_mid, inverse_mid = local_call(
        normed_kernel,
        (stream_mid, square_mid, got_square, gain_mid),
        [((half, features), BF16), ((8, half), F32)],
        "normed",
    )

    by_row = swap_row(normed_mid)
    by_z = swap_z(normed_mid)
    act_kept = act_back(after(grad_all, normed_mid), down_own, own_at, F32, "act_kept")
    by_row, by_z, act_kept, got_up_x = together(by_row, by_z, act_kept, got_up_x)
    corner_a = swap_row(by_z[:quarter])
    corner_b = swap_z(by_row[quarter:])
    got_act.extend(swap_row(after(sent, by_row)) for sent in far_sent)
    near = [
        (0, 0, normed_mid),
        (0, features, by_row),
        (half, 0, by_z),
        (half, features, corner_a),
        (half + quarter, features, corner_b),
    ]
    crossed = [(group + first, at, swap_col(piece)) for first, at, piece in near]
    mid_all = assemble((pair, 2 * features), near + crossed, "mid_all")

    gate_own, own_base = ff_block(gate_weight, row, 1)
    up_own, _ = ff_block(up_weight, row, 1)
    places = (xbit, 1 - xbit)
    pieces = ((got_gate, got_gate_x), (got_up, got_up_x))
    up_weights = (gate_own, up_own, own_base, pieces, places)
    gate_grad, up_grad, activated = gate_and_up(
        mid_all, *up_weights, act_kept, (got_act[0], got_act[2], got_act[1], got_act[3])
    )

    act_got = swap_row(activated)
    line = Line(activated)
    top_bit, lower_bits = all_bits[0], all_bits[1:]
    top_place = jnp.where(my_bit(top_bit) == row, 0, 1)

    def up_rows(grad_part, name):
        whole = product(mid_all, grad_part, "tn", BF16, features // 2, name=name)
        return whole.reshape((2,) * (levels + 1) + (features // count, ff_part))

    def first_stage(value, axis, bit):
        sent = line.passed(take(value, axis, 1 - my_bit(bit)))
        return swap_dp(sent, bit)

    def late_stage(value, got, axis, bit, next_axis, next_bit, place=None):
        place = my_bit(next_bit) if place is None else place
        kept, sent = end_stage(value, line.hold(got), axis, bit, next_axis, place)
        return kept, swap_dp(line.passed(sent), next_bit)

    mid_sent = gate_and_up_back(gate_grad, up_grad, 1, *up_weights, BF16, "mid_sent")
    line.passed(mid_sent[0])
    got_mid = [swap_col(sent) for sent in mid_sent]
    gate_rows = up_rows(line.hold(gate_grad), "gate_rows")
    gate_got = first_stage(gate_rows, levels, 1)
    mid_kept = gate_and_up_back(line.hold(gate_grad), up_grad, 0, *up_weights, F32, "mid_kept")
    *got_mid, kept_near, act_got = together(*got_mid, mid_kept[0], act_got)
    block = (half, features)
    mid_own, to_row, to_z, row_both, z_both = local_call(
        join_core_kernel,
        (kept_near, mid_kept[1], *got_mid),
        [(block, F32)] * 3 + [((quarter, features), BF16)] * 2,
        "join_core",
    )
    via_row = swap_row(row_both)
    via_z = swap_z(z_both)
    line.passed(row_both)
    up_cols = up_rows(line.hold(up_grad), "up_rows")
    up_sent = line.passed(take(up_cols, levels, 1 - xbit))
    via_row, via_z, up_sent = line.hold(via_row, via_z, up_sent)
    to_row, to_z = local_call(
        join_corner_kernel,
        (to_row, to_z, via_row, via_z),
        [(block, BF16), (block, BF16)],
        "join_corner",
    )
    got_row, got_z = swap_row(to_row), swap_z(to_z)
    up_got = swap_dp(up_sent, 1)
    line.passed(to_row)
    act_all = assemble(
        (pair, 2 * ff_part), [(0, 0, activated), (0, ff_part, line.hold(act_got))], "act_all"
    )
    down_rows = product(act_all, grad_all, "tn", BF16, ff_part // 2, name="down_first")
    down_rows = split_rows(down_rows, levels - 1)
    down_sent = line.passed(take(down_rows, levels - 2, 1 - xbit))
    got_row, got_z, down_sent = line.hold(got_row, got_z, down_sent)
    normed_mid_grad, mid_sum, feedforward_part = norm_sums(
        (mid_own, got_row, got_z), stream_mid, inverse_mid, gain_mid
    )
    got_sum = swap_row(line.passed(mid_sum))
    down_got = swap_dp(down_sent, 1)
    got_sum, gate_got = line.hold(got_sum, gate_got)
    stream_mid_grad, branch_low = norm_grad(
        normed_mid_grad, stream_mid, inverse_mid, gain_mid, mid_sum, got_sum, moved_grad, (F32, BF16)
    )
    line.passed(branch_low)
    branch_got = swap_col(branch_low)
    gate_rows, gate_got = late_stage(gate_rows, gate_got, levels, 1, 1, top_bit)
    branch = assemble(
        (group, features), [(0, 0, branch_low), (half, 0, line.hold(branch_got))], "branch"
    )
    attention_sent = product(branch, output_weight, "nt", BF16, query_part, 1 - row, query_part)
    got_attention = swap_row(attention_sent)
    line.passed(attention_sent)

    attention_kept = line.passed(
        product(
            line.hold(branch),
            output_weight,
            "nt",
            F32,
            query_part,
            row,
            query_part,
            name="attention_kept",
        )
    )
    attention_all = assemble(
        (group, 2 * query_part),
        [(0, 0, line.hold(attention)), (0, query_part, attention_other)],
        "attention_all",
    )
    output_rows = product(attention_all, branch, "tn", BF16, query_part, name="output_rows")
    output_rows = split_rows(output_rows, levels)
    output_sent = line.passed(take(output_rows, levels - 2, 1 - zbit))
    output_got = swap_dp(output_sent, 2)
    out_kept, *out_sent = down_product(
        line.hold(act_all), down_own, down_other, own_at, other_at, features // 2
    )
    line.passed(out_kept)
    out_got = [swap_col(sent) for sent in out_sent]
    got_attention, out_kept = line.hold(got_attention, out_kept)
    line.passed(got_attention)
    projected_grad, head_gains = attend_back(
        kept_heads, got_heads, shared, attention_kept, line.hold(got_attention), kv_heads, repeat
    )
    projected_grad, up_got, gate_got, output_got, *out_got = together(
        projected_grad, up_got, gate_got, output_got, *out_got
    )
    projected_other = swap_row(projected_grad)
    line.passed(projected_grad)
    up_cols, up_got = late_stage(up_cols, up_got, levels, 1, 1, top_bit)

    (normed_in,) = local_call(
        normed_in_kernel,
        (x_low, line.hold(inverse_in), gain_in),
        [((group, features), BF16)],
        "normed_in",
    )

    def projection_rows(part, name):
        whole = product(normed_in, part, "tn", BF16, features // 2, name=name)
        whole = split_rows(whole, levels)
        return whole, line.passed(take(whole, levels - 2, 1 - zbit))

    heads_first, heads_sent_own = projection_rows(line.hold(projected_grad), "heads_first")
    in_own = line.passed(heads_backward(line.hold(projected_grad), *projections, row)[0])
    heads_got = swap_dp(heads_sent_own, 2)
    out_near, out_far = local_call(
        out_near_kernel, (out_kept, *line.hold(*out_got)), [(block, F32), (block, BF16)], "out_near"
    )
    layer_z = swap_z(line.passed(out_far))
    projected_other, in_own, down_got = line.hold(projected_other, in_own, down_got)
    line.passed(projected_other)
    in_kept, in_sent = heads_backward(projected_other, *projections, 1 - row, in_own)
    in_got = swap_col(line.passed(in_sent))
    down_rows, down_got = late_stage(down_rows, down_got, levels - 2, 1, 0, top_bit, top_place)
    in_values = (moved_in, inverse_in[:, :half], gain_in)
    normed_in_grad, in_sum, attention_part = norm_sums(
        (in_kept, line.hold(in_got)), *in_values
    )
    got_sum = swap_row(line.passed(in_sum))
    output_rows, output_got = late_stage(
        output_rows, output_got, levels - 2, 2, levels - 2, 1
    )
    heads_second, heads_sent_other = projection_rows(line.hold(projected_other), "heads_second")
    got_sum, up_got, heads_got, heads_sent_other = line.hold(
        got_sum, up_got, heads_got, heads_sent_other
    )
    heads_got_other = swap_dp(heads_sent_other, 2)
    (stream_grad,) = norm_grad(
        normed_in_grad, *in_values, in_sum, got_sum, stream_mid_grad, (BF16,)
    )
    grad_back = exchange(
        line.passed(pack_back(stream_grad, attention_part, feedforward_part, head_gains, count))
    )

    for bit in lower_bits:
        gate_rows, gate_got = late_stage(gate_rows, gate_got, None, None, 1, bit)
        up_cols, up_got = late_stage(up_cols, up_got, None, None, 1, bit)
    shape = gate_rows.shape[1:-1] + (2 * ff_part,)
    side_own, side_sent = local_call(
        side_kernel,
        (gate_rows, up_cols, *line.hold(gate_got, up_got)),
        [(shape, F32), (shape, BF16)],
        "side",
    )
    side_got = swap_row(line.passed(side_sent))
    heads_own, heads_got = late_stage(heads_first, heads_got, levels - 2, 2, levels - 2, 1)
    (layer_out,) = local_call(
        layer_out_kernel, (stream_mid, out_near, line.hold(layer_z)), [(block, BF16)], "layer_out"
    )
    line.passed(layer_out)
    output_got, side_got, heads_got, layer_out = line.hold(
        output_got, side_got, heads_got, layer_out
    )
    line.passed(side_got)
    output_rows, output_got = late_stage(
        output_rows, output_got, None, None, 0, top_bit, top_place
    )
    heads_own, heads_got = late_stage(heads_own, heads_got, None, None, 0, top_bit)
    sent = jnp.stack([pick(part, 1 - zbit, 0).astype(BF16) for part in (side_own, side_got)])
    side_z = swap_z(line.passed(sent))
    grad_back, layer_out = line.hold(grad_back, layer_out)
    line.passed(grad_back)
    out_back = exchange(layer_out)
    heads_got_other, down_got = line.hold(heads_got_other, down_got)
    line.passed(down_got)
    heads_other, heads_got_other = late_stage(
        heads_second, heads_got_other, levels - 2, 2, levels - 2, 1
    )

    def finish(kept, got):
        value = line.passed(add_got(kept, line.hold(got)))
        for bit in lower_bits:
            value = pick(value, my_bit(bit), 0) + swap_dp(
                pick(value, 1 - my_bit(bit), 0).astype(BF16), bit
            ).astype(F32)
        return value

    down_grad = finish(down_rows, down_got)
    heads_other, heads_got_other = late_stage(heads_other, heads_got_other, None, None, 0, top_bit)
    output_weight_grad = finish(output_rows, output_got)
    side_z = line.hold(side_z)

    def up_columns(at):
        columns = slice(at, at + ff_part)
        keep = [pick(part[..., columns], zbit, 0) for part in (side_own, side_got.astype(F32))]
        swapped = side_z[..., columns].astype(F32)
        table = [
            by_half(zbit, near_piece, far_piece)
            for near_piece, far_piece in zip(
                by_half(row, keep[0], keep[1]), by_half(row, swapped[0], swapped[1])
            )
        ]
        return jnp.concatenate(
            [
                table[part][z][:, i * run : (i + 1) * run]
                for part in range(2)
                for i in range(runs)
                for z in range(2)
            ],
            axis=1,
        )

    gate_weight_grad = up_columns(0)
    up_weight_grad = line.passed(up_columns(ff_part))
    heads_grad_own = finish(heads_own, heads_got)
    out_back = line.passed(line.hold(out_back))
    heads_grad_other = finish(heads_other, heads_got_other)

    def head_grad(start, width):
        own = heads_grad_own[:, start : start + width]
        other = heads_grad_other[:, start : start + width]
        return jnp.concatenate(by_half(row, own, other), axis=1)

    query_weight_grad = head_grad(0, query_part)
    key_weight_grad = head_grad(query_part, key_part)
    value_weight_grad = head_grad(query_part + key_part, key_part)

    back = grad_back.reshape(count, -1, features).astype(F32)
    grad_back = back[:, :-EXTRA].reshape(half, features)
    totals = jnp.sum(back[:, -EXTRA:], axis=0)
    out_back = out_back.astype(F32)
    gains = jnp.concatenate([totals[i] + totals[i + 4] for i in range(3)])[None]
    gains = gains + swap_col(gains)
    gain_low, gain_high = (part[0] for part in by_half(row, gains, swap_row(gains)))
    attention_total = jnp.concatenate([gain_low[:features], gain_high[:features]])
    feedforward_total = jnp.concatenate(
        [gain_low[features : 2 * features], gain_high[features : 2 * features]]
    )
    head_totals = (gain_low + gain_high)[2 * features :]
    return (
        out_back,
        grad_back,
        attention_total,
        query_weight_grad,
        key_weight_grad,
        value_weight_grad,
        head_totals[:HEAD_SIZE],
        head_totals[HEAD_SIZE : 2 * HEAD_SIZE],
        output_weight_grad,
        feedforward_total,
        gate_weight_grad,
        up_weight_grad,
        down_grad,
    )


def solution(mesh):
    placed = (
        P(("dp", "col"), "row"),
        P(("dp", "col"), "row"),
        P("dp", None),
        P("dp", None),
        P("row"),
        P("row", "col"),
        P("row", "col"),
        P("row", "col"),
        P(),
        P(),
        P("col", "row"),
        P("row"),
        P("row", "col"),
        P("row", "col"),
        P("col", "row"),
    )
    return jax.shard_map(
        shards,
        mesh=mesh,
        in_specs=placed,
        out_specs=(
            P(("dp", "col"), "row"),
            P(("dp", "col"), "row"),
            P(),
            P(("row", "dp"), "col"),
            P(("row", "dp"), "col"),
            P(("row", "dp"), "col"),
            P(),
            P(),
            P(("col", "dp"), "row"),
            P(),
            P(("row", "dp"), "col"),
            P(("row", "dp"), "col"),
            P(("col", "dp"), "row"),
        ),
        check_vma=False,
    )
```
